128 devices in a mesh: row: 8 (over x, y_lo), col: 16 (over y_hi, z, core).
Axes of the slice: x: 4, y: 4 (y_hi: 2, y_lo: 2; y = y_hi * 2 + y_lo), z: 4, core: 2. Of those that a mesh axis runs over, the one named last changes fastest.
Arguments:
- record: bfloat16 [180224, 4096], P(('row', 'col')), may hold values from -6 to 6
- fir_taps: float32 [101], replicated, may hold values from -0.625 to 0.625
- bins: int32 [16], replicated, may hold values from 1 to 639
- offsets: int32 [128], P(('row', 'col')), may hold values from 0 to 28, as said below
Outputs:
- cross: bfloat16 [16, 2, 4096, 4096], P(None, None, 'row', 'col')
The draws below stay inside these ranges and needn't reach their ends.
Inputs may be any that keep to these rules, and one draw needn't show every extreme that they name: `offsets`: a window's start offset within its slot of 1408 samples.
All inputs are finite; a program needn't handle non-finite values.
Results may differ from the reference program's by a relative error of at most 0.0069.
Values may be sent and summed in bfloat16 or wider, within the bound.
A program may use at most 192 MiB of HBM per device.

```python
import math
import jax
import jax.numpy as jnp
from jax import lax

CH = 4096
F = 16
WL = 1280
TAPS = 101
SLACK = 28
WIN_DEV = 1
SEG_DEV = 1408
NW = 128
SAMPLES = 180224


def draw_offsets(key, part):
    values = jax.random.randint(key, (NW,), 0, SLACK + 1)
    values = values.at[0].set(SLACK)
    values = values.at[NW - 1].set(0)
    return values.astype(jnp.int32)


def set_ends(drawn, rng, smallest, high):
    shape = drawn.shape
    spot = [jax.random.randint(jax.random.fold_in(rng, axis), (), 0, shape[axis]) for axis in range(len(shape))]
    drawn = drawn.at[tuple(spot)].set(smallest)
    longest = shape.index(max(shape))
    spot[longest] = (spot[longest] + 1) % shape[longest]
    return drawn.at[tuple(spot)].set(high)


def levels(stream_key, shape, split, low, high):
    loudness, own = 1.0, jax.random.fold_in(stream_key, 6)
    for dim, parts in split:
        steps = jnp.exp(jax.random.uniform(jax.random.fold_in(own, dim), (parts,), jnp.float32, low / len(split), high / len(split)))
        loudness = loudness * jnp.repeat(steps, shape[dim] // parts).reshape([-1 if axis == dim else 1 for axis in range(len(shape))])
    return loudness


def gaussian(own_key, extent, width, reach, pieces=(), kind=jnp.bfloat16):
    values = width * jax.random.normal(own_key, extent, jnp.float32)
    if pieces:
        values = values * levels(own_key, extent, pieces, -0.22, 0.18)
    return jnp.clip(values, -reach, reach).astype(kind)


def setup_inputs(seed: int = 0) -> dict:
    arg_keys = jax.random.split(jax.random.key(seed), 5)
    record = gaussian(arg_keys[0], (SAMPLES, CH), 1.0, 6.0, ((0, 128),))
    fir_taps = gaussian(arg_keys[1], (TAPS,), TAPS ** -0.5, 0.625, (), jnp.float32)
    bins = set_ends(jax.random.randint(arg_keys[2], (F,), 1, WL // 2), jax.random.fold_in(arg_keys[2], 1), 1, (WL // 2) - 1).astype(jnp.int32)
    offsets = draw_offsets(jax.random.fold_in(arg_keys[4], 71), 0)
    return {"record": record, "fir_taps": fir_taps, "bins": bins, "offsets": offsets}


floor_level = 0.5

def analysis_kernel(fir_taps, bins):
    span = WL + TAPS - 1
    sample_times = jnp.arange(WL, dtype=jnp.int32)
    phase_index = bins[:, None] * sample_times[None, :] % WL
    angles = 2.0 * math.pi / WL * phase_index.astype(jnp.float32)
    centre = (jnp.arange(WL, dtype=jnp.float32) + 0.5) / WL
    window_taper = (0.5 - 0.5 * jnp.cos(2.0 * math.pi * centre)) / math.sqrt(WL)
    pattern = jnp.stack([jnp.cos(angles) * window_taper, -jnp.sin(angles) * window_taper]).reshape(2 * F, WL)
    length = WL + span - 1
    middle = jnp.zeros((length - TAPS,), jnp.float32)
    vector = jnp.concatenate([fir_taps[TAPS - 1:], middle, fir_taps[:TAPS - 1]])
    band = jnp.tile(vector, span)[:span * (length - 1)].reshape(span, length - 1)[:, :WL]
    kernel = jnp.dot(pattern, band.T, precision=lax.Precision.HIGHEST, preferred_element_type=jnp.float32)
    return kernel.astype(jnp.bfloat16)

def whiten(spectra):
    shaped = spectra.reshape(spectra.shape[0], 2, F, spectra.shape[-1])
    magnitude = jnp.sqrt(shaped[:, 0] * shaped[:, 0] + shaped[:, 1] * shaped[:, 1])
    inverse = 1.0 / jnp.maximum(magnitude, floor_level)
    return (shaped * inverse[:, None]).astype(jnp.bfloat16)

def reference(record, fir_taps, bins, offsets):
    kernel = analysis_kernel(fir_taps, bins)
    span = WL + TAPS - 1

    def one_window(window):
        first_row = window // WIN_DEV * SEG_DEV + window % WIN_DEV * WL + offsets[window]
        samples = lax.dynamic_slice_in_dim(record, first_row.astype(jnp.int32), span, 0)
        return jnp.dot(kernel, samples, preferred_element_type=jnp.float32)
    spectra = lax.map(one_window, jnp.arange(NW, dtype=jnp.int32))
    whitened = whiten(spectra)

    def one_bin(bin_index):
        real_part = whitened[:, 0, bin_index, :]
        imag_part = whitened[:, 1, bin_index, :]
        real_sum = jnp.dot(real_part.T, real_part, preferred_element_type=jnp.float32) + jnp.dot(imag_part.T, imag_part, preferred_element_type=jnp.float32)
        imag_sum = jnp.dot(real_part.T, imag_part, preferred_element_type=jnp.float32) - jnp.dot(imag_part.T, real_part, preferred_element_type=jnp.float32)
        return (jnp.stack([real_sum, imag_sum]) / NW).astype(jnp.bfloat16)
    return lax.map(one_bin, jnp.arange(F, dtype=jnp.int32))
```

```python
import math

import jax
import jax.numpy as jnp
from jax import lax
from jax.sharding import PartitionSpec as P

F = 16
WL = 1280
TAPS = 101


floor_level = 0.5


def analysis_kernel(fir_taps, bins):
    span = WL + TAPS - 1
    sample_times = jnp.arange(WL, dtype=jnp.int32)
    phase_index = bins[:, None] * sample_times[None, :] % WL
    angles = 2.0 * math.pi / WL * phase_index.astype(jnp.float32)
    centre = (jnp.arange(WL, dtype=jnp.float32) + 0.5) / WL
    window_taper = (0.5 - 0.5 * jnp.cos(2.0 * math.pi * centre)) / math.sqrt(WL)
    pattern = jnp.stack([jnp.cos(angles) * window_taper, -jnp.sin(angles) * window_taper]).reshape(
        2 * F, WL
    )
    lanes = 128
    blocks = pl_cdiv(span, lanes)
    width = 2 * lanes
    padded = jnp.pad(pattern, ((0, 0), (TAPS - 1, blocks * lanes + lanes - WL - (TAPS - 1))))
    windows = jnp.concatenate(
        [
            padded[:, : blocks * lanes].reshape(2 * F, blocks, lanes),
            padded[:, lanes : (blocks + 1) * lanes].reshape(2 * F, blocks, lanes),
        ],
        axis=2,
    )
    vector = jnp.concatenate([fir_taps, jnp.zeros((width + 1 - TAPS,), jnp.float32)])
    band = jnp.tile(vector, lanes)[: lanes * width].reshape(lanes, width)
    kernel = jnp.einsum(
        "bqs,rs->bqr",
        windows,
        band,
        precision=lax.Precision.HIGHEST,
        preferred_element_type=jnp.float32,
    ).reshape(2 * F, blocks * lanes)[:, :span]
    return kernel.astype(jnp.bfloat16)


def pl_cdiv(a, b):
    return (a + b - 1) // b


def whiten(spectra):
    shaped = spectra.reshape(spectra.shape[0], 2, F, spectra.shape[-1])
    magnitude = jnp.sqrt(shaped[:, 0] * shaped[:, 0] + shaped[:, 1] * shaped[:, 1])
    inverse = 1.0 / jnp.maximum(magnitude, floor_level)
    return (shaped * inverse[:, None]).astype(jnp.bfloat16)


def on_device(record, fir_taps, bins, offsets):
    kernel = analysis_kernel(fir_taps, bins)
    span = WL + TAPS - 1
    local_count = offsets.shape[0]

    def one_window(window):
        first_row = window * WL + offsets[window]
        samples = lax.dynamic_slice_in_dim(record, first_row, span, 0)
        return jnp.dot(kernel, samples, preferred_element_type=jnp.float32)

    spectra = lax.map(one_window, jnp.arange(local_count, dtype=jnp.int32))
    whitened = whiten(spectra)
    channels = whitened.shape[-1]
    row_count = lax.axis_size("row")
    col_count = lax.axis_size("col")
    total_windows = local_count * row_count * col_count
    row_part = lax.all_to_all(
        whitened.reshape(local_count, 2, F, row_count, channels // row_count),
        "row", split_axis=3, concat_axis=0, tiled=True,
    )
    row_block = lax.all_gather(row_part, "col", axis=0, tiled=False)
    col_part = lax.all_to_all(
        whitened.reshape(local_count, 2, F, col_count, channels // col_count),
        "col", split_axis=3, concat_axis=0, tiled=True,
    )
    col_block = lax.all_gather(col_part, "row", axis=0, tiled=False)
    left = row_block.reshape(col_count, row_count, local_count, 2, F, channels // row_count)
    right = col_block.reshape(row_count, col_count, local_count, 2, F, channels // col_count)
    right2 = jnp.stack(
        [right, jnp.stack([right[:, :, :, 1], -right[:, :, :, 0]], axis=3)], axis=5
    )
    cross_sum = jnp.einsum(
        "crwkfi,rcwkfpj->fpij", left, right2, preferred_element_type=jnp.float32
    )
    return (cross_sum * (1.0 / total_windows)).astype(jnp.bfloat16)


def solution(mesh):
    placed = (P(("row", "col"), None), P(), P(), P(("row", "col")))
    return jax.shard_map(
        on_device,
        mesh=mesh,
        in_specs=placed,
        out_specs=P(None, None, "row", "col"),
        check_vma=False,
    )
```

```python
import functools
import math

import jax
import jax.numpy as jnp
from jax import lax
from jax.sharding import PartitionSpec as P
from jax.experimental import pallas as pl
from jax.experimental.pallas import tpu as pltpu

F = 16
WL = 1280
TAPS = 101


floor_level = 0.5


def analysis_kernel(fir_taps, bins):
    span = WL + TAPS - 1
    sample_times = jnp.arange(WL, dtype=jnp.int32)
    phase_index = bins[:, None] * sample_times[None, :] % WL
    angles = 2.0 * math.pi / WL * phase_index.astype(jnp.float32)
    centre = (jnp.arange(WL, dtype=jnp.float32) + 0.5) / WL
    window_taper = (0.5 - 0.5 * jnp.cos(2.0 * math.pi * centre)) / math.sqrt(WL)
    pattern = jnp.stack([jnp.cos(angles) * window_taper, -jnp.sin(angles) * window_taper]).reshape(
        2 * F, WL
    )
    lanes = 128
    blocks = pl_cdiv(span, lanes)
    width = 2 * lanes
    padded = jnp.pad(pattern, ((0, 0), (TAPS - 1, blocks * lanes + lanes - WL - (TAPS - 1))))
    windows = jnp.concatenate(
        [
            padded[:, : blocks * lanes].reshape(2 * F, blocks, lanes),
            padded[:, lanes : (blocks + 1) * lanes].reshape(2 * F, blocks, lanes),
        ],
        axis=2,
    )
    vector = jnp.concatenate([fir_taps, jnp.zeros((width + 1 - TAPS,), jnp.float32)])
    band = jnp.tile(vector, lanes)[: lanes * width].reshape(lanes, width)
    kernel = jnp.einsum(
        "bqs,rs->bqr",
        windows,
        band,
        precision=lax.Precision.HIGHEST,
        preferred_element_type=jnp.float32,
    ).reshape(2 * F, blocks * lanes)[:, :span]
    return kernel.astype(jnp.bfloat16)


def pl_cdiv(a, b):
    return (a + b - 1) // b


def whiten(spectra):
    shaped = spectra.reshape(spectra.shape[0], 2, F, spectra.shape[-1])
    magnitude = jnp.sqrt(shaped[:, 0] * shaped[:, 0] + shaped[:, 1] * shaped[:, 1])
    inverse = 1.0 / jnp.maximum(magnitude, floor_level)
    return (shaped * inverse[:, None]).astype(jnp.bfloat16)


MESH = pl.DeviceIdType.MESH


def exchange_kernel(nr, nc, w_ref, rbuf, cbuf, r1, c1, r2, c2, s1r, s1c, s2r, s2c, loc):
    r = lax.axis_index("row")
    c = lax.axis_index("col")
    rb = rbuf.shape[-1]
    cb = cbuf.shape[-1]
    own_r = pltpu.make_async_copy(w_ref.at[:, pl.ds(r * rb, rb)], rbuf.at[c, r], loc.at[0])
    own_r.start()
    own_c = pltpu.make_async_copy(w_ref.at[:, pl.ds(c * cb, cb)], cbuf.at[r, c], loc.at[1])
    own_c.start()
    sends = []
    for d in range(1, nr):
        t = lax.rem(r + d, nr)
        cp = pltpu.make_async_remote_copy(
            src_ref=w_ref.at[:, pl.ds(t * rb, rb)], dst_ref=rbuf.at[c, r],
            send_sem=s1r.at[d], recv_sem=r1.at[r], device_id=(t, c), device_id_type=MESH,
        )
        cp.start()
        sends.append(cp)
    for d in range(1, nc):
        t = lax.rem(c + d, nc)
        cp = pltpu.make_async_remote_copy(
            src_ref=w_ref.at[:, pl.ds(t * cb, cb)], dst_ref=cbuf.at[r, c],
            send_sem=s1c.at[d], recv_sem=c1.at[c], device_id=(r, t), device_id_type=MESH,
        )
        cp.start()
        sends.append(cp)
    own_r.wait()
    for d in range(1, nr):
        src = lax.rem(r + nr - d, nr)
        pltpu.make_async_copy(rbuf.at[c, src], rbuf.at[c, src], r1.at[src]).wait()
    for d in range(1, nc):
        t = lax.rem(c + d, nc)
        cp = pltpu.make_async_remote_copy(
            src_ref=rbuf.at[c], dst_ref=rbuf.at[c],
            send_sem=s2r.at[d], recv_sem=r2.at[c], device_id=(r, t), device_id_type=MESH,
        )
        cp.start()
        sends.append(cp)
    own_c.wait()
    for d in range(1, nc):
        src = lax.rem(c + nc - d, nc)
        pltpu.make_async_copy(cbuf.at[r, src], cbuf.at[r, src], c1.at[src]).wait()
    for d in range(1, nr):
        t = lax.rem(r + d, nr)
        cp = pltpu.make_async_remote_copy(
            src_ref=cbuf.at[r], dst_ref=cbuf.at[r],
            send_sem=s2c.at[d], recv_sem=c2.at[r], device_id=(t, c), device_id_type=MESH,
        )
        cp.start()
        sends.append(cp)
    for cp in sends:
        cp.wait_send()
    for d in range(1, nc):
        src = lax.rem(c + nc - d, nc)
        pltpu.make_async_copy(rbuf.at[src], rbuf.at[src], r2.at[src]).wait()
    for d in range(1, nr):
        src = lax.rem(r + nr - d, nr)
        pltpu.make_async_copy(cbuf.at[src], cbuf.at[src], c2.at[src]).wait()


def exchange(w, nr, nc):
    rows, channels = w.shape
    rb = channels // nr
    cb = channels // nc
    dma = pltpu.SemaphoreType.DMA
    return pl.pallas_call(
        functools.partial(exchange_kernel, nr, nc),
        out_shape=(
            jax.ShapeDtypeStruct((nc, nr, rows, rb), w.dtype),
            jax.ShapeDtypeStruct((nr, nc, rows, cb), w.dtype),
        ),
        in_specs=[pl.BlockSpec(memory_space=pl.ANY)],
        out_specs=(pl.BlockSpec(memory_space=pl.ANY), pl.BlockSpec(memory_space=pl.ANY)),
        scratch_shapes=[
            dma((nr,)), dma((nc,)), dma((nc,)), dma((nr,)),
            dma((nr,)), dma((nc,)), dma((nc,)), dma((nr,)), dma((2,)),
        ],
        compiler_params=pltpu.CompilerParams(has_side_effects=True),
    )(w)


def on_device(record, fir_taps, bins, offsets):
    kernel = analysis_kernel(fir_taps, bins)
    span = WL + TAPS - 1
    local_count = offsets.shape[0]

    def one_window(window):
        first_row = window * WL + offsets[window]
        samples = lax.dynamic_slice_in_dim(record, first_row, span, 0)
        return jnp.dot(kernel, samples, preferred_element_type=jnp.float32)

    spectra = lax.map(one_window, jnp.arange(local_count, dtype=jnp.int32))
    whitened = whiten(spectra)
    channels = whitened.shape[-1]
    row_count = lax.axis_size("row")
    col_count = lax.axis_size("col")
    total_windows = local_count * row_count * col_count
    row_block, col_block = exchange(
        whitened.reshape(2 * F, channels), row_count, col_count
    )
    left = row_block.reshape(col_count, row_count, local_count, 2, F, channels // row_count)
    right = col_block.reshape(row_count, col_count, local_count, 2, F, channels // col_count)
    right2 = jnp.stack(
        [right, jnp.stack([right[:, :, :, 1], -right[:, :, :, 0]], axis=3)], axis=5
    )
    cross_sum = jnp.einsum(
        "crwkfi,rcwkfpj->fpij", left, right2, preferred_element_type=jnp.float32
    )
    return (cross_sum * (1.0 / total_windows)).astype(jnp.bfloat16)


def solution(mesh):
    placed = (P(("row", "col"), None), P(), P(), P(("row", "col")))
    return jax.shard_map(
        on_device,
        mesh=mesh,
        in_specs=placed,
        out_specs=P(None, None, "row", "col"),
        check_vma=False,
    )
```

```python
import functools
import math

import jax
import jax.numpy as jnp
from jax import lax
from jax.sharding import PartitionSpec as P
from jax.experimental import pallas as pl
from jax.experimental.pallas import tpu as pltpu

F = 16
WL = 1280
TAPS = 101


floor_level = 0.5


def analysis_kernel(fir_taps, bins):
    span = WL + TAPS - 1
    sample_times = jnp.arange(WL, dtype=jnp.int32)
    phase_index = bins[:, None] * sample_times[None, :] % WL
    angles = 2.0 * math.pi / WL * phase_index.astype(jnp.float32)
    centre = (jnp.arange(WL, dtype=jnp.float32) + 0.5) / WL
    window_taper = (0.5 - 0.5 * jnp.cos(2.0 * math.pi * centre)) / math.sqrt(WL)
    pattern = jnp.stack([jnp.cos(angles) * window_taper, -jnp.sin(angles) * window_taper]).reshape(
        2 * F, WL
    )
    lanes = 128
    blocks = pl_cdiv(span, lanes)
    width = 2 * lanes
    padded = jnp.pad(pattern, ((0, 0), (TAPS - 1, blocks * lanes + lanes - WL - (TAPS - 1))))
    windows = jnp.concatenate(
        [
            padded[:, : blocks * lanes].reshape(2 * F, blocks, lanes),
            padded[:, lanes : (blocks + 1) * lanes].reshape(2 * F, blocks, lanes),
        ],
        axis=2,
    )
    vector = jnp.concatenate([fir_taps, jnp.zeros((width + 1 - TAPS,), jnp.float32)])
    band = jnp.tile(vector, lanes)[: lanes * width].reshape(lanes, width)
    kernel = jnp.einsum(
        "bqs,rs->bqr",
        windows,
        band,
        precision=lax.Precision.HIGHEST,
        preferred_element_type=jnp.float32,
    ).reshape(2 * F, blocks * lanes)[:, :span]
    return kernel.astype(jnp.bfloat16)


def pl_cdiv(a, b):
    return (a + b - 1) // b


def whiten(spectra):
    shaped = spectra.reshape(spectra.shape[0], 2, F, spectra.shape[-1])
    magnitude = jnp.sqrt(shaped[:, 0] * shaped[:, 0] + shaped[:, 1] * shaped[:, 1])
    inverse = 1.0 / jnp.maximum(magnitude, floor_level)
    return (shaped * inverse[:, None]).astype(jnp.bfloat16)


MESH = pl.DeviceIdType.MESH


def exchange_kernel(nr, nc, w_ref, rbuf, cbuf, r1, c1, r2, c2, s1r, s1c, s2r, s2c, loc):
    r = lax.axis_index("row")
    c = lax.axis_index("col")
    rb = rbuf.shape[-1]
    cb = cbuf.shape[-1]
    own_r = pltpu.make_async_copy(w_ref.at[:, pl.ds(r * rb, rb)], rbuf.at[c, r], loc.at[0])
    own_r.start()
    own_c = pltpu.make_async_copy(w_ref.at[:, pl.ds(c * cb, cb)], cbuf.at[r, c], loc.at[1])
    own_c.start()
    sends = []
    for d in range(1, nr):
        t = lax.rem(r + d, nr)
        cp = pltpu.make_async_remote_copy(
            src_ref=w_ref.at[:, pl.ds(t * rb, rb)], dst_ref=rbuf.at[c, r],
            send_sem=s1r.at[d], recv_sem=r1.at[r], device_id=(t, c), device_id_type=MESH,
        )
        cp.start()
        sends.append(cp)
    for d in range(1, nc):
        t = lax.rem(c + d, nc)
        cp = pltpu.make_async_remote_copy(
            src_ref=w_ref.at[:, pl.ds(t * cb, cb)], dst_ref=cbuf.at[r, c],
            send_sem=s1c.at[d], recv_sem=c1.at[c], device_id=(r, t), device_id_type=MESH,
        )
        cp.start()
        sends.append(cp)
    own_r.wait()
    for d in range(1, nr):
        src = lax.rem(r + nr - d, nr)
        pltpu.make_async_copy(rbuf.at[c, src], rbuf.at[c, src], r1.at[src]).wait()
    for d in range(1, nc):
        t = lax.rem(c + d, nc)
        cp = pltpu.make_async_remote_copy(
            src_ref=rbuf.at[c], dst_ref=rbuf.at[c],
            send_sem=s2r.at[d], recv_sem=r2.at[c], device_id=(r, t), device_id_type=MESH,
        )
        cp.start()
        sends.append(cp)
    own_c.wait()
    for d in range(1, nc):
        src = lax.rem(c + nc - d, nc)
        pltpu.make_async_copy(cbuf.at[r, src], cbuf.at[r, src], c1.at[src]).wait()
    for d in range(1, nr):
        t = lax.rem(r + d, nr)
        cp = pltpu.make_async_remote_copy(
            src_ref=cbuf.at[r], dst_ref=cbuf.at[r],
            send_sem=s2c.at[d], recv_sem=c2.at[r], device_id=(t, c), device_id_type=MESH,
        )
        cp.start()
        sends.append(cp)
    for cp in sends:
        cp.wait_send()
    for d in range(1, nc):
        src = lax.rem(c + nc - d, nc)
        pltpu.make_async_copy(rbuf.at[src], rbuf.at[src], r2.at[src]).wait()
    for d in range(1, nr):
        src = lax.rem(r + nr - d, nr)
        pltpu.make_async_copy(cbuf.at[src], cbuf.at[src], c2.at[src]).wait()


def exchange(w, nr, nc):
    rows, channels = w.shape
    rb = channels // nr
    cb = channels // nc
    dma = pltpu.SemaphoreType.DMA
    return pl.pallas_call(
        functools.partial(exchange_kernel, nr, nc),
        out_shape=(
            jax.ShapeDtypeStruct((nc, nr, rows, rb), w.dtype),
            jax.ShapeDtypeStruct((nr, nc, rows, cb), w.dtype),
        ),
        in_specs=[pl.BlockSpec(memory_space=pl.ANY)],
        out_specs=(pl.BlockSpec(memory_space=pl.ANY), pl.BlockSpec(memory_space=pl.ANY)),
        scratch_shapes=[
            dma((nr,)), dma((nc,)), dma((nc,)), dma((nr,)),
            dma((nr,)), dma((nc,)), dma((nc,)), dma((nr,)), dma((2,)),
        ],
        compiler_params=pltpu.CompilerParams(has_side_effects=True),
    )(w)


def on_device(record, fir_taps, bins, offsets):
    kernel = analysis_kernel(fir_taps, bins)
    span = WL + TAPS - 1
    local_count = offsets.shape[0]

    def one_window(window):
        first_row = window * WL + offsets[window]
        samples = lax.dynamic_slice_in_dim(record, first_row, span, 0)
        return jnp.dot(kernel, samples, preferred_element_type=jnp.float32)

    spectra = lax.map(one_window, jnp.arange(local_count, dtype=jnp.int32))
    whitened = whiten(spectra)
    channels = whitened.shape[-1]
    row_count = lax.axis_size("row")
    col_count = lax.axis_size("col")
    total_windows = local_count * row_count * col_count
    row_block, col_block = exchange(
        whitened.reshape(2 * F, channels), row_count, col_count
    )
    windows = row_count * col_count * local_count
    rb = channels // row_count
    cb = channels // col_count
    left = row_block.reshape(windows, 2 * F, rb).transpose(1, 2, 0)
    right = (
        col_block.reshape(row_count, col_count, 2 * F, cb)
        .transpose(2, 1, 0, 3)
        .reshape(2 * F, windows, cb)
    )
    return cross(left, right, 1.0 / total_windows)


def cross_kernel(scale, l0, l1, r0, r1, out_ref):
    def dot(a, b):
        return jnp.dot(a[0], b[0], preferred_element_type=jnp.float32)

    real = dot(l0, r0) + dot(l1, r1)
    imag = dot(l0, r1) - dot(l1, r0)
    out_ref[0, 0] = (real * scale).astype(out_ref.dtype)
    out_ref[0, 1] = (imag * scale).astype(out_ref.dtype)


def cross(left, right, scale):
    parts, rb, windows = left.shape
    cb = right.shape[-1]
    bins = parts // 2
    return pl.pallas_call(
        functools.partial(cross_kernel, scale),
        out_shape=jax.ShapeDtypeStruct((bins, 2, rb, cb), jnp.bfloat16),
        grid=(bins,),
        in_specs=[
            pl.BlockSpec((1, rb, windows), lambda f: (f, 0, 0)),
            pl.BlockSpec((1, rb, windows), lambda f: (f + bins, 0, 0)),
            pl.BlockSpec((1, windows, cb), lambda f: (f, 0, 0)),
            pl.BlockSpec((1, windows, cb), lambda f: (f + bins, 0, 0)),
        ],
        out_specs=pl.BlockSpec((1, 2, rb, cb), lambda f: (f, 0, 0, 0)),
        cost_estimate=pl.CostEstimate(
            flops=8 * bins * rb * cb * windows,
            bytes_accessed=2 * (left.size + right.size + bins * 2 * rb * cb),
            transcendentals=0,
        ),
    )(left, left, right, right)


def solution(mesh):
    placed = (P(("row", "col"), None), P(), P(), P(("row", "col")))
    return jax.shard_map(
        on_device,
        mesh=mesh,
        in_specs=placed,
        out_specs=P(None, None, "row", "col"),
        check_vma=False,
    )
```

```python
import functools
import math

import jax
import jax.numpy as jnp
from jax import lax
from jax.sharding import PartitionSpec as P
from jax.experimental import pallas as pl
from jax.experimental.pallas import tpu as pltpu

F = 16
WL = 1280
TAPS = 101


floor_level = 0.5


def analysis_kernel(fir_taps, bins):
    span = WL + TAPS - 1
    sample_times = jnp.arange(WL, dtype=jnp.int32)
    phase_index = bins[:, None] * sample_times[None, :] % WL
    angles = 2.0 * math.pi / WL * phase_index.astype(jnp.float32)
    centre = (jnp.arange(WL, dtype=jnp.float32) + 0.5) / WL
    window_taper = (0.5 - 0.5 * jnp.cos(2.0 * math.pi * centre)) / math.sqrt(WL)
    pattern = jnp.stack([jnp.cos(angles) * window_taper, -jnp.sin(angles) * window_taper]).reshape(
        2 * F, WL
    )
    lanes = 128
    blocks = pl_cdiv(span, lanes)
    width = 2 * lanes
    padded = jnp.pad(pattern, ((0, 0), (TAPS - 1, blocks * lanes + lanes - WL - (TAPS - 1))))
    windows = jnp.concatenate(
        [
            padded[:, : blocks * lanes].reshape(2 * F, blocks, lanes),
            padded[:, lanes : (blocks + 1) * lanes].reshape(2 * F, blocks, lanes),
        ],
        axis=2,
    )
    vector = jnp.concatenate([fir_taps, jnp.zeros((width + 1 - TAPS,), jnp.float32)])
    band = jnp.tile(vector, lanes)[: lanes * width].reshape(lanes, width)
    kernel = jnp.einsum(
        "bqs,rs->bqr",
        windows,
        band,
        precision=lax.Precision.HIGHEST,
        preferred_element_type=jnp.float32,
    ).reshape(2 * F, blocks * lanes)[:, :span]
    return kernel.astype(jnp.bfloat16)


def pl_cdiv(a, b):
    return (a + b - 1) // b


def whiten(spectra):
    shaped = spectra.reshape(spectra.shape[0], 2, F, spectra.shape[-1])
    magnitude = jnp.sqrt(shaped[:, 0] * shaped[:, 0] + shaped[:, 1] * shaped[:, 1])
    inverse = 1.0 / jnp.maximum(magnitude, floor_level)
    return (shaped * inverse[:, None]).astype(jnp.bfloat16)


MESH = pl.DeviceIdType.MESH


def exchange_kernel(nr, nc, w_ref, rbuf, cbuf, r1, c1, r2, c2, sent, loc):
    r = lax.axis_index("row")
    c = lax.axis_index("col")
    rb = rbuf.shape[-1]
    cb = cbuf.shape[-1]
    nx = nr // 2
    nz = nc // 4
    x, y_lo = r // 2, r % 2
    y_hi, z, core = c // (2 * nz), (c // 2) % nz, c % 2
    sends = []

    def send(src, dst, recv_sem, device):
        cp = pltpu.make_async_remote_copy(
            src_ref=src, dst_ref=dst, send_sem=sent.at[len(sends)], recv_sem=recv_sem,
            device_id=device, device_id_type=MESH,
        )
        cp.start()
        sends.append(cp)

    def arrived(buf, sem, slot):
        pltpu.make_async_copy(buf.at[slot], buf.at[slot], sem.at[slot]).wait()

    own_r = pltpu.make_async_copy(w_ref.at[:, pl.ds(r * rb, rb)], rbuf.at[c, r], loc.at[0])
    own_r.start()
    own_c = pltpu.make_async_copy(w_ref.at[:, pl.ds(c * cb, cb)], cbuf.at[r, c], loc.at[1])
    own_c.start()
    for d in range(1, nr):
        t = lax.rem(r + d, nr)
        send(w_ref.at[:, pl.ds(t * rb, rb)], rbuf.at[c, r], r1.at[r], (t, c))
    for d in range(1, nc):
        t = lax.rem(c + d, nc)
        send(w_ref.at[:, pl.ds(t * cb, cb)], cbuf.at[r, c], c1.at[c], (r, t))

    def ring_col(hi, dz):
        return (hi * nz + lax.rem(z + dz, nz)) * 2 + core

    partner_c = ring_col(1 - y_hi, 0)
    sibling_c = c + 1 - 2 * core
    own_r.wait()
    for d in range(1, nr):
        arrived(rbuf.at[c], r1, lax.rem(r + nr - d, nr))
    send(rbuf.at[c], rbuf.at[c], r2.at[c], (r, partner_c))
    send(rbuf.at[c], rbuf.at[c], r2.at[c], (r, sibling_c))
    for dz in range(1, nz):
        send(rbuf.at[c], rbuf.at[c], r2.at[c], (r, ring_col(y_hi, dz)))

    def ring_row(lo, dx):
        return lax.rem(x + dx, nx) * 2 + lo

    partner_r = ring_row(1 - y_lo, 0)
    own_c.wait()
    for d in range(1, nc):
        arrived(cbuf.at[r], c1, lax.rem(c + nc - d, nc))
    send(cbuf.at[r], cbuf.at[r], c2.at[r], (partner_r, c))
    for dx in range(1, nx):
        send(cbuf.at[r], cbuf.at[r], c2.at[r], (ring_row(y_lo, dx), c))

    arrived(rbuf, r2, partner_c)
    for dz in range(1, nz):
        send(rbuf.at[partner_c], rbuf.at[partner_c], r2.at[partner_c], (r, ring_col(y_hi, dz)))
    arrived(cbuf, c2, partner_r)
    for dx in range(1, nx):
        send(cbuf.at[partner_r], cbuf.at[partner_r], c2.at[partner_r], (ring_row(y_lo, dx), c))

    send(rbuf.at[partner_c], rbuf.at[partner_c], r2.at[partner_c], (r, sibling_c))
    for hi in (y_hi, 1 - y_hi):
        for dz in range(1, nz):
            slot = ring_col(hi, dz)
            arrived(rbuf, r2, slot)
            send(rbuf.at[slot], rbuf.at[slot], r2.at[slot], (r, sibling_c))

    for hi in range(2):
        for zz in range(nz):
            arrived(rbuf, r2, (hi * nz + zz) * 2 + 1 - core)
    for dx in range(1, nx):
        arrived(cbuf, c2, ring_row(y_lo, dx))
        arrived(cbuf, c2, ring_row(1 - y_lo, dx))
    for cp in sends:
        cp.wait_send()


def exchange(w, nr, nc):
    rows, channels = w.shape
    rb = channels // nr
    cb = channels // nc
    dma = pltpu.SemaphoreType.DMA
    return pl.pallas_call(
        functools.partial(exchange_kernel, nr, nc),
        out_shape=(
            jax.ShapeDtypeStruct((nc, nr, rows, rb), w.dtype),
            jax.ShapeDtypeStruct((nr, nc, rows, cb), w.dtype),
        ),
        in_specs=[pl.BlockSpec(memory_space=pl.ANY)],
        out_specs=(pl.BlockSpec(memory_space=pl.ANY), pl.BlockSpec(memory_space=pl.ANY)),
        scratch_shapes=[
            dma((nr,)), dma((nc,)), dma((nc,)), dma((nr,)), dma((2 * (nr + nc),)), dma((2,)),
        ],
        compiler_params=pltpu.CompilerParams(has_side_effects=True),
    )(w)


def on_device(record, fir_taps, bins, offsets):
    kernel = analysis_kernel(fir_taps, bins)
    span = WL + TAPS - 1
    local_count = offsets.shape[0]

    def one_window(window):
        first_row = window * WL + offsets[window]
        samples = lax.dynamic_slice_in_dim(record, first_row, span, 0)
        return jnp.dot(kernel, samples, preferred_element_type=jnp.float32)

    spectra = lax.map(one_window, jnp.arange(local_count, dtype=jnp.int32))
    whitened = whiten(spectra)
    channels = whitened.shape[-1]
    row_count = lax.axis_size("row")
    col_count = lax.axis_size("col")
    total_windows = local_count * row_count * col_count
    row_block, col_block = exchange(
        whitened.reshape(2 * F, channels), row_count, col_count
    )
    windows = row_count * col_count * local_count
    rb = channels // row_count
    cb = channels // col_count
    left = row_block.reshape(windows, 2 * F, rb).transpose(1, 2, 0)
    right = (
        col_block.reshape(row_count, col_count, 2 * F, cb)
        .transpose(2, 1, 0, 3)
        .reshape(2 * F, windows, cb)
    )
    return cross(left, right, 1.0 / total_windows)


def cross_kernel(scale, l0, l1, r0, r1, out_ref):
    def dot(a, b):
        return jnp.dot(a[0], b[0], preferred_element_type=jnp.float32)

    real = dot(l0, r0) + dot(l1, r1)
    imag = dot(l0, r1) - dot(l1, r0)
    out_ref[0, 0] = (real * scale).astype(out_ref.dtype)
    out_ref[0, 1] = (imag * scale).astype(out_ref.dtype)


def cross(left, right, scale):
    parts, rb, windows = left.shape
    cb = right.shape[-1]
    bins = parts // 2
    return pl.pallas_call(
        functools.partial(cross_kernel, scale),
        out_shape=jax.ShapeDtypeStruct((bins, 2, rb, cb), jnp.bfloat16),
        grid=(bins,),
        in_specs=[
            pl.BlockSpec((1, rb, windows), lambda f: (f, 0, 0)),
            pl.BlockSpec((1, rb, windows), lambda f: (f + bins, 0, 0)),
            pl.BlockSpec((1, windows, cb), lambda f: (f, 0, 0)),
            pl.BlockSpec((1, windows, cb), lambda f: (f + bins, 0, 0)),
        ],
        out_specs=pl.BlockSpec((1, 2, rb, cb), lambda f: (f, 0, 0, 0)),
        cost_estimate=pl.CostEstimate(
            flops=8 * bins * rb * cb * windows,
            bytes_accessed=2 * (left.size + right.size + bins * 2 * rb * cb),
            transcendentals=0,
        ),
    )(left, left, right, right)


def solution(mesh):
    placed = (P(("row", "col"), None), P(), P(), P(("row", "col")))
    return jax.shard_map(
        on_device,
        mesh=mesh,
        in_specs=placed,
        out_specs=P(None, None, "row", "col"),
        check_vma=False,
    )
```

```python
import functools
import math

import jax
import jax.numpy as jnp
from jax import lax
from jax.sharding import PartitionSpec as P
from jax.experimental import pallas as pl
from jax.experimental.pallas import tpu as pltpu

F = 16
WL = 1280
TAPS = 101


floor_level = 0.5


def analysis_kernel(fir_taps, bins):
    span = WL + TAPS - 1
    sample_times = jnp.arange(WL, dtype=jnp.int32)
    phase_index = bins[:, None] * sample_times[None, :] % WL
    angles = 2.0 * math.pi / WL * phase_index.astype(jnp.float32)
    centre = (jnp.arange(WL, dtype=jnp.float32) + 0.5) / WL
    window_taper = (0.5 - 0.5 * jnp.cos(2.0 * math.pi * centre)) / math.sqrt(WL)
    pattern = jnp.stack([jnp.cos(angles) * window_taper, -jnp.sin(angles) * window_taper]).reshape(
        2 * F, WL
    )
    lanes = 128
    blocks = pl_cdiv(span, lanes)
    width = 2 * lanes
    padded = jnp.pad(pattern, ((0, 0), (TAPS - 1, blocks * lanes + lanes - WL - (TAPS - 1))))
    windows = jnp.concatenate(
        [
            padded[:, : blocks * lanes].reshape(2 * F, blocks, lanes),
            padded[:, lanes : (blocks + 1) * lanes].reshape(2 * F, blocks, lanes),
        ],
        axis=2,
    )
    vector = jnp.concatenate([fir_taps, jnp.zeros((width + 1 - TAPS,), jnp.float32)])
    band = jnp.tile(vector, lanes)[: lanes * width].reshape(lanes, width)
    kernel = jnp.einsum(
        "bqs,rs->bqr",
        windows,
        band,
        precision=lax.Precision.HIGHEST,
        preferred_element_type=jnp.float32,
    ).reshape(2 * F, blocks * lanes)[:, :span]
    return kernel.astype(jnp.bfloat16)


def pl_cdiv(a, b):
    return (a + b - 1) // b


def whiten(spectra):
    shaped = spectra.reshape(spectra.shape[0], 2, F, spectra.shape[-1])
    magnitude = jnp.sqrt(shaped[:, 0] * shaped[:, 0] + shaped[:, 1] * shaped[:, 1])
    inverse = 1.0 / jnp.maximum(magnitude, floor_level)
    return (shaped * inverse[:, None]).astype(jnp.bfloat16)


MESH = pl.DeviceIdType.MESH


def exchange_kernel(nr, nc, w_ref, rbuf, cbuf, r1, c1, r2, c2, sent, loc):
    r = lax.axis_index("row")
    c = lax.axis_index("col")
    rb = rbuf.shape[-1]
    cb = cbuf.shape[-1]
    nx = nr // 2
    nz = nc // 4
    x, y_lo = r // 2, r % 2
    y_hi, z, core = c // (2 * nz), (c // 2) % nz, c % 2
    sends = []

    def send(src, dst, recv_sem, device):
        cp = pltpu.make_async_remote_copy(
            src_ref=src, dst_ref=dst, send_sem=sent.at[len(sends)], recv_sem=recv_sem,
            device_id=device, device_id_type=MESH,
        )
        cp.start()
        sends.append(cp)

    def arrived(buf, sem, slot):
        pltpu.make_async_copy(buf.at[slot], buf.at[slot], sem.at[slot]).wait()

    own_r = pltpu.make_async_copy(w_ref.at[:, pl.ds(r * rb, rb)], rbuf.at[c, r], loc.at[0])
    own_r.start()
    own_c = pltpu.make_async_copy(w_ref.at[:, pl.ds(c * cb, cb)], cbuf.at[r, c], loc.at[1])
    own_c.start()
    for d in range(1, nr):
        t = lax.rem(r + d, nr)
        send(w_ref.at[:, pl.ds(t * rb, rb)], rbuf.at[c, r], r1.at[r], (t, c))
    for d in range(1, nc):
        t = lax.rem(c + d, nc)
        send(w_ref.at[:, pl.ds(t * cb, cb)], cbuf.at[r, c], c1.at[c], (r, t))

    def ring_col(hi, dz):
        return (hi * nz + lax.rem(z + dz, nz)) * 2 + core

    partner_c = ring_col(1 - y_hi, 0)
    sibling_c = c + 1 - 2 * core
    own_r.wait()
    for d in range(1, nr):
        arrived(rbuf.at[c], r1, lax.rem(r + nr - d, nr))
    send(rbuf.at[c], rbuf.at[c], r2.at[c], (r, partner_c))
    send(rbuf.at[c], rbuf.at[c], r2.at[c], (r, sibling_c))
    for dz in range(1, nz):
        send(rbuf.at[c], rbuf.at[c], r2.at[c], (r, ring_col(y_hi, dz)))

    def ring_row(lo, dx):
        return lax.rem(x + dx, nx) * 2 + lo

    partner_r = ring_row(1 - y_lo, 0)
    own_c.wait()
    for d in range(1, nc):
        arrived(cbuf.at[r], c1, lax.rem(c + nc - d, nc))
    send(cbuf.at[r], cbuf.at[r], c2.at[r], (partner_r, c))
    for dx in range(1, nx):
        send(cbuf.at[r], cbuf.at[r], c2.at[r], (ring_row(y_lo, dx), c))

    arrived(rbuf, r2, partner_c)
    for dz in range(1, nz):
        send(rbuf.at[partner_c], rbuf.at[partner_c], r2.at[partner_c], (r, ring_col(y_hi, dz)))
    arrived(cbuf, c2, partner_r)
    for dx in range(1, nx):
        send(cbuf.at[partner_r], cbuf.at[partner_r], c2.at[partner_r], (ring_row(y_lo, dx), c))

    send(rbuf.at[partner_c], rbuf.at[partner_c], r2.at[partner_c], (r, sibling_c))
    for hi in (y_hi, 1 - y_hi):
        for dz in range(1, nz):
            slot = ring_col(hi, dz)
            arrived(rbuf, r2, slot)
            send(rbuf.at[slot], rbuf.at[slot], r2.at[slot], (r, sibling_c))

    for hi in range(2):
        for zz in range(nz):
            arrived(rbuf, r2, (hi * nz + zz) * 2 + 1 - core)
    for dx in range(1, nx):
        arrived(cbuf, c2, ring_row(y_lo, dx))
        arrived(cbuf, c2, ring_row(1 - y_lo, dx))
    for cp in sends:
        cp.wait_send()


def exchange(w, nr, nc):
    rows, channels = w.shape
    rb = channels // nr
    cb = channels // nc
    dma = pltpu.SemaphoreType.DMA
    return pl.pallas_call(
        functools.partial(exchange_kernel, nr, nc),
        out_shape=(
            jax.ShapeDtypeStruct((nc, nr, rows, rb), w.dtype),
            jax.ShapeDtypeStruct((nr, nc, rows, cb), w.dtype),
        ),
        in_specs=[pl.BlockSpec(memory_space=pl.ANY)],
        out_specs=(pl.BlockSpec(memory_space=pl.ANY), pl.BlockSpec(memory_space=pl.ANY)),
        scratch_shapes=[
            dma((nr,)), dma((nc,)), dma((nc,)), dma((nr,)), dma((2 * (nr + nc),)), dma((2,)),
        ],
        compiler_params=pltpu.CompilerParams(has_side_effects=True),
    )(w)


def on_device(record, fir_taps, bins, offsets):
    kernel = analysis_kernel(fir_taps, bins)
    span = WL + TAPS - 1
    local_count = offsets.shape[0]

    def one_window(window):
        first_row = window * WL + offsets[window]
        samples = lax.dynamic_slice_in_dim(record, first_row, span, 0)
        return jnp.dot(kernel, samples, preferred_element_type=jnp.float32)

    spectra = lax.map(one_window, jnp.arange(local_count, dtype=jnp.int32))
    whitened = whiten(spectra)
    channels = whitened.shape[-1]
    row_count = lax.axis_size("row")
    col_count = lax.axis_size("col")
    total_windows = local_count * row_count * col_count
    row_block, col_block = exchange(
        whitened.reshape(2 * F, channels), row_count, col_count
    )
    windows = row_count * col_count * local_count
    rb = channels // row_count
    cb = channels // col_count
    left = row_block.reshape(windows, 2 * F, rb).transpose(1, 0, 2)
    right = (
        col_block.reshape(row_count, col_count, 2 * F, cb)
        .transpose(2, 1, 0, 3)
        .reshape(2 * F, windows, cb)
    )
    return cross(left, right, 1.0 / total_windows)


def cross_kernel(scale, l0, l1, r0, r1, out_ref):
    cb = r0.shape[-1]
    lhs = jnp.concatenate([l0[0], l1[0]], axis=0)
    rhs = jnp.concatenate(
        [
            jnp.concatenate([r0[0], r1[0]], axis=1),
            jnp.concatenate([r1[0], -r0[0]], axis=1),
        ],
        axis=0,
    )
    both = lax.dot_general(
        lhs, rhs, (((0,), (0,)), ((), ())), preferred_element_type=jnp.float32
    )
    out_ref[0, 0] = (both[:, :cb] * scale).astype(out_ref.dtype)
    out_ref[0, 1] = (both[:, cb:] * scale).astype(out_ref.dtype)


def cross(left, right, scale):
    parts, windows, rb = left.shape
    cb = right.shape[-1]
    bins = parts // 2
    return pl.pallas_call(
        functools.partial(cross_kernel, scale),
        out_shape=jax.ShapeDtypeStruct((bins, 2, rb, cb), jnp.bfloat16),
        grid=(bins,),
        in_specs=[
            pl.BlockSpec((1, windows, rb), lambda f: (f, 0, 0)),
            pl.BlockSpec((1, windows, rb), lambda f: (f + bins, 0, 0)),
            pl.BlockSpec((1, windows, cb), lambda f: (f, 0, 0)),
            pl.BlockSpec((1, windows, cb), lambda f: (f + bins, 0, 0)),
        ],
        out_specs=pl.BlockSpec((1, 2, rb, cb), lambda f: (f, 0, 0, 0)),
        cost_estimate=pl.CostEstimate(
            flops=8 * bins * rb * cb * windows,
            bytes_accessed=2 * (left.size + right.size + bins * 2 * rb * cb),
            transcendentals=0,
        ),
    )(left, left, right, right)


def solution(mesh):
    placed = (P(("row", "col"), None), P(), P(), P(("row", "col")))
    return jax.shard_map(
        on_device,
        mesh=mesh,
        in_specs=placed,
        out_specs=P(None, None, "row", "col"),
        check_vma=False,
    )
```

```python
import functools
import math

import jax
import jax.numpy as jnp
from jax import lax
from jax.sharding import PartitionSpec as P
from jax.experimental import pallas as pl
from jax.experimental.pallas import tpu as pltpu

F = 16
WL = 1280
TAPS = 101


floor_level = 0.5


def analysis_kernel(fir_taps, bins):
    span = WL + TAPS - 1
    sample_times = jnp.arange(WL, dtype=jnp.int32)
    phase_index = bins[:, None] * sample_times[None, :] % WL
    angles = 2.0 * math.pi / WL * phase_index.astype(jnp.float32)
    centre = (jnp.arange(WL, dtype=jnp.float32) + 0.5) / WL
    window_taper = (0.5 - 0.5 * jnp.cos(2.0 * math.pi * centre)) / math.sqrt(WL)
    pattern = jnp.stack([jnp.cos(angles) * window_taper, -jnp.sin(angles) * window_taper]).reshape(
        2 * F, WL
    )
    lanes = 128
    blocks = pl_cdiv(span, lanes)
    width = 2 * lanes
    padded = jnp.pad(pattern, ((0, 0), (TAPS - 1, blocks * lanes + lanes - WL - (TAPS - 1))))
    windows = jnp.concatenate(
        [
            padded[:, : blocks * lanes].reshape(2 * F, blocks, lanes),
            padded[:, lanes : (blocks + 1) * lanes].reshape(2 * F, blocks, lanes),
        ],
        axis=2,
    )
    vector = jnp.concatenate([fir_taps, jnp.zeros((width + 1 - TAPS,), jnp.float32)])
    band = jnp.tile(vector, lanes)[: lanes * width].reshape(lanes, width)
    kernel = jnp.einsum(
        "bqs,rs->bqr",
        windows,
        band,
        precision=lax.Precision.HIGHEST,
        preferred_element_type=jnp.float32,
    ).reshape(2 * F, blocks * lanes)[:, :span]
    return kernel.astype(jnp.bfloat16)


def pl_cdiv(a, b):
    return (a + b - 1) // b


def whiten(spectra):
    shaped = spectra.reshape(spectra.shape[0], 2, F, spectra.shape[-1])
    magnitude = jnp.sqrt(shaped[:, 0] * shaped[:, 0] + shaped[:, 1] * shaped[:, 1])
    inverse = 1.0 / jnp.maximum(magnitude, floor_level)
    return (shaped * inverse[:, None]).astype(jnp.bfloat16)


MESH = pl.DeviceIdType.MESH


def exchange_kernel(nr, nc, w_ref, rbuf, cbuf, r1, c1, r2, c2, sent, loc):
    r = lax.axis_index("row")
    c = lax.axis_index("col")
    rb = rbuf.shape[-1]
    cb = cbuf.shape[-1]
    nx = nr // 2
    nz = nc // 4
    x, y_lo = r // 2, r % 2
    y_hi, z, core = c // (2 * nz), (c // 2) % nz, c % 2
    sends = []

    def send(src, dst, recv_sem, device):
        cp = pltpu.make_async_remote_copy(
            src_ref=src, dst_ref=dst, send_sem=sent.at[len(sends)], recv_sem=recv_sem,
            device_id=device, device_id_type=MESH,
        )
        cp.start()
        sends.append(cp)

    def arrived(buf, sem, slot):
        pltpu.make_async_copy(buf.at[slot], buf.at[slot], sem.at[slot]).wait()

    own_r = pltpu.make_async_copy(w_ref.at[:, pl.ds(r * rb, rb)], rbuf.at[c, r], loc.at[0])
    own_r.start()
    own_c = pltpu.make_async_copy(w_ref.at[:, pl.ds(c * cb, cb)], cbuf.at[r, c], loc.at[1])
    own_c.start()
    for d in range(1, nr):
        t = lax.rem(r + d, nr)
        send(w_ref.at[:, pl.ds(t * rb, rb)], rbuf.at[c, r], r1.at[r], (t, c))
    for d in range(1, nc):
        t = lax.rem(c + d, nc)
        send(w_ref.at[:, pl.ds(t * cb, cb)], cbuf.at[r, c], c1.at[c], (r, t))

    step = 1 - 2 * core

    def col_slot(hi, dz):
        return (hi * nz + lax.rem(z + dz + nz, nz)) * 2 + core

    def row_slot(lo, dx):
        return lax.rem(x + dx + nx, nx) * 2 + lo

    sibling_c = c + 1 - 2 * core

    def to_cols(slot, targets):
        for t in targets:
            send(rbuf.at[slot], rbuf.at[slot], r2.at[slot], (r, t))

    def to_rows(slot, targets):
        for t in targets:
            send(cbuf.at[slot], cbuf.at[slot], c2.at[slot], (t, c))

    partner_c = col_slot(1 - y_hi, 0)
    ring_c = [col_slot(y_hi, 1), col_slot(y_hi, -1)]
    own_r.wait()
    for d in range(1, nr):
        arrived(rbuf.at[c], r1, lax.rem(r + nr - d, nr))
    to_cols(c, [partner_c, sibling_c] + ring_c)

    partner_r = row_slot(1 - y_lo, 0)
    ring_r = [row_slot(y_lo, 1), row_slot(y_lo, -1)]
    own_c.wait()
    for d in range(1, nc):
        arrived(cbuf.at[r], c1, lax.rem(c + nc - d, nc))
    to_rows(r, [partner_r] + ring_r)

    arrived(rbuf, r2, partner_c)
    to_cols(partner_c, ring_c + [sibling_c])
    arrived(cbuf, c2, partner_r)
    to_rows(partner_r, ring_r)

    for hi in (y_hi, 1 - y_hi):
        slot = col_slot(hi, -step)
        arrived(rbuf, r2, slot)
        to_cols(slot, [col_slot(y_hi, step), sibling_c])
    for lo in (y_lo, 1 - y_lo):
        slot = row_slot(lo, -step)
        arrived(cbuf, c2, slot)
        to_rows(slot, [row_slot(y_lo, step)])
    for dz in (1, 2):
        for hi in (y_hi, 1 - y_hi):
            slot = col_slot(hi, step * dz)
            arrived(rbuf, r2, slot)
            to_cols(slot, [sibling_c])

    for hi in range(2):
        for zz in range(nz):
            arrived(rbuf, r2, (hi * nz + zz) * 2 + 1 - core)
    for dx in (1, 2):
        for lo in (y_lo, 1 - y_lo):
            arrived(cbuf, c2, row_slot(lo, step * dx))
    for cp in sends:
        cp.wait_send()


def exchange(w, nr, nc):
    rows, channels = w.shape
    rb = channels // nr
    cb = channels // nc
    dma = pltpu.SemaphoreType.DMA
    return pl.pallas_call(
        functools.partial(exchange_kernel, nr, nc),
        out_shape=(
            jax.ShapeDtypeStruct((nc, nr, rows, rb), w.dtype),
            jax.ShapeDtypeStruct((nr, nc, rows, cb), w.dtype),
        ),
        in_specs=[pl.BlockSpec(memory_space=pl.ANY)],
        out_specs=(pl.BlockSpec(memory_space=pl.ANY), pl.BlockSpec(memory_space=pl.ANY)),
        scratch_shapes=[
            dma((nr,)), dma((nc,)), dma((nc,)), dma((nr,)), dma((2 * (nr + nc),)), dma((2,)),
        ],
        compiler_params=pltpu.CompilerParams(has_side_effects=True),
    )(w)


def on_device(record, fir_taps, bins, offsets):
    kernel = analysis_kernel(fir_taps, bins)
    span = WL + TAPS - 1
    local_count = offsets.shape[0]

    def one_window(window):
        first_row = window * WL + offsets[window]
        samples = lax.dynamic_slice_in_dim(record, first_row, span, 0)
        return jnp.dot(kernel, samples, preferred_element_type=jnp.float32)

    spectra = lax.map(one_window, jnp.arange(local_count, dtype=jnp.int32))
    whitened = whiten(spectra)
    channels = whitened.shape[-1]
    row_count = lax.axis_size("row")
    col_count = lax.axis_size("col")
    total_windows = local_count * row_count * col_count
    row_block, col_block = exchange(
        whitened.reshape(2 * F, channels), row_count, col_count
    )
    windows = row_count * col_count * local_count
    rb = channels // row_count
    cb = channels // col_count
    left = row_block.reshape(windows, 2 * F, rb).transpose(1, 0, 2)
    right = (
        col_block.reshape(row_count, col_count, 2 * F, cb)
        .transpose(2, 1, 0, 3)
        .reshape(2 * F, windows, cb)
    )
    return cross(left, right, 1.0 / total_windows)


def cross_kernel(scale, l0, l1, r0, r1, out_ref):
    cb = r0.shape[-1]
    lhs = jnp.concatenate([l0[0], l1[0]], axis=0)
    rhs = jnp.concatenate(
        [
            jnp.concatenate([r0[0], r1[0]], axis=1),
            jnp.concatenate([r1[0], -r0[0]], axis=1),
        ],
        axis=0,
    )
    both = lax.dot_general(
        lhs, rhs, (((0,), (0,)), ((), ())), preferred_element_type=jnp.float32
    )
    out_ref[0, 0] = (both[:, :cb] * scale).astype(out_ref.dtype)
    out_ref[0, 1] = (both[:, cb:] * scale).astype(out_ref.dtype)


def cross(left, right, scale):
    parts, windows, rb = left.shape
    cb = right.shape[-1]
    bins = parts // 2
    return pl.pallas_call(
        functools.partial(cross_kernel, scale),
        out_shape=jax.ShapeDtypeStruct((bins, 2, rb, cb), jnp.bfloat16),
        grid=(bins,),
        in_specs=[
            pl.BlockSpec((1, windows, rb), lambda f: (f, 0, 0)),
            pl.BlockSpec((1, windows, rb), lambda f: (f + bins, 0, 0)),
            pl.BlockSpec((1, windows, cb), lambda f: (f, 0, 0)),
            pl.BlockSpec((1, windows, cb), lambda f: (f + bins, 0, 0)),
        ],
        out_specs=pl.BlockSpec((1, 2, rb, cb), lambda f: (f, 0, 0, 0)),
        cost_estimate=pl.CostEstimate(
            flops=8 * bins * rb * cb * windows,
            bytes_accessed=2 * (left.size + right.size + bins * 2 * rb * cb),
            transcendentals=0,
        ),
    )(left, left, right, right)


def solution(mesh):
    placed = (P(("row", "col"), None), P(), P(), P(("row", "col")))
    return jax.shard_map(
        on_device,
        mesh=mesh,
        in_specs=placed,
        out_specs=P(None, None, "row", "col"),
        check_vma=False,
    )
```

```python
import functools
import math

import jax
import jax.numpy as jnp
from jax import lax
from jax.sharding import PartitionSpec as P
from jax.experimental import pallas as pl
from jax.experimental.pallas import tpu as pltpu

F = 16
WL = 1280
TAPS = 101


floor_level = 0.5


def analysis_kernel(fir_taps, bins):
    span = WL + TAPS - 1
    sample_times = jnp.arange(WL, dtype=jnp.int32)
    phase_index = bins[:, None] * sample_times[None, :] % WL
    angles = 2.0 * math.pi / WL * phase_index.astype(jnp.float32)
    centre = (jnp.arange(WL, dtype=jnp.float32) + 0.5) / WL
    window_taper = (0.5 - 0.5 * jnp.cos(2.0 * math.pi * centre)) / math.sqrt(WL)
    pattern = jnp.stack([jnp.cos(angles) * window_taper, -jnp.sin(angles) * window_taper]).reshape(
        2 * F, WL
    )
    lanes = 128
    blocks = pl_cdiv(span, lanes)
    width = 2 * lanes
    padded = jnp.pad(pattern, ((0, 0), (TAPS - 1, blocks * lanes + lanes - WL - (TAPS - 1))))
    windows = jnp.concatenate(
        [
            padded[:, : blocks * lanes].reshape(2 * F, blocks, lanes),
            padded[:, lanes : (blocks + 1) * lanes].reshape(2 * F, blocks, lanes),
        ],
        axis=2,
    )
    vector = jnp.concatenate([fir_taps, jnp.zeros((width + 1 - TAPS,), jnp.float32)])
    band = jnp.tile(vector, lanes)[: lanes * width].reshape(lanes, width)
    kernel = jnp.einsum(
        "bqs,rs->bqr",
        windows,
        band,
        precision=lax.Precision.HIGHEST,
        preferred_element_type=jnp.float32,
    ).reshape(2 * F, blocks * lanes)[:, :span]
    return kernel.astype(jnp.bfloat16)


def pl_cdiv(a, b):
    return (a + b - 1) // b


def whiten(spectra):
    shaped = spectra.reshape(spectra.shape[0], 2, F, spectra.shape[-1])
    magnitude = jnp.sqrt(shaped[:, 0] * shaped[:, 0] + shaped[:, 1] * shaped[:, 1])
    inverse = 1.0 / jnp.maximum(magnitude, floor_level)
    return (shaped * inverse[:, None]).astype(jnp.bfloat16)


MESH = pl.DeviceIdType.MESH


def exchange_kernel(nr, nc, w_ref, rbuf, cbuf, r1, c1, r2, c2, sent, loc):
    r = lax.axis_index("row")
    c = lax.axis_index("col")
    rb = rbuf.shape[-1]
    cb = cbuf.shape[-1]
    nx = nr // 2
    nz = nc // 4
    x, y_lo = r // 2, r % 2
    y_hi, z, core = c // (2 * nz), (c // 2) % nz, c % 2
    sends = []

    def send(src, dst, recv_sem, device):
        cp = pltpu.make_async_remote_copy(
            src_ref=src, dst_ref=dst, send_sem=sent.at[len(sends)], recv_sem=recv_sem,
            device_id=device, device_id_type=MESH,
        )
        cp.start()
        sends.append(cp)

    def arrived(buf, sem, slot):
        if buf is cbuf:
            pltpu.make_async_copy(buf.at[:, slot], buf.at[:, slot], sem.at[slot]).wait()
        else:
            pltpu.make_async_copy(buf.at[slot], buf.at[slot], sem.at[slot]).wait()

    own_r = pltpu.make_async_copy(w_ref.at[:, pl.ds(r * rb, rb)], rbuf.at[c, r], loc.at[0])
    own_r.start()
    own_c = pltpu.make_async_copy(w_ref.at[:, pl.ds(c * cb, cb)], cbuf.at[c, r], loc.at[1])
    own_c.start()
    for d in range(1, nr):
        t = lax.rem(r + d, nr)
        send(w_ref.at[:, pl.ds(t * rb, rb)], rbuf.at[c, r], r1.at[r], (t, c))
    for d in range(1, nc):
        t = lax.rem(c + d, nc)
        send(w_ref.at[:, pl.ds(t * cb, cb)], cbuf.at[c, r], c1.at[c], (r, t))

    step = 1 - 2 * core

    def col_slot(hi, dz):
        return (hi * nz + lax.rem(z + dz + nz, nz)) * 2 + core

    def row_slot(lo, dx):
        return lax.rem(x + dx + nx, nx) * 2 + lo

    sibling_c = c + 1 - 2 * core

    def to_cols(slot, targets):
        for t in targets:
            send(rbuf.at[slot], rbuf.at[slot], r2.at[slot], (r, t))

    def to_rows(slot, targets):
        for t in targets:
            send(cbuf.at[:, slot], cbuf.at[:, slot], c2.at[slot], (t, c))

    partner_c = col_slot(1 - y_hi, 0)
    ring_c = [col_slot(y_hi, 1), col_slot(y_hi, -1)]
    own_r.wait()
    for d in range(1, nr):
        arrived(rbuf.at[c], r1, lax.rem(r + nr - d, nr))
    to_cols(c, [partner_c, sibling_c] + ring_c)

    partner_r = row_slot(1 - y_lo, 0)
    ring_r = [row_slot(y_lo, 1), row_slot(y_lo, -1)]
    own_c.wait()
    for d in range(1, nc):
        src = lax.rem(c + nc - d, nc)
        pltpu.make_async_copy(cbuf.at[src, r], cbuf.at[src, r], c1.at[src]).wait()
    to_rows(r, [partner_r] + ring_r)

    arrived(rbuf, r2, partner_c)
    to_cols(partner_c, ring_c + [sibling_c])
    arrived(cbuf, c2, partner_r)
    to_rows(partner_r, ring_r)

    for hi in (y_hi, 1 - y_hi):
        slot = col_slot(hi, -step)
        arrived(rbuf, r2, slot)
        to_cols(slot, [col_slot(y_hi, step), sibling_c])
    for lo in (y_lo, 1 - y_lo):
        slot = row_slot(lo, -step)
        arrived(cbuf, c2, slot)
        to_rows(slot, [row_slot(y_lo, step)])
    for dz in (1, 2):
        for hi in (y_hi, 1 - y_hi):
            slot = col_slot(hi, step * dz)
            arrived(rbuf, r2, slot)
            to_cols(slot, [sibling_c])

    for hi in range(2):
        for zz in range(nz):
            arrived(rbuf, r2, (hi * nz + zz) * 2 + 1 - core)
    for dx in (1, 2):
        for lo in (y_lo, 1 - y_lo):
            arrived(cbuf, c2, row_slot(lo, step * dx))
    for cp in sends:
        cp.wait_send()


def exchange(w, nr, nc):
    rows, channels = w.shape
    rb = channels // nr
    cb = channels // nc
    dma = pltpu.SemaphoreType.DMA
    return pl.pallas_call(
        functools.partial(exchange_kernel, nr, nc),
        out_shape=(
            jax.ShapeDtypeStruct((nc, nr, rows, rb), w.dtype),
            jax.ShapeDtypeStruct((nc, nr, rows, cb), w.dtype),
        ),
        in_specs=[pl.BlockSpec(memory_space=pl.ANY)],
        out_specs=(pl.BlockSpec(memory_space=pl.ANY), pl.BlockSpec(memory_space=pl.ANY)),
        scratch_shapes=[
            dma((nr,)), dma((nc,)), dma((nc,)), dma((nr,)), dma((2 * (nr + nc),)), dma((2,)),
        ],
        compiler_params=pltpu.CompilerParams(has_side_effects=True),
    )(w)


def on_device(record, fir_taps, bins, offsets):
    kernel = analysis_kernel(fir_taps, bins)
    span = WL + TAPS - 1
    local_count = offsets.shape[0]

    def one_window(window):
        first_row = window * WL + offsets[window]
        samples = lax.dynamic_slice_in_dim(record, first_row, span, 0)
        return jnp.dot(kernel, samples, preferred_element_type=jnp.float32)

    spectra = lax.map(one_window, jnp.arange(local_count, dtype=jnp.int32))
    whitened = whiten(spectra)
    channels = whitened.shape[-1]
    row_count = lax.axis_size("row")
    col_count = lax.axis_size("col")
    total_windows = local_count * row_count * col_count
    row_block, col_block = exchange(
        whitened.reshape(2 * F, channels), row_count, col_count
    )
    windows = row_count * col_count * local_count
    rb = channels // row_count
    cb = channels // col_count
    left = row_block.reshape(windows, 2 * F, rb)
    right = col_block.reshape(windows, 2 * F, cb)
    return cross(left, right, 1.0 / total_windows)


def cross_kernel(scale, l_ref, r_ref, out_ref):
    f = pl.program_id(0)
    for fixed in range(l_ref.shape[1] // 2):

        @pl.when(f == fixed)
        def _():
            one_bin(scale, fixed, l_ref.shape[1] // 2, l_ref, r_ref, out_ref)


def one_bin(scale, f, bins, l_ref, r_ref, out_ref):
    cb = r_ref.shape[-1]
    l0, l1 = l_ref[:, f, :], l_ref[:, f + bins, :]
    r0, r1 = r_ref[:, f, :], r_ref[:, f + bins, :]
    lhs = jnp.concatenate([l0, l1], axis=0)
    rhs = jnp.concatenate(
        [jnp.concatenate([r0, r1], axis=1), jnp.concatenate([r1, -r0], axis=1)], axis=0
    )
    both = lax.dot_general(
        lhs, rhs, (((0,), (0,)), ((), ())), preferred_element_type=jnp.float32
    )
    out_ref[0, 0] = (both[:, :cb] * scale).astype(out_ref.dtype)
    out_ref[0, 1] = (both[:, cb:] * scale).astype(out_ref.dtype)


def cross(left, right, scale):
    windows, parts, rb = left.shape
    cb = right.shape[-1]
    bins = parts // 2
    return pl.pallas_call(
        functools.partial(cross_kernel, scale),
        out_shape=jax.ShapeDtypeStruct((bins, 2, rb, cb), jnp.bfloat16),
        grid=(bins,),
        in_specs=[
            pl.BlockSpec((windows, parts, rb), lambda f: (0, 0, 0)),
            pl.BlockSpec((windows, parts, cb), lambda f: (0, 0, 0)),
        ],
        out_specs=pl.BlockSpec((1, 2, rb, cb), lambda f: (f, 0, 0, 0)),
        cost_estimate=pl.CostEstimate(
            flops=8 * bins * rb * cb * windows,
            bytes_accessed=2 * (left.size + right.size + bins * 2 * rb * cb),
            transcendentals=0,
        ),
    )(left, right)


def solution(mesh):
    placed = (P(("row", "col"), None), P(), P(), P(("row", "col")))
    return jax.shard_map(
        on_device,
        mesh=mesh,
        in_specs=placed,
        out_specs=P(None, None, "row", "col"),
        check_vma=False,
    )
```

```python
import functools
import math

import jax
import jax.numpy as jnp
from jax import lax
from jax.sharding import PartitionSpec as P
from jax.experimental import pallas as pl
from jax.experimental.pallas import tpu as pltpu

F = 16
WL = 1280
TAPS = 101


floor_level = 0.5


def analysis_kernel(fir_taps, bins):
    span = WL + TAPS - 1
    sample_times = jnp.arange(WL, dtype=jnp.int32)
    phase_index = bins[:, None] * sample_times[None, :] % WL
    angles = 2.0 * math.pi / WL * phase_index.astype(jnp.float32)
    centre = (jnp.arange(WL, dtype=jnp.float32) + 0.5) / WL
    window_taper = (0.5 - 0.5 * jnp.cos(2.0 * math.pi * centre)) / math.sqrt(WL)
    pattern = jnp.stack([jnp.cos(angles) * window_taper, -jnp.sin(angles) * window_taper]).reshape(
        2 * F, WL
    )
    lanes = 128
    blocks = pl_cdiv(span, lanes)
    width = 2 * lanes
    padded = jnp.pad(pattern, ((0, 0), (TAPS - 1, blocks * lanes + lanes - WL - (TAPS - 1))))
    windows = jnp.concatenate(
        [
            padded[:, : blocks * lanes].reshape(2 * F, blocks, lanes),
            padded[:, lanes : (blocks + 1) * lanes].reshape(2 * F, blocks, lanes),
        ],
        axis=2,
    )
    vector = jnp.concatenate([fir_taps, jnp.zeros((width + 1 - TAPS,), jnp.float32)])
    band = jnp.tile(vector, lanes)[: lanes * width].reshape(lanes, width)
    kernel = jnp.einsum(
        "bqs,rs->bqr",
        windows,
        band,
        precision=lax.Precision.HIGHEST,
        preferred_element_type=jnp.float32,
    ).reshape(2 * F, blocks * lanes)[:, :span]
    return kernel.astype(jnp.bfloat16)


def pl_cdiv(a, b):
    return (a + b - 1) // b


def whiten(spectra):
    shaped = spectra.reshape(spectra.shape[0], 2, F, spectra.shape[-1])
    magnitude = jnp.sqrt(shaped[:, 0] * shaped[:, 0] + shaped[:, 1] * shaped[:, 1])
    inverse = 1.0 / jnp.maximum(magnitude, floor_level)
    return (shaped * inverse[:, None]).astype(jnp.bfloat16)


MESH = pl.DeviceIdType.MESH


def exchange_kernel(nr, nc, w_ref, rbuf, cbuf, r1, c1, r2, c2, sent, loc):
    r = lax.axis_index("row")
    c = lax.axis_index("col")
    rb = rbuf.shape[-1]
    cb = cbuf.shape[-1]
    nx = nr // 2
    nz = nc // 4
    x, y_lo = r // 2, r % 2
    y_hi, z, core = c // (2 * nz), (c // 2) % nz, c % 2
    sends = []

    def send(src, dst, recv_sem, device):
        cp = pltpu.make_async_remote_copy(
            src_ref=src, dst_ref=dst, send_sem=sent.at[len(sends)], recv_sem=recv_sem,
            device_id=device, device_id_type=MESH,
        )
        cp.start()
        sends.append(cp)

    def arrived(buf, sem, slot):
        if buf is cbuf:
            pltpu.make_async_copy(buf.at[:, slot], buf.at[:, slot], sem.at[slot]).wait()
        else:
            pltpu.make_async_copy(buf.at[slot], buf.at[slot], sem.at[slot]).wait()

    own_r = pltpu.make_async_copy(w_ref.at[:, pl.ds(r * rb, rb)], rbuf.at[c, r], loc.at[0])
    own_r.start()
    own_c = pltpu.make_async_copy(w_ref.at[:, pl.ds(c * cb, cb)], cbuf.at[c, r], loc.at[1])
    own_c.start()
    for d in range(1, nr):
        t = lax.rem(r + d, nr)
        send(w_ref.at[:, pl.ds(t * rb, rb)], rbuf.at[c, r], r1.at[r], (t, c))
    for d in range(1, nc):
        t = lax.rem(c + d, nc)
        send(w_ref.at[:, pl.ds(t * cb, cb)], cbuf.at[c, r], c1.at[c], (r, t))

    step = 1 - 2 * core

    def col_slot(hi, dz):
        return (hi * nz + lax.rem(z + dz + nz, nz)) * 2 + core

    def row_slot(lo, dx):
        return lax.rem(x + dx + nx, nx) * 2 + lo

    sibling_c = c + 1 - 2 * core

    def to_cols(slot, targets):
        for t in targets:
            send(rbuf.at[slot], rbuf.at[slot], r2.at[slot], (r, t))

    def to_rows(slot, targets):
        for t in targets:
            send(cbuf.at[:, slot], cbuf.at[:, slot], c2.at[slot], (t, c))

    partner_c = col_slot(1 - y_hi, 0)
    ring_c = [col_slot(y_hi, 1), col_slot(y_hi, -1)]
    own_r.wait()
    for d in range(1, nr):
        arrived(rbuf.at[c], r1, lax.rem(r + nr - d, nr))
    to_cols(c, [partner_c, sibling_c] + ring_c)

    partner_r = row_slot(1 - y_lo, 0)
    ring_r = [row_slot(y_lo, 1), row_slot(y_lo, -1)]
    own_c.wait()
    for d in range(1, nc):
        src = lax.rem(c + nc - d, nc)
        pltpu.make_async_copy(cbuf.at[src, r], cbuf.at[src, r], c1.at[src]).wait()
    to_rows(r, [partner_r] + ring_r)

    arrived(rbuf, r2, partner_c)
    to_cols(partner_c, ring_c + [sibling_c])
    arrived(cbuf, c2, partner_r)
    to_rows(partner_r, ring_r)

    for hi in (y_hi, 1 - y_hi):
        slot = col_slot(hi, -step)
        arrived(rbuf, r2, slot)
        to_cols(slot, [col_slot(y_hi, step), sibling_c])
    for lo in (y_lo, 1 - y_lo):
        slot = row_slot(lo, -step)
        arrived(cbuf, c2, slot)
        to_rows(slot, [row_slot(y_lo, step)])
    for dz in (1, 2):
        for hi in (y_hi, 1 - y_hi):
            slot = col_slot(hi, step * dz)
            arrived(rbuf, r2, slot)
            to_cols(slot, [sibling_c])

    for hi in range(2):
        for zz in range(nz):
            arrived(rbuf, r2, (hi * nz + zz) * 2 + 1 - core)
    for dx in (1, 2):
        for lo in (y_lo, 1 - y_lo):
            arrived(cbuf, c2, row_slot(lo, step * dx))
    for cp in sends:
        cp.wait_send()


def exchange(w, nr, nc):
    rows, channels = w.shape
    rb = channels // nr
    cb = channels // nc
    dma = pltpu.SemaphoreType.DMA
    return pl.pallas_call(
        functools.partial(exchange_kernel, nr, nc),
        out_shape=(
            jax.ShapeDtypeStruct((nc, nr, rows, rb), w.dtype),
            jax.ShapeDtypeStruct((nc, nr, rows, cb), w.dtype),
        ),
        in_specs=[pl.BlockSpec(memory_space=pl.ANY)],
        out_specs=(pl.BlockSpec(memory_space=pl.ANY), pl.BlockSpec(memory_space=pl.ANY)),
        scratch_shapes=[
            dma((nr,)), dma((nc,)), dma((nc,)), dma((nr,)), dma((2 * (nr + nc),)), dma((2,)),
        ],
        compiler_params=pltpu.CompilerParams(has_side_effects=True),
    )(w)


def on_device(record, fir_taps, bins, offsets):
    kernel = analysis_kernel(fir_taps, bins)
    span = WL + TAPS - 1
    local_count = offsets.shape[0]

    def one_window(window):
        first_row = window * WL + offsets[window]
        samples = lax.dynamic_slice_in_dim(record, first_row, span, 0)
        return jnp.dot(kernel, samples, preferred_element_type=jnp.float32)

    spectra = lax.map(one_window, jnp.arange(local_count, dtype=jnp.int32))
    whitened = whiten(spectra)
    channels = whitened.shape[-1]
    row_count = lax.axis_size("row")
    col_count = lax.axis_size("col")
    total_windows = local_count * row_count * col_count
    row_block, col_block = exchange(
        whitened.reshape(2 * F, channels), row_count, col_count
    )
    windows = row_count * col_count * local_count
    rb = channels // row_count
    cb = channels // col_count
    left = row_block.reshape(windows, 2 * F, rb)
    right = col_block.reshape(windows, 2 * F, cb)
    return cross(left, right, 1.0 / total_windows)


def cross_kernel(scale, l_ref, r_ref, out_ref, lt, rt):
    f = pl.program_id(0)
    bins = pl.num_programs(0)
    cb = r_ref.shape[-1]

    @pl.when(f == 0)
    def _():
        lt[...] = pltpu.einshape("nkc->knc", l_ref[...])
        rt[...] = pltpu.einshape("nkc->knc", r_ref[...])

    l0, l1 = lt[f], lt[f + bins]
    r0, r1 = rt[f], rt[f + bins]
    lhs = jnp.concatenate([l0, l1], axis=0)
    rhs = jnp.concatenate(
        [jnp.concatenate([r0, r1], axis=1), jnp.concatenate([r1, -r0], axis=1)], axis=0
    )
    both = lax.dot_general(
        lhs, rhs, (((0,), (0,)), ((), ())), preferred_element_type=jnp.float32
    )
    out_ref[0, 0] = (both[:, :cb] * scale).astype(out_ref.dtype)
    out_ref[0, 1] = (both[:, cb:] * scale).astype(out_ref.dtype)


def cross(left, right, scale):
    windows, parts, rb = left.shape
    cb = right.shape[-1]
    bins = parts // 2
    return pl.pallas_call(
        functools.partial(cross_kernel, scale),
        out_shape=jax.ShapeDtypeStruct((bins, 2, rb, cb), jnp.bfloat16),
        grid=(bins,),
        in_specs=[
            pl.BlockSpec((windows, parts, rb), lambda f: (0, 0, 0)),
            pl.BlockSpec((windows, parts, cb), lambda f: (0, 0, 0)),
        ],
        out_specs=pl.BlockSpec((1, 2, rb, cb), lambda f: (f, 0, 0, 0)),
        scratch_shapes=[
            pltpu.VMEM((parts, windows, rb), left.dtype),
            pltpu.VMEM((parts, windows, cb), right.dtype),
        ],
        cost_estimate=pl.CostEstimate(
            flops=8 * bins * rb * cb * windows,
            bytes_accessed=2 * (left.size + right.size + bins * 2 * rb * cb),
            transcendentals=0,
        ),
    )(left, right)


def solution(mesh):
    placed = (P(("row", "col"), None), P(), P(), P(("row", "col")))
    return jax.shard_map(
        on_device,
        mesh=mesh,
        in_specs=placed,
        out_specs=P(None, None, "row", "col"),
        check_vma=False,
    )
```

```python
import functools
import math

import jax
import jax.numpy as jnp
from jax import lax
from jax.sharding import PartitionSpec as P
from jax.experimental import pallas as pl
from jax.experimental.pallas import tpu as pltpu

F = 16
WL = 1280
TAPS = 101


floor_level = 0.5


def analysis_kernel(fir_taps, bins):
    span = WL + TAPS - 1
    sample_times = jnp.arange(WL, dtype=jnp.int32)
    phase_index = bins[:, None] * sample_times[None, :] % WL
    angles = 2.0 * math.pi / WL * phase_index.astype(jnp.float32)
    centre = (jnp.arange(WL, dtype=jnp.float32) + 0.5) / WL
    window_taper = (0.5 - 0.5 * jnp.cos(2.0 * math.pi * centre)) / math.sqrt(WL)
    pattern = jnp.stack(
        [jnp.cos(angles) * window_taper, -jnp.sin(angles) * window_taper], axis=1
    ).reshape(2 * F, WL)
    lanes = 128
    blocks = pl_cdiv(span, lanes)
    width = 2 * lanes
    padded = jnp.pad(pattern, ((0, 0), (TAPS - 1, blocks * lanes + lanes - WL - (TAPS - 1))))
    windows = jnp.concatenate(
        [
            padded[:, : blocks * lanes].reshape(2 * F, blocks, lanes),
            padded[:, lanes : (blocks + 1) * lanes].reshape(2 * F, blocks, lanes),
        ],
        axis=2,
    )
    vector = jnp.concatenate([fir_taps, jnp.zeros((width + 1 - TAPS,), jnp.float32)])
    band = jnp.tile(vector, lanes)[: lanes * width].reshape(lanes, width)
    kernel = jnp.einsum(
        "bqs,rs->bqr",
        windows,
        band,
        precision=lax.Precision.HIGHEST,
        preferred_element_type=jnp.float32,
    ).reshape(2 * F, blocks * lanes)[:, :span]
    return kernel.astype(jnp.bfloat16)


def pl_cdiv(a, b):
    return (a + b - 1) // b


def whiten(spectra):
    shaped = spectra.reshape(spectra.shape[0], F, 2, spectra.shape[-1])
    magnitude = jnp.sqrt(shaped[:, :, 0] * shaped[:, :, 0] + shaped[:, :, 1] * shaped[:, :, 1])
    inverse = 1.0 / jnp.maximum(magnitude, floor_level)
    return (shaped * inverse[:, :, None]).astype(jnp.bfloat16)


MESH = pl.DeviceIdType.MESH


def exchange_kernel(nr, nc, w_ref, rbuf, cbuf, r1, c1, r2, c2, sent, loc):
    r = lax.axis_index("row")
    c = lax.axis_index("col")
    rb = rbuf.shape[-1]
    cb = cbuf.shape[-1]
    nx = nr // 2
    nz = nc // 4
    x, y_lo = r // 2, r % 2
    y_hi, z, core = c // (2 * nz), (c // 2) % nz, c % 2
    sends = []

    def send(src, dst, recv_sem, device):
        cp = pltpu.make_async_remote_copy(
            src_ref=src, dst_ref=dst, send_sem=sent.at[len(sends)], recv_sem=recv_sem,
            device_id=device, device_id_type=MESH,
        )
        cp.start()
        sends.append(cp)

    def arrived(buf, sem, slot):
        if buf is cbuf:
            pltpu.make_async_copy(buf.at[:, slot], buf.at[:, slot], sem.at[slot]).wait()
        else:
            pltpu.make_async_copy(buf.at[slot], buf.at[slot], sem.at[slot]).wait()

    own_r = pltpu.make_async_copy(w_ref.at[:, pl.ds(r * rb, rb)], rbuf.at[c, r], loc.at[0])
    own_r.start()
    own_c = pltpu.make_async_copy(w_ref.at[:, pl.ds(c * cb, cb)], cbuf.at[c, r], loc.at[1])
    own_c.start()
    for d in range(1, nr):
        t = lax.rem(r + d, nr)
        send(w_ref.at[:, pl.ds(t * rb, rb)], rbuf.at[c, r], r1.at[r], (t, c))
    for d in range(1, nc):
        t = lax.rem(c + d, nc)
        send(w_ref.at[:, pl.ds(t * cb, cb)], cbuf.at[c, r], c1.at[c], (r, t))

    step = 1 - 2 * core

    def col_slot(hi, dz):
        return (hi * nz + lax.rem(z + dz + nz, nz)) * 2 + core

    def row_slot(lo, dx):
        return lax.rem(x + dx + nx, nx) * 2 + lo

    sibling_c = c + 1 - 2 * core

    def to_cols(slot, targets):
        for t in targets:
            send(rbuf.at[slot], rbuf.at[slot], r2.at[slot], (r, t))

    def to_rows(slot, targets):
        for t in targets:
            send(cbuf.at[:, slot], cbuf.at[:, slot], c2.at[slot], (t, c))

    partner_c = col_slot(1 - y_hi, 0)
    ring_c = [col_slot(y_hi, 1), col_slot(y_hi, -1)]
    own_r.wait()
    for d in range(1, nr):
        arrived(rbuf.at[c], r1, lax.rem(r + nr - d, nr))
    to_cols(c, [partner_c, sibling_c] + ring_c)

    partner_r = row_slot(1 - y_lo, 0)
    ring_r = [row_slot(y_lo, 1), row_slot(y_lo, -1)]
    own_c.wait()
    for d in range(1, nc):
        src = lax.rem(c + nc - d, nc)
        pltpu.make_async_copy(cbuf.at[src, r], cbuf.at[src, r], c1.at[src]).wait()
    to_rows(r, [partner_r] + ring_r)

    arrived(rbuf, r2, partner_c)
    to_cols(partner_c, ring_c + [sibling_c])
    arrived(cbuf, c2, partner_r)
    to_rows(partner_r, ring_r)

    for hi in (y_hi, 1 - y_hi):
        slot = col_slot(hi, -step)
        arrived(rbuf, r2, slot)
        to_cols(slot, [col_slot(y_hi, step), sibling_c])
    for lo in (y_lo, 1 - y_lo):
        slot = row_slot(lo, -step)
        arrived(cbuf, c2, slot)
        to_rows(slot, [row_slot(y_lo, step)])
    for dz in (1, 2):
        for hi in (y_hi, 1 - y_hi):
            slot = col_slot(hi, step * dz)
            arrived(rbuf, r2, slot)
            to_cols(slot, [sibling_c])

    for hi in range(2):
        for zz in range(nz):
            arrived(rbuf, r2, (hi * nz + zz) * 2 + 1 - core)
    for dx in (1, 2):
        for lo in (y_lo, 1 - y_lo):
            arrived(cbuf, c2, row_slot(lo, step * dx))
    for cp in sends:
        cp.wait_send()


def exchange(w, nr, nc):
    rows, channels = w.shape
    rb = channels // nr
    cb = channels // nc
    dma = pltpu.SemaphoreType.DMA
    return pl.pallas_call(
        functools.partial(exchange_kernel, nr, nc),
        out_shape=(
            jax.ShapeDtypeStruct((nc, nr, rows, rb), w.dtype),
            jax.ShapeDtypeStruct((nc, nr, rows, cb), w.dtype),
        ),
        in_specs=[pl.BlockSpec(memory_space=pl.ANY)],
        out_specs=(pl.BlockSpec(memory_space=pl.ANY), pl.BlockSpec(memory_space=pl.ANY)),
        scratch_shapes=[
            dma((nr,)), dma((nc,)), dma((nc,)), dma((nr,)), dma((2 * (nr + nc),)), dma((2,)),
        ],
        compiler_params=pltpu.CompilerParams(has_side_effects=True),
    )(w)


def on_device(record, fir_taps, bins, offsets):
    kernel = analysis_kernel(fir_taps, bins)
    span = WL + TAPS - 1
    local_count = offsets.shape[0]

    def one_window(window):
        first_row = window * WL + offsets[window]
        samples = lax.dynamic_slice_in_dim(record, first_row, span, 0)
        return jnp.dot(kernel, samples, preferred_element_type=jnp.float32)

    spectra = lax.map(one_window, jnp.arange(local_count, dtype=jnp.int32))
    whitened = whiten(spectra)
    channels = whitened.shape[-1]
    row_count = lax.axis_size("row")
    col_count = lax.axis_size("col")
    total_windows = local_count * row_count * col_count
    row_block, col_block = exchange(
        whitened.reshape(2 * F, channels), row_count, col_count
    )
    windows = row_count * col_count * local_count
    rb = channels // row_count
    cb = channels // col_count
    left = row_block.reshape(windows, 2 * F, rb)
    right = col_block.reshape(windows, 2 * F, cb)
    return cross(left, right, 1.0 / total_windows)


def cross_kernel(scale, group, l_ref, r_ref, out_ref, lt, rt):
    f = pl.program_id(0)
    cb = r_ref.shape[-1]
    within = lax.rem(f, group)

    @pl.when(within == 0)
    def _():
        lt[...] = pltpu.einshape("nkc->knc", l_ref[...])
        rt[...] = pltpu.einshape("nkc->knc", r_ref[...])

    l0, l1 = lt[2 * within], lt[2 * within + 1]
    r0, r1 = rt[2 * within], rt[2 * within + 1]
    lhs = jnp.concatenate([l0, l1], axis=0)
    rhs = jnp.concatenate(
        [jnp.concatenate([r0, r1], axis=1), jnp.concatenate([r1, -r0], axis=1)], axis=0
    )
    both = lax.dot_general(
        lhs, rhs, (((0,), (0,)), ((), ())), preferred_element_type=jnp.float32
    )
    out_ref[0, 0] = (both[:, :cb] * scale).astype(out_ref.dtype)
    out_ref[0, 1] = (both[:, cb:] * scale).astype(out_ref.dtype)


def cross(left, right, scale):
    windows, parts, rb = left.shape
    cb = right.shape[-1]
    bins = parts // 2
    group = 4
    rows = 2 * group
    return pl.pallas_call(
        functools.partial(cross_kernel, scale, group),
        out_shape=jax.ShapeDtypeStruct((bins, 2, rb, cb), jnp.bfloat16),
        grid=(bins,),
        in_specs=[
            pl.BlockSpec((windows, rows, rb), lambda f: (0, f // group, 0)),
            pl.BlockSpec((windows, rows, cb), lambda f: (0, f // group, 0)),
        ],
        out_specs=pl.BlockSpec((1, 2, rb, cb), lambda f: (f, 0, 0, 0)),
        scratch_shapes=[
            pltpu.VMEM((rows, windows, rb), left.dtype),
            pltpu.VMEM((rows, windows, cb), right.dtype),
        ],
        cost_estimate=pl.CostEstimate(
            flops=8 * bins * rb * cb * windows,
            bytes_accessed=2 * (left.size + right.size + bins * 2 * rb * cb),
            transcendentals=0,
        ),
    )(left, right)


def solution(mesh):
    placed = (P(("row", "col"), None), P(), P(), P(("row", "col")))
    return jax.shard_map(
        on_device,
        mesh=mesh,
        in_specs=placed,
        out_specs=P(None, None, "row", "col"),
        check_vma=False,
    )
```

```python
import functools
import math

import jax
import jax.numpy as jnp
from jax import lax
from jax.sharding import PartitionSpec as P
from jax.experimental import pallas as pl
from jax.experimental.pallas import tpu as pltpu

F = 16
WL = 1280
TAPS = 101


floor_level = 0.5


def analysis_kernel(fir_taps, bins):
    span = WL + TAPS - 1
    sample_times = jnp.arange(WL, dtype=jnp.int32)
    phase_index = bins[:, None] * sample_times[None, :] % WL
    angles = 2.0 * math.pi / WL * phase_index.astype(jnp.float32)
    centre = (jnp.arange(WL, dtype=jnp.float32) + 0.5) / WL
    window_taper = (0.5 - 0.5 * jnp.cos(2.0 * math.pi * centre)) / math.sqrt(WL)
    pattern = jnp.stack([jnp.cos(angles) * window_taper, -jnp.sin(angles) * window_taper]).reshape(
        2 * F, WL
    )
    lanes = 128
    blocks = pl_cdiv(span, lanes)
    width = 2 * lanes
    padded = jnp.pad(pattern, ((0, 0), (TAPS - 1, blocks * lanes + lanes - WL - (TAPS - 1))))
    windows = jnp.concatenate(
        [
            padded[:, : blocks * lanes].reshape(2 * F, blocks, lanes),
            padded[:, lanes : (blocks + 1) * lanes].reshape(2 * F, blocks, lanes),
        ],
        axis=2,
    )
    vector = jnp.concatenate([fir_taps, jnp.zeros((width + 1 - TAPS,), jnp.float32)])
    band = jnp.tile(vector, lanes)[: lanes * width].reshape(lanes, width)
    kernel = jnp.einsum(
        "bqs,rs->bqr",
        windows,
        band,
        precision=lax.Precision.HIGHEST,
        preferred_element_type=jnp.float32,
    ).reshape(2 * F, blocks * lanes)[:, :span]
    return kernel.astype(jnp.bfloat16)


def pl_cdiv(a, b):
    return (a + b - 1) // b


def whiten(spectra):
    shaped = spectra.reshape(spectra.shape[0], 2, F, spectra.shape[-1])
    magnitude = jnp.sqrt(shaped[:, 0] * shaped[:, 0] + shaped[:, 1] * shaped[:, 1])
    inverse = 1.0 / jnp.maximum(magnitude, floor_level)
    return (shaped * inverse[:, None]).astype(jnp.bfloat16)


MESH = pl.DeviceIdType.MESH


def exchange_kernel(nr, nc, w_ref, rbuf, cbuf, r1, c1, r2, c2, sent, loc):
    r = lax.axis_index("row")
    c = lax.axis_index("col")
    rb = rbuf.shape[-1]
    cb = cbuf.shape[-1]
    nx = nr // 2
    nz = nc // 4
    x, y_lo = r // 2, r % 2
    y_hi, z, core = c // (2 * nz), (c // 2) % nz, c % 2
    sends = []

    def send(src, dst, recv_sem, device):
        cp = pltpu.make_async_remote_copy(
            src_ref=src, dst_ref=dst, send_sem=sent.at[len(sends)], recv_sem=recv_sem,
            device_id=device, device_id_type=MESH,
        )
        cp.start()
        sends.append(cp)

    def arrived(buf, sem, slot):
        if buf is cbuf:
            pltpu.make_async_copy(buf.at[:, slot], buf.at[:, slot], sem.at[slot]).wait()
        else:
            pltpu.make_async_copy(buf.at[slot], buf.at[slot], sem.at[slot]).wait()

    own_r = pltpu.make_async_copy(w_ref.at[:, pl.ds(r * rb, rb)], rbuf.at[c, r], loc.at[0])
    own_r.start()
    own_c = pltpu.make_async_copy(w_ref.at[:, pl.ds(c * cb, cb)], cbuf.at[c, r], loc.at[1])
    own_c.start()
    for d in range(1, nr):
        t = lax.rem(r + d, nr)
        send(w_ref.at[:, pl.ds(t * rb, rb)], rbuf.at[c, r], r1.at[r], (t, c))
    for d in range(1, nc):
        t = lax.rem(c + d, nc)
        send(w_ref.at[:, pl.ds(t * cb, cb)], cbuf.at[c, r], c1.at[c], (r, t))

    step = 1 - 2 * core

    def col_slot(hi, dz):
        return (hi * nz + lax.rem(z + dz + nz, nz)) * 2 + core

    def row_slot(lo, dx):
        return lax.rem(x + dx + nx, nx) * 2 + lo

    sibling_c = c + 1 - 2 * core

    def to_cols(slot, targets):
        for t in targets:
            send(rbuf.at[slot], rbuf.at[slot], r2.at[slot], (r, t))

    def to_rows(slot, targets):
        for t in targets:
            send(cbuf.at[:, slot], cbuf.at[:, slot], c2.at[slot], (t, c))

    partner_c = col_slot(1 - y_hi, 0)
    ring_c = [col_slot(y_hi, 1), col_slot(y_hi, -1)]
    own_r.wait()
    for d in range(1, nr):
        arrived(rbuf.at[c], r1, lax.rem(r + nr - d, nr))
    to_cols(c, [partner_c, sibling_c] + ring_c)

    partner_r = row_slot(1 - y_lo, 0)
    ring_r = [row_slot(y_lo, 1), row_slot(y_lo, -1)]
    own_c.wait()
    for d in range(1, nc):
        src = lax.rem(c + nc - d, nc)
        pltpu.make_async_copy(cbuf.at[src, r], cbuf.at[src, r], c1.at[src]).wait()
    to_rows(r, [partner_r] + ring_r)

    arrived(rbuf, r2, partner_c)
    to_cols(partner_c, ring_c + [sibling_c])
    arrived(cbuf, c2, partner_r)
    to_rows(partner_r, ring_r)

    for hi in (y_hi, 1 - y_hi):
        slot = col_slot(hi, -step)
        arrived(rbuf, r2, slot)
        to_cols(slot, [col_slot(y_hi, step), sibling_c])
    for lo in (y_lo, 1 - y_lo):
        slot = row_slot(lo, -step)
        arrived(cbuf, c2, slot)
        to_rows(slot, [row_slot(y_lo, step)])
    for dz in (1, 2):
        for hi in (y_hi, 1 - y_hi):
            slot = col_slot(hi, step * dz)
            arrived(rbuf, r2, slot)
            to_cols(slot, [sibling_c])

    for hi in range(2):
        for zz in range(nz):
            arrived(rbuf, r2, (hi * nz + zz) * 2 + 1 - core)
    for dx in (1, 2):
        for lo in (y_lo, 1 - y_lo):
            arrived(cbuf, c2, row_slot(lo, step * dx))
    for cp in sends:
        cp.wait_send()


def exchange(w, nr, nc):
    rows, channels = w.shape
    rb = channels // nr
    cb = channels // nc
    dma = pltpu.SemaphoreType.DMA
    return pl.pallas_call(
        functools.partial(exchange_kernel, nr, nc),
        out_shape=(
            jax.ShapeDtypeStruct((nc, nr, rows, rb), w.dtype),
            jax.ShapeDtypeStruct((nc, nr, rows, cb), w.dtype),
        ),
        in_specs=[pl.BlockSpec(memory_space=pl.ANY)],
        out_specs=(pl.BlockSpec(memory_space=pl.ANY), pl.BlockSpec(memory_space=pl.ANY)),
        scratch_shapes=[
            dma((nr,)), dma((nc,)), dma((nc,)), dma((nr,)), dma((2 * (nr + nc),)), dma((2,)),
        ],
        compiler_params=pltpu.CompilerParams(has_side_effects=True),
    )(w)


def on_device(record, fir_taps, bins, offsets):
    kernel = analysis_kernel(fir_taps, bins)
    span = WL + TAPS - 1
    local_count = offsets.shape[0]

    assert local_count == 1
    placed = lax.dynamic_update_slice(
        jnp.zeros((kernel.shape[0], record.shape[0]), kernel.dtype), kernel, (0, offsets[0])
    )
    spectra = jnp.dot(placed, record, preferred_element_type=jnp.float32)[None]
    whitened = whiten(spectra)
    channels = whitened.shape[-1]
    row_count = lax.axis_size("row")
    col_count = lax.axis_size("col")
    total_windows = local_count * row_count * col_count
    row_block, col_block = exchange(
        whitened.reshape(2 * F, channels), row_count, col_count
    )
    windows = row_count * col_count * local_count
    rb = channels // row_count
    cb = channels // col_count
    left = row_block.reshape(windows, 2 * F, rb)
    right = col_block.reshape(windows, 2 * F, cb)
    return cross(left, right, 1.0 / total_windows)


def cross_kernel(scale, l_ref, r_ref, out_ref, lt, rt):
    f = pl.program_id(0)
    bins = pl.num_programs(0)
    cb = r_ref.shape[-1]

    @pl.when(f == 0)
    def _():
        lt[...] = pltpu.einshape("nkc->knc", l_ref[...])
        rt[...] = pltpu.einshape("nkc->knc", r_ref[...])

    l0, l1 = lt[f], lt[f + bins]
    r0, r1 = rt[f], rt[f + bins]
    lhs = jnp.concatenate([l0, l1], axis=0)
    rhs = jnp.concatenate(
        [jnp.concatenate([r0, r1], axis=1), jnp.concatenate([r1, -r0], axis=1)], axis=0
    )
    both = lax.dot_general(
        lhs, rhs, (((0,), (0,)), ((), ())), preferred_element_type=jnp.float32
    )
    out_ref[0, 0] = (both[:, :cb] * scale).astype(out_ref.dtype)
    out_ref[0, 1] = (both[:, cb:] * scale).astype(out_ref.dtype)


def cross(left, right, scale):
    windows, parts, rb = left.shape
    cb = right.shape[-1]
    bins = parts // 2
    return pl.pallas_call(
        functools.partial(cross_kernel, scale),
        out_shape=jax.ShapeDtypeStruct((bins, 2, rb, cb), jnp.bfloat16),
        grid=(bins,),
        in_specs=[
            pl.BlockSpec((windows, parts, rb), lambda f: (0, 0, 0)),
            pl.BlockSpec((windows, parts, cb), lambda f: (0, 0, 0)),
        ],
        out_specs=pl.BlockSpec((1, 2, rb, cb), lambda f: (f, 0, 0, 0)),
        scratch_shapes=[
            pltpu.VMEM((parts, windows, rb), left.dtype),
            pltpu.VMEM((parts, windows, cb), right.dtype),
        ],
        cost_estimate=pl.CostEstimate(
            flops=8 * bins * rb * cb * windows,
            bytes_accessed=2 * (left.size + right.size + bins * 2 * rb * cb),
            transcendentals=0,
        ),
    )(left, right)


def solution(mesh):
    placed = (P(("row", "col"), None), P(), P(), P(("row", "col")))
    return jax.shard_map(
        on_device,
        mesh=mesh,
        in_specs=placed,
        out_specs=P(None, None, "row", "col"),
        check_vma=False,
    )
```

```python
import functools
import math

import jax
import jax.numpy as jnp
from jax import lax
from jax.sharding import PartitionSpec as P
from jax.experimental import pallas as pl
from jax.experimental.pallas import tpu as pltpu

F = 16
WL = 1280
TAPS = 101


floor_level = 0.5


def analysis_kernel(fir_taps, bins):
    span = WL + TAPS - 1
    sample_times = jnp.arange(WL, dtype=jnp.int32)
    phase_index = bins[:, None] * sample_times[None, :] % WL
    angles = 2.0 * math.pi / WL * phase_index.astype(jnp.float32)
    centre = (jnp.arange(WL, dtype=jnp.float32) + 0.5) / WL
    window_taper = (0.5 - 0.5 * jnp.cos(2.0 * math.pi * centre)) / math.sqrt(WL)
    pattern = jnp.stack([jnp.cos(angles) * window_taper, -jnp.sin(angles) * window_taper]).reshape(
        2 * F, WL
    )
    lanes = 128
    blocks = pl_cdiv(span, lanes)
    width = 2 * lanes
    padded = jnp.pad(pattern, ((0, 0), (TAPS - 1, blocks * lanes + lanes - WL - (TAPS - 1))))
    windows = jnp.concatenate(
        [
            padded[:, : blocks * lanes].reshape(2 * F, blocks, lanes),
            padded[:, lanes : (blocks + 1) * lanes].reshape(2 * F, blocks, lanes),
        ],
        axis=2,
    )
    vector = jnp.concatenate([fir_taps, jnp.zeros((width + 1 - TAPS,), jnp.float32)])
    band = jnp.tile(vector, lanes)[: lanes * width].reshape(lanes, width)
    kernel = jnp.einsum(
        "bqs,rs->bqr",
        windows,
        band,
        precision=lax.Precision.HIGHEST,
        preferred_element_type=jnp.float32,
    ).reshape(2 * F, blocks * lanes)[:, :span]
    return kernel.astype(jnp.bfloat16)


def pl_cdiv(a, b):
    return (a + b - 1) // b


def whiten(spectra):
    shaped = spectra.reshape(spectra.shape[0], 2, F, spectra.shape[-1])
    magnitude = jnp.sqrt(shaped[:, 0] * shaped[:, 0] + shaped[:, 1] * shaped[:, 1])
    inverse = 1.0 / jnp.maximum(magnitude, floor_level)
    return (shaped * inverse[:, None]).astype(jnp.bfloat16)


MESH = pl.DeviceIdType.MESH


def exchange_kernel(nr, nc, w_ref, rbuf, cbuf, r1, c1, r2, c2, sent, loc):
    r = lax.axis_index("row")
    c = lax.axis_index("col")
    rb = rbuf.shape[-1]
    cb = cbuf.shape[-1]
    nx = nr // 2
    nz = nc // 4
    x, y_lo = r // 2, r % 2
    y_hi, z, core = c // (2 * nz), (c // 2) % nz, c % 2
    sends = []

    def send(src, dst, recv_sem, device):
        cp = pltpu.make_async_remote_copy(
            src_ref=src, dst_ref=dst, send_sem=sent.at[len(sends)], recv_sem=recv_sem,
            device_id=device, device_id_type=MESH,
        )
        cp.start()
        sends.append(cp)

    def arrived(buf, sem, slot):
        if buf is cbuf:
            pltpu.make_async_copy(buf.at[:, slot], buf.at[:, slot], sem.at[slot]).wait()
        else:
            pltpu.make_async_copy(buf.at[slot], buf.at[slot], sem.at[slot]).wait()

    own_r = pltpu.make_async_copy(w_ref.at[:, pl.ds(r * rb, rb)], rbuf.at[c, r], loc.at[0])
    own_r.start()
    own_c = pltpu.make_async_copy(w_ref.at[:, pl.ds(c * cb, cb)], cbuf.at[c, r], loc.at[1])
    own_c.start()
    for d in range(1, nr):
        t = lax.rem(r + d, nr)
        send(w_ref.at[:, pl.ds(t * rb, rb)], rbuf.at[c, r], r1.at[r], (t, c))
    for d in range(1, nc):
        t = lax.rem(c + d, nc)
        send(w_ref.at[:, pl.ds(t * cb, cb)], cbuf.at[c, r], c1.at[c], (r, t))

    step = 1 - 2 * core

    def col_slot(hi, dz):
        return (hi * nz + lax.rem(z + dz + nz, nz)) * 2 + core

    def row_slot(lo, dx):
        return lax.rem(x + dx + nx, nx) * 2 + lo

    sibling_c = c + 1 - 2 * core

    def to_cols(slot, targets):
        for t in targets:
            send(rbuf.at[slot], rbuf.at[slot], r2.at[slot], (r, t))

    def to_rows(slot, targets):
        for t in targets:
            send(cbuf.at[:, slot], cbuf.at[:, slot], c2.at[slot], (t, c))

    partner_c = col_slot(1 - y_hi, 0)
    ring_c = [col_slot(y_hi, 1), col_slot(y_hi, -1)]
    own_r.wait()
    for d in range(1, nr):
        arrived(rbuf.at[c], r1, lax.rem(r + nr - d, nr))
    to_cols(c, [partner_c, sibling_c] + ring_c)

    partner_r = row_slot(1 - y_lo, 0)
    ring_r = [row_slot(y_lo, 1), row_slot(y_lo, -1)]
    own_c.wait()
    for d in range(1, nc):
        src = lax.rem(c + nc - d, nc)
        pltpu.make_async_copy(cbuf.at[src, r], cbuf.at[src, r], c1.at[src]).wait()
    to_rows(r, [partner_r] + ring_r)

    arrived(rbuf, r2, partner_c)
    to_cols(partner_c, ring_c + [sibling_c])
    arrived(cbuf, c2, partner_r)
    to_rows(partner_r, ring_r)

    for hi in (y_hi, 1 - y_hi):
        slot = col_slot(hi, -step)
        arrived(rbuf, r2, slot)
        to_cols(slot, [col_slot(y_hi, step), sibling_c])
    for lo in (y_lo, 1 - y_lo):
        slot = row_slot(lo, -step)
        arrived(cbuf, c2, slot)
        to_rows(slot, [row_slot(y_lo, step)])
    for dz in (1, 2):
        for hi in (y_hi, 1 - y_hi):
            slot = col_slot(hi, step * dz)
            arrived(rbuf, r2, slot)
            to_cols(slot, [sibling_c])

    for hi in range(2):
        for zz in range(nz):
            arrived(rbuf, r2, (hi * nz + zz) * 2 + 1 - core)
    for dx in (1, 2):
        for lo in (y_lo, 1 - y_lo):
            arrived(cbuf, c2, row_slot(lo, step * dx))
    for cp in sends:
        cp.wait_send()


def exchange(w, nr, nc):
    rows, channels = w.shape
    rb = channels // nr
    cb = channels // nc
    dma = pltpu.SemaphoreType.DMA
    return pl.pallas_call(
        functools.partial(exchange_kernel, nr, nc),
        out_shape=(
            jax.ShapeDtypeStruct((nc, nr, rows, rb), w.dtype),
            jax.ShapeDtypeStruct((nc, nr, rows, cb), w.dtype),
        ),
        in_specs=[pl.BlockSpec(memory_space=pl.ANY)],
        out_specs=(pl.BlockSpec(memory_space=pl.ANY), pl.BlockSpec(memory_space=pl.ANY)),
        scratch_shapes=[
            dma((nr,)), dma((nc,)), dma((nc,)), dma((nr,)), dma((2 * (nr + nc),)), dma((2,)),
        ],
        compiler_params=pltpu.CompilerParams(has_side_effects=True),
    )(w)


def on_device(record, fir_taps, bins, offsets):
    kernel = analysis_kernel(fir_taps, bins)
    span = WL + TAPS - 1
    local_count = offsets.shape[0]

    assert local_count == 1
    placed = lax.dynamic_update_slice(
        jnp.zeros((kernel.shape[0], record.shape[0]), kernel.dtype), kernel, (0, offsets[0])
    )
    spectra = jnp.dot(placed, record, preferred_element_type=jnp.float32)[None]
    whitened = whiten(spectra)
    channels = whitened.shape[-1]
    row_count = lax.axis_size("row")
    col_count = lax.axis_size("col")
    total_windows = local_count * row_count * col_count
    row_block, col_block = exchange(
        whitened.reshape(2 * F, channels), row_count, col_count
    )
    windows = row_count * col_count * local_count
    rb = channels // row_count
    cb = channels // col_count
    left = row_block.reshape(windows, 2 * F, rb)
    right = col_block.reshape(windows, 2 * F, cb)
    return cross(left, right, 1.0 / total_windows)


def cross_kernel(scale, chunks, l_hbm, r_hbm, out_ref, l_in, r_in, lt, rt, sems):
    f = pl.program_id(0)
    bins = pl.num_programs(0)
    cb = r_hbm.shape[-1]
    size = l_hbm.shape[0] // chunks

    @pl.when(f == 0)
    def _():
        copies = []
        for i in range(chunks):
            part = pl.ds(i * size, size)
            for j, (src, dst) in enumerate(((l_hbm, l_in), (r_hbm, r_in))):
                cp = pltpu.make_async_copy(src.at[part], dst.at[part], sems.at[j, i])
                cp.start()
                copies.append(cp)
        for i in range(chunks):
            part = pl.ds(i * size, size)
            copies[2 * i].wait()
            lt[:, part, :] = pltpu.einshape("nkc->knc", l_in[part])
            copies[2 * i + 1].wait()
            rt[:, part, :] = pltpu.einshape("nkc->knc", r_in[part])

    l0, l1 = lt[f], lt[f + bins]
    r0, r1 = rt[f], rt[f + bins]
    lhs = jnp.concatenate([l0, l1], axis=0)
    rhs = jnp.concatenate(
        [jnp.concatenate([r0, r1], axis=1), jnp.concatenate([r1, -r0], axis=1)], axis=0
    )
    both = lax.dot_general(
        lhs, rhs, (((0,), (0,)), ((), ())), preferred_element_type=jnp.float32
    )
    out_ref[0, 0] = (both[:, :cb] * scale).astype(out_ref.dtype)
    out_ref[0, 1] = (both[:, cb:] * scale).astype(out_ref.dtype)


def cross(left, right, scale):
    windows, parts, rb = left.shape
    cb = right.shape[-1]
    bins = parts // 2
    chunks = 8
    return pl.pallas_call(
        functools.partial(cross_kernel, scale, chunks),
        out_shape=jax.ShapeDtypeStruct((bins, 2, rb, cb), jnp.bfloat16),
        grid=(bins,),
        in_specs=[pl.BlockSpec(memory_space=pl.ANY), pl.BlockSpec(memory_space=pl.ANY)],
        out_specs=pl.BlockSpec((1, 2, rb, cb), lambda f: (f, 0, 0, 0)),
        scratch_shapes=[
            pltpu.VMEM((windows, parts, rb), left.dtype),
            pltpu.VMEM((windows, parts, cb), right.dtype),
            pltpu.VMEM((parts, windows, rb), left.dtype),
            pltpu.VMEM((parts, windows, cb), right.dtype),
            pltpu.SemaphoreType.DMA((2, chunks)),
        ],
        cost_estimate=pl.CostEstimate(
            flops=8 * bins * rb * cb * windows,
            bytes_accessed=2 * (left.size + right.size + bins * 2 * rb * cb),
            transcendentals=0,
        ),
    )(left, right)


def solution(mesh):
    placed = (P(("row", "col"), None), P(), P(), P(("row", "col")))
    return jax.shard_map(
        on_device,
        mesh=mesh,
        in_specs=placed,
        out_specs=P(None, None, "row", "col"),
        check_vma=False,
    )
```

```python
import functools
import math

import jax
import jax.numpy as jnp
from jax import lax
from jax.sharding import PartitionSpec as P
from jax.experimental import pallas as pl
from jax.experimental.pallas import tpu as pltpu

F = 16
WL = 1280
TAPS = 101


floor_level = 0.5


def analysis_kernel(fir_taps, bins, offset, length):
    span = WL + TAPS - 1
    sample_times = jnp.arange(WL, dtype=jnp.int32)
    phase_index = bins[:, None] * sample_times[None, :] % WL
    angles = 2.0 * math.pi / WL * phase_index.astype(jnp.float32)
    centre = (jnp.arange(WL, dtype=jnp.float32) + 0.5) / WL
    window_taper = (0.5 - 0.5 * jnp.cos(2.0 * math.pi * centre)) / math.sqrt(WL)
    pattern = jnp.stack([jnp.cos(angles) * window_taper, -jnp.sin(angles) * window_taper]).reshape(
        2 * F, WL
    )
    lanes = 128
    blocks = pl_cdiv(length, lanes)
    width = 2 * lanes
    padded = lax.dynamic_update_slice(
        jnp.zeros((2 * F, (blocks + 1) * lanes), jnp.float32), pattern, (0, TAPS - 1 + offset)
    )
    windows = jnp.concatenate(
        [
            padded[:, : blocks * lanes].reshape(2 * F, blocks, lanes),
            padded[:, lanes : (blocks + 1) * lanes].reshape(2 * F, blocks, lanes),
        ],
        axis=2,
    )
    vector = jnp.concatenate([fir_taps, jnp.zeros((width + 1 - TAPS,), jnp.float32)])
    band = jnp.tile(vector, lanes)[: lanes * width].reshape(lanes, width)
    kernel = jnp.einsum(
        "bqs,rs->bqr",
        windows,
        band,
        precision=lax.Precision.HIGHEST,
        preferred_element_type=jnp.float32,
    ).reshape(2 * F, blocks * lanes)[:, :length]
    return kernel.astype(jnp.bfloat16)


def pl_cdiv(a, b):
    return (a + b - 1) // b


def whiten(spectra):
    shaped = spectra.reshape(spectra.shape[0], 2, F, spectra.shape[-1])
    magnitude = jnp.sqrt(shaped[:, 0] * shaped[:, 0] + shaped[:, 1] * shaped[:, 1])
    inverse = 1.0 / jnp.maximum(magnitude, floor_level)
    return (shaped * inverse[:, None]).astype(jnp.bfloat16)


MESH = pl.DeviceIdType.MESH


def exchange_kernel(nr, nc, w_ref, rbuf, cbuf, r1, c1, r2, c2, sent, loc):
    r = lax.axis_index("row")
    c = lax.axis_index("col")
    rb = rbuf.shape[-1]
    cb = cbuf.shape[-1]
    nx = nr // 2
    nz = nc // 4
    x, y_lo = r // 2, r % 2
    y_hi, z, core = c // (2 * nz), (c // 2) % nz, c % 2
    sends = []

    def send(src, dst, recv_sem, device):
        cp = pltpu.make_async_remote_copy(
            src_ref=src, dst_ref=dst, send_sem=sent.at[len(sends)], recv_sem=recv_sem,
            device_id=device, device_id_type=MESH,
        )
        cp.start()
        sends.append(cp)

    def arrived(buf, sem, slot):
        if buf is cbuf:
            pltpu.make_async_copy(buf.at[:, slot], buf.at[:, slot], sem.at[slot]).wait()
        else:
            pltpu.make_async_copy(buf.at[slot], buf.at[slot], sem.at[slot]).wait()

    own_r = pltpu.make_async_copy(w_ref.at[:, pl.ds(r * rb, rb)], rbuf.at[c, r], loc.at[0])
    own_r.start()
    own_c = pltpu.make_async_copy(w_ref.at[:, pl.ds(c * cb, cb)], cbuf.at[c, r], loc.at[1])
    own_c.start()
    for d in range(1, nr):
        t = lax.rem(r + d, nr)
        send(w_ref.at[:, pl.ds(t * rb, rb)], rbuf.at[c, r], r1.at[r], (t, c))
    for d in range(1, nc):
        t = lax.rem(c + d, nc)
        send(w_ref.at[:, pl.ds(t * cb, cb)], cbuf.at[c, r], c1.at[c], (r, t))

    step = 1 - 2 * core

    def col_slot(hi, dz):
        return (hi * nz + lax.rem(z + dz + nz, nz)) * 2 + core

    def row_slot(lo, dx):
        return lax.rem(x + dx + nx, nx) * 2 + lo

    sibling_c = c + 1 - 2 * core

    def to_cols(slot, targets):
        for t in targets:
            send(rbuf.at[slot], rbuf.at[slot], r2.at[slot], (r, t))

    def to_rows(slot, targets):
        for t in targets:
            send(cbuf.at[:, slot], cbuf.at[:, slot], c2.at[slot], (t, c))

    partner_c = col_slot(1 - y_hi, 0)
    ring_c = [col_slot(y_hi, 1), col_slot(y_hi, -1)]
    own_r.wait()
    for d in range(1, nr):
        arrived(rbuf.at[c], r1, lax.rem(r + nr - d, nr))
    to_cols(c, [partner_c, sibling_c] + ring_c)

    partner_r = row_slot(1 - y_lo, 0)
    ring_r = [row_slot(y_lo, 1), row_slot(y_lo, -1)]
    own_c.wait()
    for d in range(1, nc):
        src = lax.rem(c + nc - d, nc)
        pltpu.make_async_copy(cbuf.at[src, r], cbuf.at[src, r], c1.at[src]).wait()
    to_rows(r, [partner_r] + ring_r)

    arrived(rbuf, r2, partner_c)
    to_cols(partner_c, ring_c + [sibling_c])
    arrived(cbuf, c2, partner_r)
    to_rows(partner_r, ring_r)

    for hi in (y_hi, 1 - y_hi):
        slot = col_slot(hi, -step)
        arrived(rbuf, r2, slot)
        to_cols(slot, [col_slot(y_hi, step), sibling_c])
    for lo in (y_lo, 1 - y_lo):
        slot = row_slot(lo, -step)
        arrived(cbuf, c2, slot)
        to_rows(slot, [row_slot(y_lo, step)])
    for dz in (1, 2):
        for hi in (y_hi, 1 - y_hi):
            slot = col_slot(hi, step * dz)
            arrived(rbuf, r2, slot)
            to_cols(slot, [sibling_c])

    for hi in range(2):
        for zz in range(nz):
            arrived(rbuf, r2, (hi * nz + zz) * 2 + 1 - core)
    for dx in (1, 2):
        for lo in (y_lo, 1 - y_lo):
            arrived(cbuf, c2, row_slot(lo, step * dx))
    for cp in sends:
        cp.wait_send()


def exchange(w, nr, nc):
    rows, channels = w.shape
    rb = channels // nr
    cb = channels // nc
    dma = pltpu.SemaphoreType.DMA
    return pl.pallas_call(
        functools.partial(exchange_kernel, nr, nc),
        out_shape=(
            jax.ShapeDtypeStruct((nc, nr, rows, rb), w.dtype),
            jax.ShapeDtypeStruct((nc, nr, rows, cb), w.dtype),
        ),
        in_specs=[pl.BlockSpec(memory_space=pl.ANY)],
        out_specs=(pl.BlockSpec(memory_space=pl.ANY), pl.BlockSpec(memory_space=pl.ANY)),
        scratch_shapes=[
            dma((nr,)), dma((nc,)), dma((nc,)), dma((nr,)), dma((2 * (nr + nc),)), dma((2,)),
        ],
        compiler_params=pltpu.CompilerParams(has_side_effects=True),
    )(w)


def on_device(record, fir_taps, bins, offsets):
    local_count = offsets.shape[0]
    assert local_count == 1
    placed = analysis_kernel(fir_taps, bins, offsets[0], record.shape[0])
    spectra = jnp.dot(placed, record, preferred_element_type=jnp.float32)[None]
    whitened = whiten(spectra)
    channels = whitened.shape[-1]
    row_count = lax.axis_size("row")
    col_count = lax.axis_size("col")
    total_windows = local_count * row_count * col_count
    row_block, col_block = exchange(
        whitened.reshape(2 * F, channels), row_count, col_count
    )
    windows = row_count * col_count * local_count
    rb = channels // row_count
    cb = channels // col_count
    left = row_block.reshape(windows, 2 * F, rb)
    right = col_block.reshape(windows, 2 * F, cb)
    return cross(left, right, 1.0 / total_windows)


def cross_kernel(scale, chunks, l_hbm, r_hbm, out_ref, l_in, r_in, lt, rt, sems):
    f = pl.program_id(0)
    bins = pl.num_programs(0)
    cb = r_hbm.shape[-1]
    size = l_hbm.shape[0] // chunks

    @pl.when(f == 0)
    def _():
        copies = []
        for i in range(chunks):
            part = pl.ds(i * size, size)
            for j, (src, dst) in enumerate(((l_hbm, l_in), (r_hbm, r_in))):
                cp = pltpu.make_async_copy(src.at[part], dst.at[part], sems.at[j, i])
                cp.start()
                copies.append(cp)
        for i in range(chunks):
            part = pl.ds(i * size, size)
            copies[2 * i].wait()
            lt[:, part, :] = pltpu.einshape("nkc->knc", l_in[part])
            copies[2 * i + 1].wait()
            rt[:, part, :] = pltpu.einshape("nkc->knc", r_in[part])

    l0, l1 = lt[f], lt[f + bins]
    r0, r1 = rt[f], rt[f + bins]
    lhs = jnp.concatenate([l0, l1], axis=0)
    rhs = jnp.concatenate(
        [jnp.concatenate([r0, r1], axis=1), jnp.concatenate([r1, -r0], axis=1)], axis=0
    )
    both = lax.dot_general(
        lhs, rhs, (((0,), (0,)), ((), ())), preferred_element_type=jnp.float32
    )
    out_ref[0, 0] = (both[:, :cb] * scale).astype(out_ref.dtype)
    out_ref[0, 1] = (both[:, cb:] * scale).astype(out_ref.dtype)


def cross(left, right, scale):
    windows, parts, rb = left.shape
    cb = right.shape[-1]
    bins = parts // 2
    chunks = 8
    return pl.pallas_call(
        functools.partial(cross_kernel, scale, chunks),
        out_shape=jax.ShapeDtypeStruct((bins, 2, rb, cb), jnp.bfloat16),
        grid=(bins,),
        in_specs=[pl.BlockSpec(memory_space=pl.ANY), pl.BlockSpec(memory_space=pl.ANY)],
        out_specs=pl.BlockSpec((1, 2, rb, cb), lambda f: (f, 0, 0, 0)),
        scratch_shapes=[
            pltpu.VMEM((windows, parts, rb), left.dtype),
            pltpu.VMEM((windows, parts, cb), right.dtype),
            pltpu.VMEM((parts, windows, rb), left.dtype),
            pltpu.VMEM((parts, windows, cb), right.dtype),
            pltpu.SemaphoreType.DMA((2, chunks)),
        ],
        cost_estimate=pl.CostEstimate(
            flops=8 * bins * rb * cb * windows,
            bytes_accessed=2 * (left.size + right.size + bins * 2 * rb * cb),
            transcendentals=0,
        ),
    )(left, right)


def solution(mesh):
    placed = (P(("row", "col"), None), P(), P(), P(("row", "col")))
    return jax.shard_map(
        on_device,
        mesh=mesh,
        in_specs=placed,
        out_specs=P(None, None, "row", "col"),
        check_vma=False,
    )
```

```python
import functools
import math

import jax
import jax.numpy as jnp
from jax import lax
from jax.sharding import PartitionSpec as P
from jax.experimental import pallas as pl
from jax.experimental.pallas import tpu as pltpu

F = 16
WL = 1280
TAPS = 101


floor_level = 0.5


def analysis_kernel(fir_taps, bins):
    span = WL + TAPS - 1
    sample_times = jnp.arange(WL, dtype=jnp.int32)
    phase_index = bins[:, None] * sample_times[None, :] % WL
    angles = 2.0 * math.pi / WL * phase_index.astype(jnp.float32)
    centre = (jnp.arange(WL, dtype=jnp.float32) + 0.5) / WL
    window_taper = (0.5 - 0.5 * jnp.cos(2.0 * math.pi * centre)) / math.sqrt(WL)
    pattern = jnp.stack([jnp.cos(angles) * window_taper, -jnp.sin(angles) * window_taper]).reshape(
        2 * F, WL
    )
    lanes = 128
    blocks = pl_cdiv(span, lanes)
    width = 2 * lanes
    padded = jnp.pad(pattern, ((0, 0), (TAPS - 1, blocks * lanes + lanes - WL - (TAPS - 1))))
    windows = jnp.concatenate(
        [
            padded[:, : blocks * lanes].reshape(2 * F, blocks, lanes),
            padded[:, lanes : (blocks + 1) * lanes].reshape(2 * F, blocks, lanes),
        ],
        axis=2,
    )
    vector = jnp.concatenate([fir_taps, jnp.zeros((width + 1 - TAPS,), jnp.float32)])
    band = jnp.tile(vector, lanes)[: lanes * width].reshape(lanes, width)
    kernel = jnp.einsum(
        "bqs,rs->bqr",
        windows,
        band,
        precision=lax.Precision.HIGHEST,
        preferred_element_type=jnp.float32,
    ).reshape(2 * F, blocks * lanes)[:, :span]
    return kernel.astype(jnp.bfloat16)


def pl_cdiv(a, b):
    return (a + b - 1) // b


def whiten(spectra):
    shaped = spectra.reshape(spectra.shape[0], 2, F, spectra.shape[-1])
    magnitude = jnp.sqrt(shaped[:, 0] * shaped[:, 0] + shaped[:, 1] * shaped[:, 1])
    inverse = 1.0 / jnp.maximum(magnitude, floor_level)
    return (shaped * inverse[:, None]).astype(jnp.bfloat16)


MESH = pl.DeviceIdType.MESH


def exchange_kernel(nr, nc, w_ref, rbuf, cbuf, r1, c1, r2, c2, sent, loc):
    r = lax.axis_index("row")
    c = lax.axis_index("col")
    rb = rbuf.shape[-1]
    cb = cbuf.shape[-1]
    nx = nr // 2
    nz = nc // 4
    x, y_lo = r // 2, r % 2
    y_hi, z, core = c // (2 * nz), (c // 2) % nz, c % 2
    sends = []

    def send(src, dst, recv_sem, device):
        cp = pltpu.make_async_remote_copy(
            src_ref=src, dst_ref=dst, send_sem=sent.at[len(sends)], recv_sem=recv_sem,
            device_id=device, device_id_type=MESH,
        )
        cp.start()
        sends.append(cp)

    def arrived(buf, sem, slot):
        if buf is cbuf:
            pltpu.make_async_copy(buf.at[:, slot], buf.at[:, slot], sem.at[slot]).wait()
        else:
            pltpu.make_async_copy(buf.at[slot], buf.at[slot], sem.at[slot]).wait()

    own_r = pltpu.make_async_copy(w_ref.at[:, pl.ds(r * rb, rb)], rbuf.at[c, r], loc.at[0])
    own_r.start()
    own_c = pltpu.make_async_copy(w_ref.at[:, pl.ds(c * cb, cb)], cbuf.at[c, r], loc.at[1])
    own_c.start()
    for d in range(1, nr):
        t = lax.rem(r + d, nr)
        send(w_ref.at[:, pl.ds(t * rb, rb)], rbuf.at[c, r], r1.at[r], (t, c))
    for d in range(1, nc):
        t = lax.rem(c + d, nc)
        send(w_ref.at[:, pl.ds(t * cb, cb)], cbuf.at[c, r], c1.at[c], (r, t))

    step = 1 - 2 * core

    def col_slot(hi, dz):
        return (hi * nz + lax.rem(z + dz + nz, nz)) * 2 + core

    def row_slot(lo, dx):
        return lax.rem(x + dx + nx, nx) * 2 + lo

    sibling_c = c + 1 - 2 * core

    def to_cols(slot, targets):
        for t in targets:
            send(rbuf.at[slot], rbuf.at[slot], r2.at[slot], (r, t))

    def to_rows(slot, targets):
        for t in targets:
            send(cbuf.at[:, slot], cbuf.at[:, slot], c2.at[slot], (t, c))

    partner_c = col_slot(1 - y_hi, 0)
    ring_c = [col_slot(y_hi, 1), col_slot(y_hi, -1)]
    own_r.wait()
    for d in range(1, nr):
        arrived(rbuf.at[c], r1, lax.rem(r + nr - d, nr))
    to_cols(c, [partner_c, sibling_c] + ring_c)

    partner_r = row_slot(1 - y_lo, 0)
    ring_r = [row_slot(y_lo, 1), row_slot(y_lo, -1)]
    own_c.wait()
    for d in range(1, nc):
        src = lax.rem(c + nc - d, nc)
        pltpu.make_async_copy(cbuf.at[src, r], cbuf.at[src, r], c1.at[src]).wait()
    to_rows(r, [partner_r] + ring_r)

    arrived(rbuf, r2, partner_c)
    to_cols(partner_c, ring_c + [sibling_c])
    arrived(cbuf, c2, partner_r)
    to_rows(partner_r, ring_r)

    for hi in (y_hi, 1 - y_hi):
        slot = col_slot(hi, -step)
        arrived(rbuf, r2, slot)
        to_cols(slot, [col_slot(y_hi, step), sibling_c])
    for lo in (y_lo, 1 - y_lo):
        slot = row_slot(lo, -step)
        arrived(cbuf, c2, slot)
        to_rows(slot, [row_slot(y_lo, step)])
    for dz in (1, 2):
        for hi in (y_hi, 1 - y_hi):
            slot = col_slot(hi, step * dz)
            arrived(rbuf, r2, slot)
            to_cols(slot, [sibling_c])

    for hi in range(2):
        for zz in range(nz):
            arrived(rbuf, r2, (hi * nz + zz) * 2 + 1 - core)
    for dx in (1, 2):
        for lo in (y_lo, 1 - y_lo):
            arrived(cbuf, c2, row_slot(lo, step * dx))
    for cp in sends:
        cp.wait_send()


def exchange(w, nr, nc):
    rows, channels = w.shape
    rb = channels // nr
    cb = channels // nc
    dma = pltpu.SemaphoreType.DMA
    return pl.pallas_call(
        functools.partial(exchange_kernel, nr, nc),
        out_shape=(
            jax.ShapeDtypeStruct((nc, nr, rows, rb), w.dtype),
            jax.ShapeDtypeStruct((nc, nr, rows, cb), w.dtype),
        ),
        in_specs=[pl.BlockSpec(memory_space=pl.ANY)],
        out_specs=(pl.BlockSpec(memory_space=pl.ANY), pl.BlockSpec(memory_space=pl.ANY)),
        scratch_shapes=[
            dma((nr,)), dma((nc,)), dma((nc,)), dma((nr,)), dma((2 * (nr + nc),)), dma((2,)),
        ],
        compiler_params=pltpu.CompilerParams(has_side_effects=True),
    )(w)


def on_device(record, fir_taps, bins, offsets):
    kernel = analysis_kernel(fir_taps, bins)
    span = WL + TAPS - 1
    local_count = offsets.shape[0]

    assert local_count == 1
    placed = lax.dynamic_update_slice(
        jnp.zeros((kernel.shape[0], record.shape[0]), kernel.dtype), kernel, (0, offsets[0])
    )
    spectra = jnp.dot(placed, record, preferred_element_type=jnp.float32)[None]
    whitened = whiten(spectra)
    channels = whitened.shape[-1]
    row_count = lax.axis_size("row")
    col_count = lax.axis_size("col")
    total_windows = local_count * row_count * col_count
    row_block, col_block = exchange(
        whitened.reshape(2 * F, channels), row_count, col_count
    )
    windows = row_count * col_count * local_count
    rb = channels // row_count
    cb = channels // col_count
    left = row_block.reshape(windows, 2 * F, rb)
    right = col_block.reshape(windows, 2 * F, cb)
    return cross(left, right, 1.0 / total_windows)


def cross_kernel(scale, chunks, l_hbm, r_hbm, out_ref, l_in, r_in, lt, rt, sems):
    f = pl.program_id(0)
    bins = pl.num_programs(0)
    cb = r_hbm.shape[-1]
    size = l_hbm.shape[0] // chunks

    @pl.when(f == 0)
    def _():
        copies = []
        for i in range(chunks):
            part = pl.ds(i * size, size)
            for j, (src, dst) in enumerate(((l_hbm, l_in), (r_hbm, r_in))):
                cp = pltpu.make_async_copy(src.at[part], dst.at[part], sems.at[j, i])
                cp.start()
                copies.append(cp)
        for i in range(chunks):
            part = pl.ds(i * size, size)
            copies[2 * i].wait()
            lt[:, part, :] = pltpu.einshape("nkc->knc", l_in[part])
            copies[2 * i + 1].wait()
            rt[:, part, :] = pltpu.einshape("nkc->knc", r_in[part]) * jnp.asarray(scale, rt.dtype)

    l0, l1 = lt[f], lt[f + bins]
    r0, r1 = rt[f], rt[f + bins]
    lhs = jnp.concatenate([l0, l1], axis=0)
    rhs = jnp.concatenate(
        [jnp.concatenate([r0, r1], axis=1), jnp.concatenate([r1, -r0], axis=1)], axis=0
    )
    both = lax.dot_general(
        lhs, rhs, (((0,), (0,)), ((), ())), preferred_element_type=jnp.float32
    )
    out_ref[0, 0] = both[:, :cb].astype(out_ref.dtype)
    out_ref[0, 1] = both[:, cb:].astype(out_ref.dtype)


def cross(left, right, scale):
    windows, parts, rb = left.shape
    cb = right.shape[-1]
    bins = parts // 2
    chunks = 8
    return pl.pallas_call(
        functools.partial(cross_kernel, scale, chunks),
        out_shape=jax.ShapeDtypeStruct((bins, 2, rb, cb), jnp.bfloat16),
        grid=(bins,),
        in_specs=[pl.BlockSpec(memory_space=pl.ANY), pl.BlockSpec(memory_space=pl.ANY)],
        out_specs=pl.BlockSpec((1, 2, rb, cb), lambda f: (f, 0, 0, 0)),
        scratch_shapes=[
            pltpu.VMEM((windows, parts, rb), left.dtype),
            pltpu.VMEM((windows, parts, cb), right.dtype),
            pltpu.VMEM((parts, windows, rb), left.dtype),
            pltpu.VMEM((parts, windows, cb), right.dtype),
            pltpu.SemaphoreType.DMA((2, chunks)),
        ],
        cost_estimate=pl.CostEstimate(
            flops=8 * bins * rb * cb * windows,
            bytes_accessed=2 * (left.size + right.size + bins * 2 * rb * cb),
            transcendentals=0,
        ),
    )(left, right)


def solution(mesh):
    placed = (P(("row", "col"), None), P(), P(), P(("row", "col")))
    return jax.shard_map(
        on_device,
        mesh=mesh,
        in_specs=placed,
        out_specs=P(None, None, "row", "col"),
        check_vma=False,
    )
```

```python
import functools
import math

import jax
import jax.numpy as jnp
from jax import lax
from jax.sharding import PartitionSpec as P
from jax.experimental import pallas as pl
from jax.experimental.pallas import tpu as pltpu

F = 16
WL = 1280
TAPS = 101


floor_level = 0.5


def analysis_kernel(fir_taps, bins):
    span = WL + TAPS - 1
    sample_times = jnp.arange(WL, dtype=jnp.int32)
    phase_index = bins[:, None] * sample_times[None, :] % WL
    angles = 2.0 * math.pi / WL * phase_index.astype(jnp.float32)
    centre = (jnp.arange(WL, dtype=jnp.float32) + 0.5) / WL
    window_taper = (0.5 - 0.5 * jnp.cos(2.0 * math.pi * centre)) / math.sqrt(WL)
    pattern = jnp.stack([jnp.cos(angles) * window_taper, -jnp.sin(angles) * window_taper]).reshape(
        2 * F, WL
    )
    lanes = 128
    blocks = pl_cdiv(span, lanes)
    width = 2 * lanes
    padded = jnp.pad(pattern, ((0, 0), (TAPS - 1, blocks * lanes + lanes - WL - (TAPS - 1))))
    windows = jnp.concatenate(
        [
            padded[:, : blocks * lanes].reshape(2 * F, blocks, lanes),
            padded[:, lanes : (blocks + 1) * lanes].reshape(2 * F, blocks, lanes),
        ],
        axis=2,
    )
    vector = jnp.concatenate([fir_taps, jnp.zeros((width + 1 - TAPS,), jnp.float32)])
    band = jnp.tile(vector, lanes)[: lanes * width].reshape(lanes, width)
    kernel = jnp.einsum(
        "bqs,rs->bqr",
        windows,
        band,
        precision=lax.Precision.HIGHEST,
        preferred_element_type=jnp.float32,
    ).reshape(2 * F, blocks * lanes)[:, :span]
    return kernel.astype(jnp.bfloat16)


def pl_cdiv(a, b):
    return (a + b - 1) // b


def whiten(spectra):
    shaped = spectra.reshape(spectra.shape[0], 2, F, spectra.shape[-1])
    magnitude = jnp.sqrt(shaped[:, 0] * shaped[:, 0] + shaped[:, 1] * shaped[:, 1])
    inverse = 1.0 / jnp.maximum(magnitude, floor_level)
    return (shaped * inverse[:, None]).astype(jnp.bfloat16)


MESH = pl.DeviceIdType.MESH


def exchange_kernel(nr, nc, w_ref, rbuf, cbuf, r1, c1, r2, c2, sent, loc):
    r = lax.axis_index("row")
    c = lax.axis_index("col")
    rb = rbuf.shape[-1]
    cb = cbuf.shape[-1]
    nx = nr // 2
    nz = nc // 4
    x, y_lo = r // 2, r % 2
    y_hi, z, core = c // (2 * nz), (c // 2) % nz, c % 2
    sends = []

    def send(src, dst, recv_sem, device):
        cp = pltpu.make_async_remote_copy(
            src_ref=src, dst_ref=dst, send_sem=sent.at[len(sends)], recv_sem=recv_sem,
            device_id=device, device_id_type=MESH,
        )
        cp.start()
        sends.append(cp)

    def arrived(buf, sem, slot):
        if buf is cbuf:
            pltpu.make_async_copy(buf.at[:, slot], buf.at[:, slot], sem.at[slot]).wait()
        else:
            pltpu.make_async_copy(buf.at[slot], buf.at[slot], sem.at[slot]).wait()

    own_r = pltpu.make_async_copy(w_ref.at[:, pl.ds(r * rb, rb)], rbuf.at[c, r], loc.at[0])
    own_r.start()
    own_c = pltpu.make_async_copy(w_ref.at[:, pl.ds(c * cb, cb)], cbuf.at[c, r], loc.at[1])
    own_c.start()
    for d in range(1, nr):
        t = lax.rem(r + d, nr)
        send(w_ref.at[:, pl.ds(t * rb, rb)], rbuf.at[c, r], r1.at[r], (t, c))
    for d in range(1, nc):
        t = lax.rem(c + d, nc)
        send(w_ref.at[:, pl.ds(t * cb, cb)], cbuf.at[c, r], c1.at[c], (r, t))

    step = 1 - 2 * core

    def col_slot(hi, dz):
        return (hi * nz + lax.rem(z + dz + nz, nz)) * 2 + core

    def row_slot(lo, dx):
        return lax.rem(x + dx + nx, nx) * 2 + lo

    sibling_c = c + 1 - 2 * core

    def to_cols(slot, targets):
        for t in targets:
            send(rbuf.at[slot], rbuf.at[slot], r2.at[slot], (r, t))

    def to_rows(slot, targets):
        for t in targets:
            send(cbuf.at[:, slot], cbuf.at[:, slot], c2.at[slot], (t, c))

    partner_c = col_slot(1 - y_hi, 0)
    ring_c = [col_slot(y_hi, 1), col_slot(y_hi, -1)]
    own_r.wait()
    for d in range(1, nr):
        arrived(rbuf.at[c], r1, lax.rem(r + nr - d, nr))
    to_cols(c, [partner_c, sibling_c] + ring_c)

    partner_r = row_slot(1 - y_lo, 0)
    ring_r = [row_slot(y_lo, 1), row_slot(y_lo, -1)]
    own_c.wait()
    for d in range(1, nc):
        src = lax.rem(c + nc - d, nc)
        pltpu.make_async_copy(cbuf.at[src, r], cbuf.at[src, r], c1.at[src]).wait()
    to_rows(r, [partner_r] + ring_r)

    arrived(rbuf, r2, partner_c)
    to_cols(partner_c, ring_c + [sibling_c])
    arrived(cbuf, c2, partner_r)
    to_rows(partner_r, ring_r)

    for hi in (y_hi, 1 - y_hi):
        slot = col_slot(hi, -step)
        arrived(rbuf, r2, slot)
        to_cols(slot, [col_slot(y_hi, step), sibling_c])
    for lo in (y_lo, 1 - y_lo):
        slot = row_slot(lo, -step)
        arrived(cbuf, c2, slot)
        to_rows(slot, [row_slot(y_lo, step)])
    for dz in (1, 2):
        for hi in (y_hi, 1 - y_hi):
            slot = col_slot(hi, step * dz)
            arrived(rbuf, r2, slot)
            to_cols(slot, [sibling_c])

    for hi in range(2):
        for zz in range(nz):
            arrived(rbuf, r2, (hi * nz + zz) * 2 + 1 - core)
    for dx in (1, 2):
        for lo in (y_lo, 1 - y_lo):
            arrived(cbuf, c2, row_slot(lo, step * dx))
    for cp in sends:
        cp.wait_send()


def exchange(w, nr, nc):
    rows, channels = w.shape
    rb = channels // nr
    cb = channels // nc
    dma = pltpu.SemaphoreType.DMA
    return pl.pallas_call(
        functools.partial(exchange_kernel, nr, nc),
        out_shape=(
            jax.ShapeDtypeStruct((nc, nr, rows, rb), w.dtype),
            jax.ShapeDtypeStruct((nc, nr, rows, cb), w.dtype),
        ),
        in_specs=[pl.BlockSpec(memory_space=pl.ANY)],
        out_specs=(pl.BlockSpec(memory_space=pl.ANY), pl.BlockSpec(memory_space=pl.ANY)),
        scratch_shapes=[
            dma((nr,)), dma((nc,)), dma((nc,)), dma((nr,)), dma((2 * (nr + nc),)), dma((2,)),
        ],
        compiler_params=pltpu.CompilerParams(has_side_effects=True),
    )(w)


def on_device(record, fir_taps, bins, offsets):
    kernel = analysis_kernel(fir_taps, bins)
    span = WL + TAPS - 1
    local_count = offsets.shape[0]

    assert local_count == 1
    placed = lax.dynamic_update_slice(
        jnp.zeros((kernel.shape[0], record.shape[0]), kernel.dtype), kernel, (0, offsets[0])
    )
    spectra = jnp.dot(placed, record, preferred_element_type=jnp.float32)[None]
    whitened = whiten(spectra)
    channels = whitened.shape[-1]
    row_count = lax.axis_size("row")
    col_count = lax.axis_size("col")
    total_windows = local_count * row_count * col_count
    row_block, col_block = exchange(
        whitened.reshape(2 * F, channels), row_count, col_count
    )
    windows = row_count * col_count * local_count
    rb = channels // row_count
    cb = channels // col_count
    left = row_block.reshape(windows, 2 * F, rb)
    right = col_block.reshape(windows, 2 * F, cb)
    return cross(left, right, 1.0 / total_windows)


def cross_kernel(scale, chunks, l_hbm, r_hbm, out_ref, l_in, r_in, lt, rt, sems):
    f = pl.program_id(0)
    bins = pl.num_programs(0)
    cb = r_hbm.shape[-1]
    size = l_hbm.shape[0] // chunks

    @pl.when(f == 0)
    def _():
        copies = []
        for i in range(chunks):
            part = pl.ds(i * size, size)
            for j, (src, dst) in enumerate(((l_hbm, l_in), (r_hbm, r_in))):
                cp = pltpu.make_async_copy(src.at[part], dst.at[part], sems.at[j, i])
                cp.start()
                copies.append(cp)
        for i in range(chunks):
            part = pl.ds(i * size, size)
            copies[2 * i].wait()
            lt[:, :, part] = pltpu.einshape("nkc->kcn", l_in[part])
            copies[2 * i + 1].wait()
            rt[:, part, :] = pltpu.einshape("nkc->knc", r_in[part]) * jnp.asarray(scale, rt.dtype)

    l0, l1 = lt[f], lt[f + bins]
    r0, r1 = rt[f], rt[f + bins]
    lhs = jnp.concatenate([l0, l1], axis=1)
    rhs = jnp.concatenate(
        [jnp.concatenate([r0, r1], axis=1), jnp.concatenate([r1, -r0], axis=1)], axis=0
    )
    both = jnp.dot(lhs, rhs, preferred_element_type=jnp.float32)
    out_ref[0, 0] = both[:, :cb].astype(out_ref.dtype)
    out_ref[0, 1] = both[:, cb:].astype(out_ref.dtype)


def cross(left, right, scale):
    windows, parts, rb = left.shape
    cb = right.shape[-1]
    bins = parts // 2
    chunks = 8
    return pl.pallas_call(
        functools.partial(cross_kernel, scale, chunks),
        out_shape=jax.ShapeDtypeStruct((bins, 2, rb, cb), jnp.bfloat16),
        grid=(bins,),
        in_specs=[pl.BlockSpec(memory_space=pl.ANY), pl.BlockSpec(memory_space=pl.ANY)],
        out_specs=pl.BlockSpec((1, 2, rb, cb), lambda f: (f, 0, 0, 0)),
        scratch_shapes=[
            pltpu.VMEM((windows, parts, rb), left.dtype),
            pltpu.VMEM((windows, parts, cb), right.dtype),
            pltpu.VMEM((parts, rb, windows), left.dtype),
            pltpu.VMEM((parts, windows, cb), right.dtype),
            pltpu.SemaphoreType.DMA((2, chunks)),
        ],
        cost_estimate=pl.CostEstimate(
            flops=8 * bins * rb * cb * windows,
            bytes_accessed=2 * (left.size + right.size + bins * 2 * rb * cb),
            transcendentals=0,
        ),
    )(left, right)


def solution(mesh):
    placed = (P(("row", "col"), None), P(), P(), P(("row", "col")))
    return jax.shard_map(
        on_device,
        mesh=mesh,
        in_specs=placed,
        out_specs=P(None, None, "row", "col"),
        check_vma=False,
    )
```

```python
import functools
import math

import jax
import jax.numpy as jnp
from jax import lax
from jax.sharding import PartitionSpec as P
from jax.experimental import pallas as pl
from jax.experimental.pallas import tpu as pltpu

F = 16
WL = 1280
TAPS = 101


floor_level = 0.5


def analysis_kernel(fir_taps, bins):
    span = WL + TAPS - 1
    sample_times = jnp.arange(WL, dtype=jnp.int32)
    phase_index = bins[:, None] * sample_times[None, :] % WL
    angles = 2.0 * math.pi / WL * phase_index.astype(jnp.float32)
    centre = (jnp.arange(WL, dtype=jnp.float32) + 0.5) / WL
    window_taper = (0.5 - 0.5 * jnp.cos(2.0 * math.pi * centre)) / math.sqrt(WL)
    pattern = jnp.stack([jnp.cos(angles) * window_taper, -jnp.sin(angles) * window_taper]).reshape(
        2 * F, WL
    )
    lanes = 128
    blocks = pl_cdiv(span, lanes)
    width = 2 * lanes
    padded = jnp.pad(pattern, ((0, 0), (TAPS - 1, blocks * lanes + lanes - WL - (TAPS - 1))))
    windows = jnp.concatenate(
        [
            padded[:, : blocks * lanes].reshape(2 * F, blocks, lanes),
            padded[:, lanes : (blocks + 1) * lanes].reshape(2 * F, blocks, lanes),
        ],
        axis=2,
    )
    vector = jnp.concatenate([fir_taps, jnp.zeros((width + 1 - TAPS,), jnp.float32)])
    band = jnp.tile(vector, lanes)[: lanes * width].reshape(lanes, width)
    kernel = jnp.einsum(
        "bqs,rs->bqr",
        windows,
        band,
        precision=lax.Precision.HIGHEST,
        preferred_element_type=jnp.float32,
    ).reshape(2 * F, blocks * lanes)[:, :span]
    return kernel.astype(jnp.bfloat16)


def pl_cdiv(a, b):
    return (a + b - 1) // b


def whiten(spectra):
    shaped = spectra.reshape(spectra.shape[0], 2, F, spectra.shape[-1])
    magnitude = jnp.sqrt(shaped[:, 0] * shaped[:, 0] + shaped[:, 1] * shaped[:, 1])
    inverse = 1.0 / jnp.maximum(magnitude, floor_level)
    return (shaped * inverse[:, None]).astype(jnp.bfloat16)


def spectra_kernel(k_ref, rec_ref, out_ref):
    spectra = jnp.dot(k_ref[...], rec_ref[...], preferred_element_type=jnp.float32)
    re, im = spectra[:F], spectra[F:]
    inverse = 1.0 / jnp.maximum(jnp.sqrt(re * re + im * im), floor_level)
    out_ref[...] = (spectra * jnp.concatenate([inverse, inverse], axis=0)).astype(out_ref.dtype)


def spectra_whitened(placed, record):
    rows, length = placed.shape
    channels = record.shape[-1]
    block = 512
    return pl.pallas_call(
        spectra_kernel,
        out_shape=jax.ShapeDtypeStruct((rows, channels), jnp.bfloat16),
        grid=(channels // block,),
        in_specs=[
            pl.BlockSpec((rows, length), lambda j: (0, 0)),
            pl.BlockSpec((length, block), lambda j: (0, j)),
        ],
        out_specs=pl.BlockSpec((rows, block), lambda j: (0, j)),
        cost_estimate=pl.CostEstimate(
            flops=2 * rows * length * channels,
            bytes_accessed=2 * (placed.size + record.size + rows * channels),
            transcendentals=2 * F * channels,
        ),
    )(placed, record)


MESH = pl.DeviceIdType.MESH


def exchange_kernel(nr, nc, w_ref, rbuf, cbuf, r1, c1, r2, c2, sent, loc):
    r = lax.axis_index("row")
    c = lax.axis_index("col")
    rb = rbuf.shape[-1]
    cb = cbuf.shape[-1]
    nx = nr // 2
    nz = nc // 4
    x, y_lo = r // 2, r % 2
    y_hi, z, core = c // (2 * nz), (c // 2) % nz, c % 2
    sends = []

    def send(src, dst, recv_sem, device):
        cp = pltpu.make_async_remote_copy(
            src_ref=src, dst_ref=dst, send_sem=sent.at[len(sends)], recv_sem=recv_sem,
            device_id=device, device_id_type=MESH,
        )
        cp.start()
        sends.append(cp)

    def arrived(buf, sem, slot):
        if buf is cbuf:
            pltpu.make_async_copy(buf.at[:, slot], buf.at[:, slot], sem.at[slot]).wait()
        else:
            pltpu.make_async_copy(buf.at[slot], buf.at[slot], sem.at[slot]).wait()

    own_r = pltpu.make_async_copy(w_ref.at[:, pl.ds(r * rb, rb)], rbuf.at[c, r], loc.at[0])
    own_r.start()
    own_c = pltpu.make_async_copy(w_ref.at[:, pl.ds(c * cb, cb)], cbuf.at[c, r], loc.at[1])
    own_c.start()
    for d in range(1, nr):
        t = lax.rem(r + d, nr)
        send(w_ref.at[:, pl.ds(t * rb, rb)], rbuf.at[c, r], r1.at[r], (t, c))
    for d in range(1, nc):
        t = lax.rem(c + d, nc)
        send(w_ref.at[:, pl.ds(t * cb, cb)], cbuf.at[c, r], c1.at[c], (r, t))

    step = 1 - 2 * core

    def col_slot(hi, dz):
        return (hi * nz + lax.rem(z + dz + nz, nz)) * 2 + core

    def row_slot(lo, dx):
        return lax.rem(x + dx + nx, nx) * 2 + lo

    sibling_c = c + 1 - 2 * core

    def to_cols(slot, targets):
        for t in targets:
            send(rbuf.at[slot], rbuf.at[slot], r2.at[slot], (r, t))

    def to_rows(slot, targets):
        for t in targets:
            send(cbuf.at[:, slot], cbuf.at[:, slot], c2.at[slot], (t, c))

    partner_c = col_slot(1 - y_hi, 0)
    ring_c = [col_slot(y_hi, 1), col_slot(y_hi, -1)]
    own_r.wait()
    for d in range(1, nr):
        arrived(rbuf.at[c], r1, lax.rem(r + nr - d, nr))
    to_cols(c, [partner_c, sibling_c] + ring_c)

    partner_r = row_slot(1 - y_lo, 0)
    ring_r = [row_slot(y_lo, 1), row_slot(y_lo, -1)]
    own_c.wait()
    for d in range(1, nc):
        src = lax.rem(c + nc - d, nc)
        pltpu.make_async_copy(cbuf.at[src, r], cbuf.at[src, r], c1.at[src]).wait()
    to_rows(r, [partner_r] + ring_r)

    arrived(rbuf, r2, partner_c)
    to_cols(partner_c, ring_c + [sibling_c])
    arrived(cbuf, c2, partner_r)
    to_rows(partner_r, ring_r)

    for hi in (y_hi, 1 - y_hi):
        slot = col_slot(hi, -step)
        arrived(rbuf, r2, slot)
        to_cols(slot, [col_slot(y_hi, step), sibling_c])
    for lo in (y_lo, 1 - y_lo):
        slot = row_slot(lo, -step)
        arrived(cbuf, c2, slot)
        to_rows(slot, [row_slot(y_lo, step)])
    for dz in (1, 2):
        for hi in (y_hi, 1 - y_hi):
            slot = col_slot(hi, step * dz)
            arrived(rbuf, r2, slot)
            to_cols(slot, [sibling_c])

    for hi in range(2):
        for zz in range(nz):
            arrived(rbuf, r2, (hi * nz + zz) * 2 + 1 - core)
    for dx in (1, 2):
        for lo in (y_lo, 1 - y_lo):
            arrived(cbuf, c2, row_slot(lo, step * dx))
    for cp in sends:
        cp.wait_send()


def exchange(w, nr, nc):
    rows, channels = w.shape
    rb = channels // nr
    cb = channels // nc
    dma = pltpu.SemaphoreType.DMA
    return pl.pallas_call(
        functools.partial(exchange_kernel, nr, nc),
        out_shape=(
            jax.ShapeDtypeStruct((nc, nr, rows, rb), w.dtype),
            jax.ShapeDtypeStruct((nc, nr, rows, cb), w.dtype),
        ),
        in_specs=[pl.BlockSpec(memory_space=pl.ANY)],
        out_specs=(pl.BlockSpec(memory_space=pl.ANY), pl.BlockSpec(memory_space=pl.ANY)),
        scratch_shapes=[
            dma((nr,)), dma((nc,)), dma((nc,)), dma((nr,)), dma((2 * (nr + nc),)), dma((2,)),
        ],
        compiler_params=pltpu.CompilerParams(has_side_effects=True),
    )(w)


def on_device(record, fir_taps, bins, offsets):
    kernel = analysis_kernel(fir_taps, bins)
    span = WL + TAPS - 1
    local_count = offsets.shape[0]

    assert local_count == 1
    placed = lax.dynamic_update_slice(
        jnp.zeros((kernel.shape[0], record.shape[0]), kernel.dtype), kernel, (0, offsets[0])
    )
    whitened = spectra_whitened(placed, record)[None]
    channels = whitened.shape[-1]
    row_count = lax.axis_size("row")
    col_count = lax.axis_size("col")
    total_windows = local_count * row_count * col_count
    row_block, col_block = exchange(
        whitened.reshape(2 * F, channels), row_count, col_count
    )
    windows = row_count * col_count * local_count
    rb = channels // row_count
    cb = channels // col_count
    left = row_block.reshape(windows, 2 * F, rb)
    right = col_block.reshape(windows, 2 * F, cb)
    return cross(left, right, 1.0 / total_windows)


def cross_kernel(scale, chunks, l_hbm, r_hbm, out_ref, l_in, r_in, lt, rt, sems):
    f = pl.program_id(0)
    bins = pl.num_programs(0)
    cb = r_hbm.shape[-1]
    size = l_hbm.shape[0] // chunks

    @pl.when(f == 0)
    def _():
        copies = []
        for i in range(chunks):
            part = pl.ds(i * size, size)
            for j, (src, dst) in enumerate(((l_hbm, l_in), (r_hbm, r_in))):
                cp = pltpu.make_async_copy(src.at[part], dst.at[part], sems.at[j, i])
                cp.start()
                copies.append(cp)
        for i in range(chunks):
            part = pl.ds(i * size, size)
            copies[2 * i].wait()
            lt[:, part, :] = pltpu.einshape("nkc->knc", l_in[part])
            copies[2 * i + 1].wait()
            rt[:, part, :] = pltpu.einshape("nkc->knc", r_in[part]) * jnp.asarray(scale, rt.dtype)

    l0, l1 = lt[f], lt[f + bins]
    r0, r1 = rt[f], rt[f + bins]
    lhs = jnp.concatenate([l0, l1], axis=0)
    rhs = jnp.concatenate(
        [jnp.concatenate([r0, r1], axis=1), jnp.concatenate([r1, -r0], axis=1)], axis=0
    )
    both = lax.dot_general(
        lhs, rhs, (((0,), (0,)), ((), ())), preferred_element_type=jnp.float32
    )
    out_ref[0, 0] = both[:, :cb].astype(out_ref.dtype)
    out_ref[0, 1] = both[:, cb:].astype(out_ref.dtype)


def cross(left, right, scale):
    windows, parts, rb = left.shape
    cb = right.shape[-1]
    bins = parts // 2
    chunks = 8
    return pl.pallas_call(
        functools.partial(cross_kernel, scale, chunks),
        out_shape=jax.ShapeDtypeStruct((bins, 2, rb, cb), jnp.bfloat16),
        grid=(bins,),
        in_specs=[pl.BlockSpec(memory_space=pl.ANY), pl.BlockSpec(memory_space=pl.ANY)],
        out_specs=pl.BlockSpec((1, 2, rb, cb), lambda f: (f, 0, 0, 0)),
        scratch_shapes=[
            pltpu.VMEM((windows, parts, rb), left.dtype),
            pltpu.VMEM((windows, parts, cb), right.dtype),
            pltpu.VMEM((parts, windows, rb), left.dtype),
            pltpu.VMEM((parts, windows, cb), right.dtype),
            pltpu.SemaphoreType.DMA((2, chunks)),
        ],
        cost_estimate=pl.CostEstimate(
            flops=8 * bins * rb * cb * windows,
            bytes_accessed=2 * (left.size + right.size + bins * 2 * rb * cb),
            transcendentals=0,
        ),
    )(left, right)


def solution(mesh):
    placed = (P(("row", "col"), None), P(), P(), P(("row", "col")))
    return jax.shard_map(
        on_device,
        mesh=mesh,
        in_specs=placed,
        out_specs=P(None, None, "row", "col"),
        check_vma=False,
    )
```

```python
import functools
import math

import jax
import jax.numpy as jnp
from jax import lax
from jax.sharding import PartitionSpec as P
from jax.experimental import pallas as pl
from jax.experimental.pallas import tpu as pltpu

F = 16
WL = 1280
TAPS = 101


floor_level = 0.5


def analysis_kernel(fir_taps, bins):
    span = WL + TAPS - 1
    sample_times = jnp.arange(WL, dtype=jnp.int32)
    phase_index = bins[:, None] * sample_times[None, :] % WL
    angles = 2.0 * math.pi / WL * phase_index.astype(jnp.float32)
    centre = (jnp.arange(WL, dtype=jnp.float32) + 0.5) / WL
    window_taper = (0.5 - 0.5 * jnp.cos(2.0 * math.pi * centre)) / math.sqrt(WL)
    pattern = jnp.stack([jnp.cos(angles) * window_taper, -jnp.sin(angles) * window_taper]).reshape(
        2 * F, WL
    )
    lanes = 128
    blocks = pl_cdiv(span, lanes)
    width = 2 * lanes
    padded = jnp.pad(pattern, ((0, 0), (TAPS - 1, blocks * lanes + lanes - WL - (TAPS - 1))))
    windows = jnp.concatenate(
        [
            padded[:, : blocks * lanes].reshape(2 * F, blocks, lanes),
            padded[:, lanes : (blocks + 1) * lanes].reshape(2 * F, blocks, lanes),
        ],
        axis=2,
    )
    vector = jnp.concatenate([fir_taps, jnp.zeros((width + 1 - TAPS,), jnp.float32)])
    band = jnp.tile(vector, lanes)[: lanes * width].reshape(lanes, width)
    kernel = jnp.einsum(
        "bqs,rs->bqr",
        windows,
        band,
        precision=lax.Precision.HIGHEST,
        preferred_element_type=jnp.float32,
    ).reshape(2 * F, blocks * lanes)[:, :span]
    return kernel.astype(jnp.bfloat16)


def pl_cdiv(a, b):
    return (a + b - 1) // b


def whiten(spectra):
    shaped = spectra.reshape(spectra.shape[0], 2, F, spectra.shape[-1])
    magnitude = jnp.sqrt(shaped[:, 0] * shaped[:, 0] + shaped[:, 1] * shaped[:, 1])
    inverse = 1.0 / jnp.maximum(magnitude, floor_level)
    return (shaped * inverse[:, None]).astype(jnp.bfloat16)


MESH = pl.DeviceIdType.MESH


def exchange_kernel(nr, nc, w_ref, rbuf, cbuf, r1, c1, r2, c2, sent, loc):
    r = lax.axis_index("row")
    c = lax.axis_index("col")
    rb = rbuf.shape[-1]
    cb = cbuf.shape[-1]
    nx = nr // 2
    nz = nc // 4
    x, y_lo = r // 2, r % 2
    y_hi, z, core = c // (2 * nz), (c // 2) % nz, c % 2
    sends = []

    def send(src, dst, recv_sem, device):
        cp = pltpu.make_async_remote_copy(
            src_ref=src, dst_ref=dst, send_sem=sent.at[len(sends)], recv_sem=recv_sem,
            device_id=device, device_id_type=MESH,
        )
        cp.start()
        sends.append(cp)

    def arrived(buf, sem, slot):
        if buf is cbuf:
            pltpu.make_async_copy(buf.at[:, slot], buf.at[:, slot], sem.at[slot]).wait()
        else:
            pltpu.make_async_copy(buf.at[slot], buf.at[slot], sem.at[slot]).wait()

    own_r = pltpu.make_async_copy(w_ref.at[:, pl.ds(r * rb, rb)], rbuf.at[c, r], loc.at[0])
    own_r.start()
    own_c = pltpu.make_async_copy(w_ref.at[:, pl.ds(c * cb, cb)], cbuf.at[c, r], loc.at[1])
    own_c.start()
    for d in range(1, nr):
        t = lax.rem(r + d, nr)
        send(w_ref.at[:, pl.ds(t * rb, rb)], rbuf.at[c, r], r1.at[r], (t, c))
    for d in range(1, nc):
        t = lax.rem(c + d, nc)
        send(w_ref.at[:, pl.ds(t * cb, cb)], cbuf.at[c, r], c1.at[c], (r, t))

    step = 1 - 2 * core

    def col_slot(hi, dz):
        return (hi * nz + lax.rem(z + dz + nz, nz)) * 2 + core

    def row_slot(lo, dx):
        return lax.rem(x + dx + nx, nx) * 2 + lo

    sibling_c = c + 1 - 2 * core

    def to_cols(slot, targets):
        for t in targets:
            send(rbuf.at[slot], rbuf.at[slot], r2.at[slot], (r, t))

    def to_rows(slot, targets):
        for t in targets:
            send(cbuf.at[:, slot], cbuf.at[:, slot], c2.at[slot], (t, c))

    partner_c = col_slot(1 - y_hi, 0)
    ring_c = [col_slot(y_hi, 1), col_slot(y_hi, -1)]
    own_r.wait()
    for d in range(1, nr):
        arrived(rbuf.at[c], r1, lax.rem(r + nr - d, nr))
    to_cols(c, [partner_c, sibling_c] + ring_c)

    partner_r = row_slot(1 - y_lo, 0)
    ring_r = [row_slot(y_lo, 1), row_slot(y_lo, -1)]
    own_c.wait()
    for d in range(1, nc):
        src = lax.rem(c + nc - d, nc)
        pltpu.make_async_copy(cbuf.at[src, r], cbuf.at[src, r], c1.at[src]).wait()
    to_rows(r, [partner_r] + ring_r)

    arrived(rbuf, r2, partner_c)
    to_cols(partner_c, ring_c + [sibling_c])
    arrived(cbuf, c2, partner_r)
    to_rows(partner_r, ring_r)

    for hi in (y_hi, 1 - y_hi):
        slot = col_slot(hi, -step)
        arrived(rbuf, r2, slot)
        to_cols(slot, [col_slot(y_hi, step), sibling_c])
    for lo in (y_lo, 1 - y_lo):
        slot = row_slot(lo, -step)
        arrived(cbuf, c2, slot)
        to_rows(slot, [row_slot(y_lo, step)])
    for dz in (1, 2):
        for hi in (y_hi, 1 - y_hi):
            slot = col_slot(hi, step * dz)
            arrived(rbuf, r2, slot)
            to_cols(slot, [sibling_c])

    for hi in range(2):
        for zz in range(nz):
            arrived(rbuf, r2, (hi * nz + zz) * 2 + 1 - core)
    for dx in (1, 2):
        for lo in (y_lo, 1 - y_lo):
            arrived(cbuf, c2, row_slot(lo, step * dx))
    for cp in sends:
        cp.wait_send()


def exchange(w, nr, nc):
    rows, channels = w.shape
    rb = channels // nr
    cb = channels // nc
    dma = pltpu.SemaphoreType.DMA
    return pl.pallas_call(
        functools.partial(exchange_kernel, nr, nc),
        out_shape=(
            jax.ShapeDtypeStruct((nc, nr, rows, rb), w.dtype),
            jax.ShapeDtypeStruct((nc, nr, rows, cb), w.dtype),
        ),
        in_specs=[pl.BlockSpec(memory_space=pl.ANY)],
        out_specs=(pl.BlockSpec(memory_space=pl.ANY), pl.BlockSpec(memory_space=pl.ANY)),
        scratch_shapes=[
            dma((nr,)), dma((nc,)), dma((nc,)), dma((nr,)), dma((2 * (nr + nc),)), dma((2,)),
        ],
        compiler_params=pltpu.CompilerParams(has_side_effects=True),
    )(w)


def on_device(record, fir_taps, bins, offsets):
    kernel = analysis_kernel(fir_taps, bins)
    span = WL + TAPS - 1
    local_count = offsets.shape[0]

    assert local_count == 1
    placed = lax.dynamic_update_slice(
        jnp.zeros((kernel.shape[0], record.shape[0]), kernel.dtype), kernel, (0, offsets[0])
    )
    spectra = jnp.dot(placed, record, preferred_element_type=jnp.float32)[None]
    whitened = whiten(spectra)
    channels = whitened.shape[-1]
    row_count = lax.axis_size("row")
    col_count = lax.axis_size("col")
    total_windows = local_count * row_count * col_count
    row_block, col_block = exchange(
        whitened.reshape(2 * F, channels), row_count, col_count
    )
    windows = row_count * col_count * local_count
    rb = channels // row_count
    cb = channels // col_count
    left = row_block.reshape(windows, 2 * F, rb)
    right = col_block.reshape(windows, 2 * F, cb)
    return cross(left, right, 1.0 / total_windows)


def cross_kernel(scale, chunks, l_hbm, r_hbm, out_ref, l_in, r_in, lt, rt, sems):
    f = pl.program_id(0)
    bins = pl.num_programs(0)
    cb = r_hbm.shape[-1]
    size = l_hbm.shape[0] // chunks

    @pl.when(f == 0)
    def _():
        copies = []
        for i in range(chunks):
            part = pl.ds(i * size, size)
            for j, (src, dst) in enumerate(((l_hbm, l_in), (r_hbm, r_in))):
                cp = pltpu.make_async_copy(src.at[part], dst.at[part], sems.at[j, i])
                cp.start()
                copies.append(cp)
        for i in range(chunks):
            part = pl.ds(i * size, size)
            copies[2 * i].wait()
            lt[:, part, :] = pltpu.einshape("nkc->knc", l_in[part])
            copies[2 * i + 1].wait()
            rt[:, part, :] = pltpu.einshape("nkc->knc", r_in[part]) * jnp.asarray(scale, rt.dtype)

    l0, l1 = lt[f], lt[f + bins]
    r0, r1 = rt[f], rt[f + bins]
    lhs = jnp.concatenate([l0, l1], axis=0)
    rhs = jnp.concatenate(
        [jnp.concatenate([r0, r1], axis=1), jnp.concatenate([r1, -r0], axis=1)], axis=0
    )
    both = lax.dot_general(
        lhs, rhs, (((0,), (0,)), ((), ())), preferred_element_type=jnp.float32
    )
    out_ref[0, 0] = both[:, :cb].astype(out_ref.dtype)
    out_ref[0, 1] = both[:, cb:].astype(out_ref.dtype)


def cross(left, right, scale):
    windows, parts, rb = left.shape
    cb = right.shape[-1]
    bins = parts // 2
    chunks = 16
    return pl.pallas_call(
        functools.partial(cross_kernel, scale, chunks),
        out_shape=jax.ShapeDtypeStruct((bins, 2, rb, cb), jnp.bfloat16),
        grid=(bins,),
        in_specs=[pl.BlockSpec(memory_space=pl.ANY), pl.BlockSpec(memory_space=pl.ANY)],
        out_specs=pl.BlockSpec((1, 2, rb, cb), lambda f: (f, 0, 0, 0)),
        scratch_shapes=[
            pltpu.VMEM((windows, parts, rb), left.dtype),
            pltpu.VMEM((windows, parts, cb), right.dtype),
            pltpu.VMEM((parts, windows, rb), left.dtype),
            pltpu.VMEM((parts, windows, cb), right.dtype),
            pltpu.SemaphoreType.DMA((2, chunks)),
        ],
        cost_estimate=pl.CostEstimate(
            flops=8 * bins * rb * cb * windows,
            bytes_accessed=2 * (left.size + right.size + bins * 2 * rb * cb),
            transcendentals=0,
        ),
    )(left, right)


def solution(mesh):
    placed = (P(("row", "col"), None), P(), P(), P(("row", "col")))
    return jax.shard_map(
        on_device,
        mesh=mesh,
        in_specs=placed,
        out_specs=P(None, None, "row", "col"),
        check_vma=False,
    )
```

```python
import functools
import math

import jax
import jax.numpy as jnp
from jax import lax
from jax.sharding import PartitionSpec as P
from jax.experimental import pallas as pl
from jax.experimental.pallas import tpu as pltpu

F = 16
WL = 1280
TAPS = 101


floor_level = 0.5


def analysis_kernel(fir_taps, bins):
    span = WL + TAPS - 1
    sample_times = jnp.arange(WL, dtype=jnp.int32)
    phase_index = bins[:, None] * sample_times[None, :] % WL
    angles = 2.0 * math.pi / WL * phase_index.astype(jnp.float32)
    centre = (jnp.arange(WL, dtype=jnp.float32) + 0.5) / WL
    window_taper = (0.5 - 0.5 * jnp.cos(2.0 * math.pi * centre)) / math.sqrt(WL)
    pattern = jnp.stack([jnp.cos(angles) * window_taper, -jnp.sin(angles) * window_taper]).reshape(
        2 * F, WL
    )
    lanes = 128
    blocks = pl_cdiv(span, lanes)
    width = 2 * lanes
    padded = jnp.pad(pattern, ((0, 0), (TAPS - 1, blocks * lanes + lanes - WL - (TAPS - 1))))
    windows = jnp.concatenate(
        [
            padded[:, : blocks * lanes].reshape(2 * F, blocks, lanes),
            padded[:, lanes : (blocks + 1) * lanes].reshape(2 * F, blocks, lanes),
        ],
        axis=2,
    )
    vector = jnp.concatenate([fir_taps, jnp.zeros((width + 1 - TAPS,), jnp.float32)])
    band = jnp.tile(vector, lanes)[: lanes * width].reshape(lanes, width)
    kernel = jnp.einsum(
        "bqs,rs->bqr",
        windows,
        band,
        precision=lax.Precision.HIGHEST,
        preferred_element_type=jnp.float32,
    ).reshape(2 * F, blocks * lanes)[:, :span]
    return kernel.astype(jnp.bfloat16)


def pl_cdiv(a, b):
    return (a + b - 1) // b


def whiten(spectra):
    shaped = spectra.reshape(spectra.shape[0], 2, F, spectra.shape[-1])
    magnitude = jnp.sqrt(shaped[:, 0] * shaped[:, 0] + shaped[:, 1] * shaped[:, 1])
    inverse = 1.0 / jnp.maximum(magnitude, floor_level)
    return (shaped * inverse[:, None]).astype(jnp.bfloat16)


MESH = pl.DeviceIdType.MESH


def exchange_kernel(nr, nc, w_ref, rbuf, cbuf, r1, c1, r2, c2, sent, loc):
    r = lax.axis_index("row")
    c = lax.axis_index("col")
    rb = rbuf.shape[-1]
    cb = cbuf.shape[-1]
    nx = nr // 2
    nz = nc // 4
    x, y_lo = r // 2, r % 2
    y_hi, z, core = c // (2 * nz), (c // 2) % nz, c % 2
    sends = []

    def send(src, dst, recv_sem, device):
        cp = pltpu.make_async_remote_copy(
            src_ref=src, dst_ref=dst, send_sem=sent.at[len(sends)], recv_sem=recv_sem,
            device_id=device, device_id_type=MESH,
        )
        cp.start()
        sends.append(cp)

    def arrived(buf, sem, slot):
        if buf is cbuf:
            pltpu.make_async_copy(buf.at[:, slot], buf.at[:, slot], sem.at[slot]).wait()
        else:
            pltpu.make_async_copy(buf.at[slot], buf.at[slot], sem.at[slot]).wait()

    own_r = pltpu.make_async_copy(w_ref.at[:, pl.ds(r * rb, rb)], rbuf.at[c, r], loc.at[0])
    own_r.start()
    own_c = pltpu.make_async_copy(w_ref.at[:, pl.ds(c * cb, cb)], cbuf.at[c, r], loc.at[1])
    own_c.start()
    for d in range(1, nr):
        t = lax.rem(r + d, nr)
        send(w_ref.at[:, pl.ds(t * rb, rb)], rbuf.at[c, r], r1.at[r], (t, c))
    for d in range(1, nc):
        t = lax.rem(c + d, nc)
        send(w_ref.at[:, pl.ds(t * cb, cb)], cbuf.at[c, r], c1.at[c], (r, t))

    step = 1 - 2 * core

    def col_slot(hi, dz):
        return (hi * nz + lax.rem(z + dz + nz, nz)) * 2 + core

    def row_slot(lo, dx):
        return lax.rem(x + dx + nx, nx) * 2 + lo

    sibling_c = c + 1 - 2 * core

    def to_cols(slot, targets):
        for t in targets:
            send(rbuf.at[slot], rbuf.at[slot], r2.at[slot], (r, t))

    def to_rows(slot, targets):
        for t in targets:
            send(cbuf.at[:, slot], cbuf.at[:, slot], c2.at[slot], (t, c))

    partner_c = col_slot(1 - y_hi, 0)
    ring_c = [col_slot(y_hi, 1), col_slot(y_hi, -1)]
    own_r.wait()
    for d in range(1, nr):
        arrived(rbuf.at[c], r1, lax.rem(r + nr - d, nr))
    to_cols(c, [partner_c, sibling_c] + ring_c)

    partner_r = row_slot(1 - y_lo, 0)
    ring_r = [row_slot(y_lo, 1), row_slot(y_lo, -1)]
    own_c.wait()
    for d in range(1, nc):
        src = lax.rem(c + nc - d, nc)
        pltpu.make_async_copy(cbuf.at[src, r], cbuf.at[src, r], c1.at[src]).wait()
    to_rows(r, [partner_r] + ring_r)

    arrived(rbuf, r2, partner_c)
    to_cols(partner_c, ring_c + [sibling_c])
    arrived(cbuf, c2, partner_r)
    to_rows(partner_r, ring_r)

    for hi in (y_hi, 1 - y_hi):
        slot = col_slot(hi, -step)
        arrived(rbuf, r2, slot)
        to_cols(slot, [col_slot(y_hi, step), sibling_c])
    for lo in (y_lo, 1 - y_lo):
        slot = row_slot(lo, -step)
        arrived(cbuf, c2, slot)
        to_rows(slot, [row_slot(y_lo, step)])
    for dz in (1, 2):
        for hi in (y_hi, 1 - y_hi):
            slot = col_slot(hi, step * dz)
            arrived(rbuf, r2, slot)
            to_cols(slot, [sibling_c])

    for hi in range(2):
        for zz in range(nz):
            arrived(rbuf, r2, (hi * nz + zz) * 2 + 1 - core)
    for dx in (1, 2):
        for lo in (y_lo, 1 - y_lo):
            arrived(cbuf, c2, row_slot(lo, step * dx))
    for cp in sends:
        cp.wait_send()


def exchange(w, nr, nc):
    rows, channels = w.shape
    rb = channels // nr
    cb = channels // nc
    dma = pltpu.SemaphoreType.DMA
    return pl.pallas_call(
        functools.partial(exchange_kernel, nr, nc),
        out_shape=(
            jax.ShapeDtypeStruct((nc, nr, rows, rb), w.dtype),
            jax.ShapeDtypeStruct((nc, nr, rows, cb), w.dtype),
        ),
        in_specs=[pl.BlockSpec(memory_space=pl.ANY)],
        out_specs=(pl.BlockSpec(memory_space=pl.ANY), pl.BlockSpec(memory_space=pl.ANY)),
        scratch_shapes=[
            dma((nr,)), dma((nc,)), dma((nc,)), dma((nr,)), dma((2 * (nr + nc),)), dma((2,)),
        ],
        compiler_params=pltpu.CompilerParams(has_side_effects=True),
    )(w)


def on_device(record, fir_taps, bins, offsets):
    kernel = analysis_kernel(fir_taps, bins)
    span = WL + TAPS - 1
    local_count = offsets.shape[0]

    assert local_count == 1
    placed = lax.dynamic_update_slice(
        jnp.zeros((kernel.shape[0], record.shape[0]), kernel.dtype), kernel, (0, offsets[0])
    )
    spectra = jnp.dot(placed, record, preferred_element_type=jnp.float32)[None]
    whitened = whiten(spectra)
    channels = whitened.shape[-1]
    row_count = lax.axis_size("row")
    col_count = lax.axis_size("col")
    total_windows = local_count * row_count * col_count
    row_block, col_block = exchange(
        whitened.reshape(2 * F, channels), row_count, col_count
    )
    windows = row_count * col_count * local_count
    rb = channels // row_count
    cb = channels // col_count
    left = row_block.reshape(windows, 2 * F, rb)
    right = col_block.reshape(windows, 2 * F, cb)
    return cross(left, right, 1.0 / total_windows)


def cross_kernel(scale, chunks, l_hbm, r_hbm, out_ref, l_in, r_in, lt, rt, sems):
    f = pl.program_id(0)
    cb = r_hbm.shape[-1]
    size = l_hbm.shape[0] // chunks

    @pl.when(f == 0)
    def _():
        copies = []
        for i in range(chunks):
            part = pl.ds(i * size, size)
            for j, (src, dst) in enumerate(((l_hbm, l_in), (r_hbm, r_in))):
                cp = pltpu.make_async_copy(src.at[part], dst.at[part], sems.at[j, i])
                cp.start()
                copies.append(cp)
        for i in range(chunks):
            part = pl.ds(i * size, size)
            copies[2 * i].wait()
            lt[:, part, :] = pltpu.einshape("nkc->knc", l_in[part])
            copies[2 * i + 1].wait()
            rt[:, part, :] = pltpu.einshape("nkc->knc", r_in[part]) * jnp.asarray(scale, rt.dtype)

    per_step = out_ref.shape[0]
    half = lt.shape[0] // 2
    for t in range(per_step):
        b = f * per_step + t
        l0, l1 = lt[b], lt[b + half]
        r0, r1 = rt[b], rt[b + half]
        lhs = jnp.concatenate([l0, l1], axis=0)
        rhs = jnp.concatenate(
            [jnp.concatenate([r0, r1], axis=1), jnp.concatenate([r1, -r0], axis=1)], axis=0
        )
        both = lax.dot_general(
            lhs, rhs, (((0,), (0,)), ((), ())), preferred_element_type=jnp.float32
        )
        out_ref[t, 0] = both[:, :cb].astype(out_ref.dtype)
        out_ref[t, 1] = both[:, cb:].astype(out_ref.dtype)


def cross(left, right, scale):
    windows, parts, rb = left.shape
    cb = right.shape[-1]
    bins = parts // 2
    chunks = 16
    per_step = 2
    return pl.pallas_call(
        functools.partial(cross_kernel, scale, chunks),
        out_shape=jax.ShapeDtypeStruct((bins, 2, rb, cb), jnp.bfloat16),
        grid=(bins // per_step,),
        in_specs=[pl.BlockSpec(memory_space=pl.ANY), pl.BlockSpec(memory_space=pl.ANY)],
        out_specs=pl.BlockSpec((per_step, 2, rb, cb), lambda f: (f, 0, 0, 0)),
        scratch_shapes=[
            pltpu.VMEM((windows, parts, rb), left.dtype),
            pltpu.VMEM((windows, parts, cb), right.dtype),
            pltpu.VMEM((parts, windows, rb), left.dtype),
            pltpu.VMEM((parts, windows, cb), right.dtype),
            pltpu.SemaphoreType.DMA((2, chunks)),
        ],
        cost_estimate=pl.CostEstimate(
            flops=8 * bins * rb * cb * windows,
            bytes_accessed=2 * (left.size + right.size + bins * 2 * rb * cb),
            transcendentals=0,
        ),
    )(left, right)


def solution(mesh):
    placed = (P(("row", "col"), None), P(), P(), P(("row", "col")))
    return jax.shard_map(
        on_device,
        mesh=mesh,
        in_specs=placed,
        out_specs=P(None, None, "row", "col"),
        check_vma=False,
    )
```

```python
import functools
import math

import jax
import jax.numpy as jnp
from jax import lax
from jax.sharding import PartitionSpec as P
from jax.experimental import pallas as pl
from jax.experimental.pallas import tpu as pltpu

F = 16
WL = 1280
TAPS = 101


floor_level = 0.5


def analysis_kernel(fir_taps, bins):
    span = WL + TAPS - 1
    sample_times = jnp.arange(WL, dtype=jnp.int32)
    phase_index = bins[:, None] * sample_times[None, :] % WL
    angles = 2.0 * math.pi / WL * phase_index.astype(jnp.float32)
    centre = (jnp.arange(WL, dtype=jnp.float32) + 0.5) / WL
    window_taper = (0.5 - 0.5 * jnp.cos(2.0 * math.pi * centre)) / math.sqrt(WL)
    pattern = jnp.stack([jnp.cos(angles) * window_taper, -jnp.sin(angles) * window_taper]).reshape(
        2 * F, WL
    )
    lanes = 128
    blocks = pl_cdiv(span, lanes)
    width = 2 * lanes
    padded = jnp.pad(pattern, ((0, 0), (TAPS - 1, blocks * lanes + lanes - WL - (TAPS - 1))))
    windows = jnp.concatenate(
        [
            padded[:, : blocks * lanes].reshape(2 * F, blocks, lanes),
            padded[:, lanes : (blocks + 1) * lanes].reshape(2 * F, blocks, lanes),
        ],
        axis=2,
    )
    vector = jnp.concatenate([fir_taps, jnp.zeros((width + 1 - TAPS,), jnp.float32)])
    band = jnp.tile(vector, lanes)[: lanes * width].reshape(lanes, width)
    kernel = jnp.einsum(
        "bqs,rs->bqr",
        windows,
        band,
        precision=lax.Precision.HIGHEST,
        preferred_element_type=jnp.float32,
    ).reshape(2 * F, blocks * lanes)[:, :span]
    return kernel.astype(jnp.bfloat16)


def pl_cdiv(a, b):
    return (a + b - 1) // b


def whiten(spectra):
    shaped = spectra.reshape(spectra.shape[0], 2, F, spectra.shape[-1])
    magnitude = jnp.sqrt(shaped[:, 0] * shaped[:, 0] + shaped[:, 1] * shaped[:, 1])
    inverse = 1.0 / jnp.maximum(magnitude, floor_level)
    return (shaped * inverse[:, None]).astype(jnp.bfloat16)


MESH = pl.DeviceIdType.MESH


def exchange_kernel(nr, nc, w_ref, rbuf, cbuf, r1, c1, r2, c2, sent, loc):
    r = lax.axis_index("row")
    c = lax.axis_index("col")
    rb = rbuf.shape[-1]
    cb = cbuf.shape[-1]
    nx = nr // 2
    nz = nc // 4
    x, y_lo = r // 2, r % 2
    y_hi, z, core = c // (2 * nz), (c // 2) % nz, c % 2
    sends = []

    def send(src, dst, recv_sem, device):
        cp = pltpu.make_async_remote_copy(
            src_ref=src, dst_ref=dst, send_sem=sent.at[len(sends)], recv_sem=recv_sem,
            device_id=device, device_id_type=MESH,
        )
        cp.start()
        sends.append(cp)

    def arrived(buf, sem, slot):
        if buf is cbuf:
            pltpu.make_async_copy(buf.at[:, slot], buf.at[:, slot], sem.at[slot]).wait()
        else:
            pltpu.make_async_copy(buf.at[slot], buf.at[slot], sem.at[slot]).wait()

    own_r = pltpu.make_async_copy(w_ref.at[:, pl.ds(r * rb, rb)], rbuf.at[c, r], loc.at[0])
    own_r.start()
    own_c = pltpu.make_async_copy(w_ref.at[:, pl.ds(c * cb, cb)], cbuf.at[c, r], loc.at[1])
    own_c.start()
    for d in range(1, nr):
        t = lax.rem(r + d, nr)
        send(w_ref.at[:, pl.ds(t * rb, rb)], rbuf.at[c, r], r1.at[r], (t, c))
    for d in range(1, nc):
        t = lax.rem(c + d, nc)
        send(w_ref.at[:, pl.ds(t * cb, cb)], cbuf.at[c, r], c1.at[c], (r, t))

    step = 1 - 2 * core

    def col_slot(hi, dz):
        return (hi * nz + lax.rem(z + dz + nz, nz)) * 2 + core

    def row_slot(lo, dx):
        return lax.rem(x + dx + nx, nx) * 2 + lo

    sibling_c = c + 1 - 2 * core

    def to_cols(slot, targets):
        for t in targets:
            send(rbuf.at[slot], rbuf.at[slot], r2.at[slot], (r, t))

    def to_rows(slot, targets):
        for t in targets:
            send(cbuf.at[:, slot], cbuf.at[:, slot], c2.at[slot], (t, c))

    partner_c = col_slot(1 - y_hi, 0)
    ring_c = [col_slot(y_hi, 1), col_slot(y_hi, -1)]
    own_r.wait()
    for d in range(1, nr):
        arrived(rbuf.at[c], r1, lax.rem(r + nr - d, nr))
    to_cols(c, [partner_c, sibling_c] + ring_c)

    partner_r = row_slot(1 - y_lo, 0)
    ring_r = [row_slot(y_lo, 1), row_slot(y_lo, -1)]
    own_c.wait()
    for d in range(1, nc):
        src = lax.rem(c + nc - d, nc)
        pltpu.make_async_copy(cbuf.at[src, r], cbuf.at[src, r], c1.at[src]).wait()
    to_rows(r, [partner_r] + ring_r)

    arrived(rbuf, r2, partner_c)
    to_cols(partner_c, ring_c + [sibling_c])
    arrived(cbuf, c2, partner_r)
    to_rows(partner_r, ring_r)

    for hi in (y_hi, 1 - y_hi):
        slot = col_slot(hi, -step)
        arrived(rbuf, r2, slot)
        to_cols(slot, [col_slot(y_hi, step), sibling_c])
    for lo in (y_lo, 1 - y_lo):
        slot = row_slot(lo, -step)
        arrived(cbuf, c2, slot)
        to_rows(slot, [row_slot(y_lo, step)])
    for dz in (1, 2):
        for hi in (y_hi, 1 - y_hi):
            slot = col_slot(hi, step * dz)
            arrived(rbuf, r2, slot)
            to_cols(slot, [sibling_c])

    for hi in range(2):
        for zz in range(nz):
            arrived(rbuf, r2, (hi * nz + zz) * 2 + 1 - core)
    for dx in (1, 2):
        for lo in (y_lo, 1 - y_lo):
            arrived(cbuf, c2, row_slot(lo, step * dx))
    for cp in sends:
        cp.wait_send()


def exchange(w, nr, nc):
    rows, channels = w.shape
    rb = channels // nr
    cb = channels // nc
    dma = pltpu.SemaphoreType.DMA
    return pl.pallas_call(
        functools.partial(exchange_kernel, nr, nc),
        out_shape=(
            jax.ShapeDtypeStruct((nc, nr, rows, rb), w.dtype),
            jax.ShapeDtypeStruct((nc, nr, rows, cb), w.dtype),
        ),
        in_specs=[pl.BlockSpec(memory_space=pl.ANY)],
        out_specs=(pl.BlockSpec(memory_space=pl.ANY), pl.BlockSpec(memory_space=pl.ANY)),
        scratch_shapes=[
            dma((nr,)), dma((nc,)), dma((nc,)), dma((nr,)), dma((2 * (nr + nc),)), dma((2,)),
        ],
        compiler_params=pltpu.CompilerParams(has_side_effects=True),
    )(w)


def on_device(record, fir_taps, bins, offsets):
    kernel = analysis_kernel(fir_taps, bins)
    span = WL + TAPS - 1
    local_count = offsets.shape[0]

    assert local_count == 1
    placed = lax.dynamic_update_slice(
        jnp.zeros((kernel.shape[0], record.shape[0]), kernel.dtype), kernel, (0, offsets[0])
    )
    spectra = jnp.dot(placed, record, preferred_element_type=jnp.float32)[None]
    whitened = whiten(spectra)
    channels = whitened.shape[-1]
    row_count = lax.axis_size("row")
    col_count = lax.axis_size("col")
    total_windows = local_count * row_count * col_count
    row_block, col_block = exchange(
        whitened.reshape(2 * F, channels), row_count, col_count
    )
    windows = row_count * col_count * local_count
    rb = channels // row_count
    cb = channels // col_count
    left = row_block.reshape(windows, 2 * F, rb)
    right = col_block.reshape(windows, 2 * F, cb)
    return cross(left, right, 1.0 / total_windows)


def cross_kernel(scale, chunks, l_hbm, r_hbm, out_ref, l_in, r_in, lt, rt, sems):
    f = pl.program_id(0)
    cb = r_hbm.shape[-1]
    size = l_hbm.shape[0] // chunks

    @pl.when(f == 0)
    def _():
        copies = []
        for i in range(chunks):
            part = pl.ds(i * size, size)
            for j, (src, dst) in enumerate(((l_hbm, l_in), (r_hbm, r_in))):
                cp = pltpu.make_async_copy(src.at[part], dst.at[part], sems.at[j, i])
                cp.start()
                copies.append(cp)
        for i in range(chunks):
            part = pl.ds(i * size, size)
            copies[2 * i].wait()
            lt[:, part, :] = pltpu.einshape("nkc->knc", l_in[part])
            copies[2 * i + 1].wait()
            rt[:, part, :] = pltpu.einshape("nkc->knc", r_in[part]) * jnp.asarray(scale, rt.dtype)

    per_step = out_ref.shape[0]
    half = lt.shape[0] // 2
    for t in range(per_step):
        b = f * per_step + t
        l0, l1 = lt[b], lt[b + half]
        r0, r1 = rt[b], rt[b + half]
        lhs = jnp.concatenate([l0, l1], axis=0)
        rhs = jnp.concatenate(
            [jnp.concatenate([r0, r1], axis=1), jnp.concatenate([r1, -r0], axis=1)], axis=0
        )
        both = lax.dot_general(
            lhs, rhs, (((0,), (0,)), ((), ())), preferred_element_type=jnp.float32
        )
        out_ref[t, 0] = both[:, :cb].astype(out_ref.dtype)
        out_ref[t, 1] = both[:, cb:].astype(out_ref.dtype)


def cross(left, right, scale):
    windows, parts, rb = left.shape
    cb = right.shape[-1]
    bins = parts // 2
    chunks = 16
    per_step = 4
    return pl.pallas_call(
        functools.partial(cross_kernel, scale, chunks),
        out_shape=jax.ShapeDtypeStruct((bins, 2, rb, cb), jnp.bfloat16),
        grid=(bins // per_step,),
        in_specs=[pl.BlockSpec(memory_space=pl.ANY), pl.BlockSpec(memory_space=pl.ANY)],
        out_specs=pl.BlockSpec((per_step, 2, rb, cb), lambda f: (f, 0, 0, 0)),
        scratch_shapes=[
            pltpu.VMEM((windows, parts, rb), left.dtype),
            pltpu.VMEM((windows, parts, cb), right.dtype),
            pltpu.VMEM((parts, windows, rb), left.dtype),
            pltpu.VMEM((parts, windows, cb), right.dtype),
            pltpu.SemaphoreType.DMA((2, chunks)),
        ],
        cost_estimate=pl.CostEstimate(
            flops=8 * bins * rb * cb * windows,
            bytes_accessed=2 * (left.size + right.size + bins * 2 * rb * cb),
            transcendentals=0,
        ),
    )(left, right)


def solution(mesh):
    placed = (P(("row", "col"), None), P(), P(), P(("row", "col")))
    return jax.shard_map(
        on_device,
        mesh=mesh,
        in_specs=placed,
        out_specs=P(None, None, "row", "col"),
        check_vma=False,
    )
```

```python
import functools
import math

import jax
import jax.numpy as jnp
from jax import lax
from jax.sharding import PartitionSpec as P
from jax.experimental import pallas as pl
from jax.experimental.pallas import tpu as pltpu

F = 16
WL = 1280
TAPS = 101


floor_level = 0.5


def analysis_kernel(fir_taps, bins):
    span = WL + TAPS - 1
    sample_times = jnp.arange(WL, dtype=jnp.int32)
    phase_index = bins[:, None] * sample_times[None, :] % WL
    angles = 2.0 * math.pi / WL * phase_index.astype(jnp.float32)
    centre = (jnp.arange(WL, dtype=jnp.float32) + 0.5) / WL
    window_taper = (0.5 - 0.5 * jnp.cos(2.0 * math.pi * centre)) / math.sqrt(WL)
    pattern = jnp.stack([jnp.cos(angles) * window_taper, -jnp.sin(angles) * window_taper]).reshape(
        2 * F, WL
    )
    lanes = 128
    blocks = pl_cdiv(span, lanes)
    width = 2 * lanes
    padded = jnp.pad(pattern, ((0, 0), (TAPS - 1, blocks * lanes + lanes - WL - (TAPS - 1))))
    windows = jnp.concatenate(
        [
            padded[:, : blocks * lanes].reshape(2 * F, blocks, lanes),
            padded[:, lanes : (blocks + 1) * lanes].reshape(2 * F, blocks, lanes),
        ],
        axis=2,
    )
    vector = jnp.concatenate([fir_taps, jnp.zeros((width + 1 - TAPS,), jnp.float32)])
    band = jnp.tile(vector, lanes)[: lanes * width].reshape(lanes, width)
    kernel = jnp.einsum(
        "bqs,rs->bqr",
        windows,
        band,
        precision=lax.Precision.HIGHEST,
        preferred_element_type=jnp.float32,
    ).reshape(2 * F, blocks * lanes)[:, :span]
    return kernel.astype(jnp.bfloat16)


def pl_cdiv(a, b):
    return (a + b - 1) // b


def whiten(spectra):
    shaped = spectra.reshape(spectra.shape[0], 2, F, spectra.shape[-1])
    magnitude = jnp.sqrt(shaped[:, 0] * shaped[:, 0] + shaped[:, 1] * shaped[:, 1])
    inverse = 1.0 / jnp.maximum(magnitude, floor_level)
    return (shaped * inverse[:, None]).astype(jnp.bfloat16)


MESH = pl.DeviceIdType.MESH


def exchange_kernel(nr, nc, w_ref, rbuf, cbuf, r1, c1, r2, c2, sent, loc):
    r = lax.axis_index("row")
    c = lax.axis_index("col")
    rb = rbuf.shape[-1]
    cb = cbuf.shape[-1]
    nx = nr // 2
    nz = nc // 4
    x, y_lo = r // 2, r % 2
    y_hi, z, core = c // (2 * nz), (c // 2) % nz, c % 2
    sends = []

    def send(src, dst, recv_sem, device):
        cp = pltpu.make_async_remote_copy(
            src_ref=src, dst_ref=dst, send_sem=sent.at[len(sends)], recv_sem=recv_sem,
            device_id=device, device_id_type=MESH,
        )
        cp.start()
        sends.append(cp)

    def arrived(buf, sem, slot):
        if buf is cbuf:
            pltpu.make_async_copy(buf.at[:, slot], buf.at[:, slot], sem.at[slot]).wait()
        else:
            pltpu.make_async_copy(buf.at[slot], buf.at[slot], sem.at[slot]).wait()

    own_r = pltpu.make_async_copy(w_ref.at[:, pl.ds(r * rb, rb)], rbuf.at[c, r], loc.at[0])
    own_r.start()
    own_c = pltpu.make_async_copy(w_ref.at[:, pl.ds(c * cb, cb)], cbuf.at[c, r], loc.at[1])
    own_c.start()
    for d in range(1, nr):
        t = lax.rem(r + d, nr)
        send(w_ref.at[:, pl.ds(t * rb, rb)], rbuf.at[c, r], r1.at[r], (t, c))
    for d in range(1, nc):
        t = lax.rem(c + d, nc)
        send(w_ref.at[:, pl.ds(t * cb, cb)], cbuf.at[c, r], c1.at[c], (r, t))

    step = 1 - 2 * core

    def col_slot(hi, dz):
        return (hi * nz + lax.rem(z + dz + nz, nz)) * 2 + core

    def row_slot(lo, dx):
        return lax.rem(x + dx + nx, nx) * 2 + lo

    sibling_c = c + 1 - 2 * core

    def to_cols(slot, targets):
        for t in targets:
            send(rbuf.at[slot], rbuf.at[slot], r2.at[slot], (r, t))

    def to_rows(slot, targets):
        for t in targets:
            send(cbuf.at[:, slot], cbuf.at[:, slot], c2.at[slot], (t, c))

    partner_c = col_slot(1 - y_hi, 0)
    ring_c = [col_slot(y_hi, 1), col_slot(y_hi, -1)]
    own_r.wait()
    for d in range(1, nr):
        arrived(rbuf.at[c], r1, lax.rem(r + nr - d, nr))
    to_cols(c, [partner_c, sibling_c] + ring_c)

    partner_r = row_slot(1 - y_lo, 0)
    ring_r = [row_slot(y_lo, 1), row_slot(y_lo, -1)]
    own_c.wait()
    for d in range(1, nc):
        src = lax.rem(c + nc - d, nc)
        pltpu.make_async_copy(cbuf.at[src, r], cbuf.at[src, r], c1.at[src]).wait()
    to_rows(r, [partner_r] + ring_r)

    arrived(rbuf, r2, partner_c)
    to_cols(partner_c, ring_c + [sibling_c])
    arrived(cbuf, c2, partner_r)
    to_rows(partner_r, ring_r)

    for hi in (y_hi, 1 - y_hi):
        slot = col_slot(hi, -step)
        arrived(rbuf, r2, slot)
        to_cols(slot, [col_slot(y_hi, step), sibling_c])
    for lo in (y_lo, 1 - y_lo):
        slot = row_slot(lo, -step)
        arrived(cbuf, c2, slot)
        to_rows(slot, [row_slot(y_lo, step)])
    for dz in (1, 2):
        for hi in (y_hi, 1 - y_hi):
            slot = col_slot(hi, step * dz)
            arrived(rbuf, r2, slot)
            to_cols(slot, [sibling_c])

    for hi in range(2):
        for zz in range(nz):
            arrived(rbuf, r2, (hi * nz + zz) * 2 + 1 - core)
    for dx in (1, 2):
        for lo in (y_lo, 1 - y_lo):
            arrived(cbuf, c2, row_slot(lo, step * dx))
    for cp in sends:
        cp.wait_send()


def exchange(w, nr, nc):
    rows, channels = w.shape
    rb = channels // nr
    cb = channels // nc
    dma = pltpu.SemaphoreType.DMA
    return pl.pallas_call(
        functools.partial(exchange_kernel, nr, nc),
        out_shape=(
            jax.ShapeDtypeStruct((nc, nr, rows, rb), w.dtype),
            jax.ShapeDtypeStruct((nc, nr, rows, cb), w.dtype),
        ),
        in_specs=[pl.BlockSpec(memory_space=pl.ANY)],
        out_specs=(pl.BlockSpec(memory_space=pl.ANY), pl.BlockSpec(memory_space=pl.ANY)),
        scratch_shapes=[
            dma((nr,)), dma((nc,)), dma((nc,)), dma((nr,)), dma((2 * (nr + nc),)), dma((2,)),
        ],
        compiler_params=pltpu.CompilerParams(has_side_effects=True),
    )(w)


def on_device(record, fir_taps, bins, offsets):
    kernel = analysis_kernel(fir_taps, bins)
    span = WL + TAPS - 1
    local_count = offsets.shape[0]

    assert local_count == 1
    placed = lax.dynamic_update_slice(
        jnp.zeros((kernel.shape[0], record.shape[0]), kernel.dtype), kernel, (0, offsets[0])
    )
    spectra = jnp.dot(placed, record, preferred_element_type=jnp.float32)[None]
    whitened = whiten(spectra)
    channels = whitened.shape[-1]
    row_count = lax.axis_size("row")
    col_count = lax.axis_size("col")
    total_windows = local_count * row_count * col_count
    row_block, col_block = exchange(
        whitened.reshape(2 * F, channels), row_count, col_count
    )
    windows = row_count * col_count * local_count
    rb = channels // row_count
    cb = channels // col_count
    left = row_block.reshape(windows, 2 * F, rb)
    right = col_block.reshape(windows, 2 * F, cb)
    return cross(left, right, 1.0 / total_windows)


def cross_kernel(scale, chunks, l_hbm, r_hbm, out_ref, l_in, r_in, lt, rt, sems):
    f = pl.program_id(0)
    cb = r_hbm.shape[-1]
    size = l_hbm.shape[0] // chunks

    @pl.when(f == 0)
    def _():
        copies = []
        for i in range(chunks):
            part = pl.ds(i * size, size)
            for j, (src, dst) in enumerate(((l_hbm, l_in), (r_hbm, r_in))):
                cp = pltpu.make_async_copy(src.at[part], dst.at[part], sems.at[j, i])
                cp.start()
                copies.append(cp)
        for i in range(chunks):
            part = pl.ds(i * size, size)
            copies[2 * i].wait()
            lt[:, part, :] = pltpu.einshape("nkc->knc", l_in[part])
            copies[2 * i + 1].wait()
            rt[:, part, :] = pltpu.einshape("nkc->knc", r_in[part]) * jnp.asarray(scale, rt.dtype)

    per_step = out_ref.shape[0]
    half = lt.shape[0] // 2
    for t in range(per_step):
        b = f * per_step + t
        l0, l1 = lt[b], lt[b + half]
        r0, r1 = rt[b], rt[b + half]
        lhs = jnp.concatenate([l0, l1], axis=0)
        rhs = jnp.concatenate(
            [jnp.concatenate([r0, r1], axis=1), jnp.concatenate([r1, -r0], axis=1)], axis=0
        )
        both = lax.dot_general(
            lhs, rhs, (((0,), (0,)), ((), ())), preferred_element_type=jnp.float32
        )
        out_ref[t, 0] = both[:, :cb].astype(out_ref.dtype)
        out_ref[t, 1] = both[:, cb:].astype(out_ref.dtype)


def cross(left, right, scale):
    windows, parts, rb = left.shape
    cb = right.shape[-1]
    bins = parts // 2
    chunks = 16
    per_step = 8
    return pl.pallas_call(
        functools.partial(cross_kernel, scale, chunks),
        out_shape=jax.ShapeDtypeStruct((bins, 2, rb, cb), jnp.bfloat16),
        grid=(bins // per_step,),
        in_specs=[pl.BlockSpec(memory_space=pl.ANY), pl.BlockSpec(memory_space=pl.ANY)],
        out_specs=pl.BlockSpec((per_step, 2, rb, cb), lambda f: (f, 0, 0, 0)),
        scratch_shapes=[
            pltpu.VMEM((windows, parts, rb), left.dtype),
            pltpu.VMEM((windows, parts, cb), right.dtype),
            pltpu.VMEM((parts, windows, rb), left.dtype),
            pltpu.VMEM((parts, windows, cb), right.dtype),
            pltpu.SemaphoreType.DMA((2, chunks)),
        ],
        cost_estimate=pl.CostEstimate(
            flops=8 * bins * rb * cb * windows,
            bytes_accessed=2 * (left.size + right.size + bins * 2 * rb * cb),
            transcendentals=0,
        ),
    )(left, right)


def solution(mesh):
    placed = (P(("row", "col"), None), P(), P(), P(("row", "col")))
    return jax.shard_map(
        on_device,
        mesh=mesh,
        in_specs=placed,
        out_specs=P(None, None, "row", "col"),
        check_vma=False,
    )
```

```python
import functools
import math

import jax
import jax.numpy as jnp
from jax import lax
from jax.sharding import PartitionSpec as P
from jax.experimental import pallas as pl
from jax.experimental.pallas import tpu as pltpu

F = 16
WL = 1280
TAPS = 101


floor_level = 0.5


def analysis_kernel(fir_taps, bins):
    span = WL + TAPS - 1
    sample_times = jnp.arange(WL, dtype=jnp.int32)
    phase_index = bins[:, None] * sample_times[None, :] % WL
    angles = 2.0 * math.pi / WL * phase_index.astype(jnp.float32)
    centre = (jnp.arange(WL, dtype=jnp.float32) + 0.5) / WL
    window_taper = (0.5 - 0.5 * jnp.cos(2.0 * math.pi * centre)) / math.sqrt(WL)
    pattern = jnp.stack([jnp.cos(angles) * window_taper, -jnp.sin(angles) * window_taper]).reshape(
        2 * F, WL
    )
    lanes = 128
    blocks = pl_cdiv(span, lanes)
    width = 2 * lanes
    padded = jnp.pad(pattern, ((0, 0), (TAPS - 1, blocks * lanes + lanes - WL - (TAPS - 1))))
    windows = jnp.concatenate(
        [
            padded[:, : blocks * lanes].reshape(2 * F, blocks, lanes),
            padded[:, lanes : (blocks + 1) * lanes].reshape(2 * F, blocks, lanes),
        ],
        axis=2,
    )
    vector = jnp.concatenate([fir_taps, jnp.zeros((width + 1 - TAPS,), jnp.float32)])
    band = jnp.tile(vector, lanes)[: lanes * width].reshape(lanes, width)
    kernel = jnp.einsum(
        "bqs,rs->bqr",
        windows,
        band,
        precision=lax.Precision.HIGHEST,
        preferred_element_type=jnp.float32,
    ).reshape(2 * F, blocks * lanes)[:, :span]
    return kernel.astype(jnp.bfloat16)


def pl_cdiv(a, b):
    return (a + b - 1) // b


def whiten(spectra):
    shaped = spectra.reshape(spectra.shape[0], 2, F, spectra.shape[-1])
    magnitude = jnp.sqrt(shaped[:, 0] * shaped[:, 0] + shaped[:, 1] * shaped[:, 1])
    inverse = 1.0 / jnp.maximum(magnitude, floor_level)
    return (shaped * inverse[:, None]).astype(jnp.bfloat16)


MESH = pl.DeviceIdType.MESH


def exchange_kernel(nr, nc, w_ref, rbuf, cbuf, r1, c1, r2, c2, sent, loc):
    r = lax.axis_index("row")
    c = lax.axis_index("col")
    rb = rbuf.shape[-1]
    cb = cbuf.shape[-1]
    nx = nr // 2
    nz = nc // 4
    x, y_lo = r // 2, r % 2
    y_hi, z, core = c // (2 * nz), (c // 2) % nz, c % 2
    sends = []

    def send(src, dst, recv_sem, device):
        cp = pltpu.make_async_remote_copy(
            src_ref=src, dst_ref=dst, send_sem=sent.at[len(sends)], recv_sem=recv_sem,
            device_id=device, device_id_type=MESH,
        )
        cp.start()
        sends.append(cp)

    def arrived(buf, sem, slot):
        if buf is cbuf:
            pltpu.make_async_copy(buf.at[:, slot], buf.at[:, slot], sem.at[slot]).wait()
        else:
            pltpu.make_async_copy(buf.at[slot], buf.at[slot], sem.at[slot]).wait()

    own_r = pltpu.make_async_copy(w_ref.at[:, pl.ds(r * rb, rb)], rbuf.at[c, r], loc.at[0])
    own_r.start()
    own_c = pltpu.make_async_copy(w_ref.at[:, pl.ds(c * cb, cb)], cbuf.at[c, r], loc.at[1])
    own_c.start()
    for d in range(1, nr):
        t = lax.rem(r + d, nr)
        send(w_ref.at[:, pl.ds(t * rb, rb)], rbuf.at[c, r], r1.at[r], (t, c))
    for d in range(1, nc):
        t = lax.rem(c + d, nc)
        send(w_ref.at[:, pl.ds(t * cb, cb)], cbuf.at[c, r], c1.at[c], (r, t))

    step = 1 - 2 * core

    def col_slot(hi, dz):
        return (hi * nz + lax.rem(z + dz + nz, nz)) * 2 + core

    def row_slot(lo, dx):
        return lax.rem(x + dx + nx, nx) * 2 + lo

    sibling_c = c + 1 - 2 * core

    def to_cols(slot, targets):
        for t in targets:
            send(rbuf.at[slot], rbuf.at[slot], r2.at[slot], (r, t))

    def to_rows(slot, targets):
        for t in targets:
            send(cbuf.at[:, slot], cbuf.at[:, slot], c2.at[slot], (t, c))

    partner_c = col_slot(1 - y_hi, 0)
    ring_c = [col_slot(y_hi, 1), col_slot(y_hi, -1)]
    own_r.wait()
    for d in range(1, nr):
        arrived(rbuf.at[c], r1, lax.rem(r + nr - d, nr))
    to_cols(c, [partner_c, sibling_c] + ring_c)

    partner_r = row_slot(1 - y_lo, 0)
    ring_r = [row_slot(y_lo, 1), row_slot(y_lo, -1)]
    own_c.wait()
    for d in range(1, nc):
        src = lax.rem(c + nc - d, nc)
        pltpu.make_async_copy(cbuf.at[src, r], cbuf.at[src, r], c1.at[src]).wait()
    to_rows(r, [partner_r] + ring_r)

    arrived(rbuf, r2, partner_c)
    to_cols(partner_c, ring_c + [sibling_c])
    arrived(cbuf, c2, partner_r)
    to_rows(partner_r, ring_r)

    for hi in (y_hi, 1 - y_hi):
        slot = col_slot(hi, -step)
        arrived(rbuf, r2, slot)
        to_cols(slot, [col_slot(y_hi, step), sibling_c])
    for lo in (y_lo, 1 - y_lo):
        slot = row_slot(lo, -step)
        arrived(cbuf, c2, slot)
        to_rows(slot, [row_slot(y_lo, step)])
    for dz in (1, 2):
        for hi in (y_hi, 1 - y_hi):
            slot = col_slot(hi, step * dz)
            arrived(rbuf, r2, slot)
            to_cols(slot, [sibling_c])

    for hi in range(2):
        for zz in range(nz):
            arrived(rbuf, r2, (hi * nz + zz) * 2 + 1 - core)
    for dx in (1, 2):
        for lo in (y_lo, 1 - y_lo):
            arrived(cbuf, c2, row_slot(lo, step * dx))
    for cp in sends:
        cp.wait_send()


def exchange(w, nr, nc):
    rows, channels = w.shape
    rb = channels // nr
    cb = channels // nc
    dma = pltpu.SemaphoreType.DMA
    return pl.pallas_call(
        functools.partial(exchange_kernel, nr, nc),
        out_shape=(
            jax.ShapeDtypeStruct((nc, nr, rows, rb), w.dtype),
            jax.ShapeDtypeStruct((nc, nr, rows, cb), w.dtype),
        ),
        in_specs=[pl.BlockSpec(memory_space=pl.ANY)],
        out_specs=(pl.BlockSpec(memory_space=pl.ANY), pl.BlockSpec(memory_space=pl.ANY)),
        scratch_shapes=[
            dma((nr,)), dma((nc,)), dma((nc,)), dma((nr,)), dma((2 * (nr + nc),)), dma((2,)),
        ],
        compiler_params=pltpu.CompilerParams(has_side_effects=True),
    )(w)


def on_device(record, fir_taps, bins, offsets):
    kernel = analysis_kernel(fir_taps, bins)
    span = WL + TAPS - 1
    local_count = offsets.shape[0]

    assert local_count == 1
    placed = lax.dynamic_update_slice(
        jnp.zeros((kernel.shape[0], record.shape[0]), kernel.dtype), kernel, (0, offsets[0])
    )
    spectra = jnp.dot(placed, record, preferred_element_type=jnp.float32)[None]
    whitened = whiten(spectra)
    channels = whitened.shape[-1]
    row_count = lax.axis_size("row")
    col_count = lax.axis_size("col")
    total_windows = local_count * row_count * col_count
    row_block, col_block = exchange(
        whitened.reshape(2 * F, channels), row_count, col_count
    )
    windows = row_count * col_count * local_count
    rb = channels // row_count
    cb = channels // col_count
    left = row_block.reshape(windows, 2 * F, rb)
    right = col_block.reshape(windows, 2 * F, cb)
    return cross(left, right, 1.0 / total_windows)


def cross_kernel(scale, chunks, l_hbm, r_hbm, out_hbm, l_in, r_in, lt, rt, out_v, sems, out_sems):
    cb = r_hbm.shape[-1]
    size = l_hbm.shape[0] // chunks
    copies = []
    for i in range(chunks):
        part = pl.ds(i * size, size)
        for j, (src, dst) in enumerate(((l_hbm, l_in), (r_hbm, r_in))):
            cp = pltpu.make_async_copy(src.at[part], dst.at[part], sems.at[j, i])
            cp.start()
            copies.append(cp)
    for i in range(chunks):
        part = pl.ds(i * size, size)
        copies[2 * i].wait()
        lt[:, part, :] = pltpu.einshape("nkc->knc", l_in[part])
        copies[2 * i + 1].wait()
        rt[:, part, :] = pltpu.einshape("nkc->knc", r_in[part]) * jnp.asarray(scale, rt.dtype)

    half = lt.shape[0] // 2
    outs = []
    for b in range(half):
        l0, l1 = lt[b], lt[b + half]
        r0, r1 = rt[b], rt[b + half]
        lhs = jnp.concatenate([l0, l1], axis=0)
        rhs = jnp.concatenate(
            [jnp.concatenate([r0, r1], axis=1), jnp.concatenate([r1, -r0], axis=1)], axis=0
        )
        both = lax.dot_general(
            lhs, rhs, (((0,), (0,)), ((), ())), preferred_element_type=jnp.float32
        )
        out_v[b, 0] = both[:, :cb].astype(out_v.dtype)
        out_v[b, 1] = both[:, cb:].astype(out_v.dtype)
        cp = pltpu.make_async_copy(out_v.at[b], out_hbm.at[b], out_sems.at[b])
        cp.start()
        outs.append(cp)
    for cp in outs:
        cp.wait()


def cross(left, right, scale):
    windows, parts, rb = left.shape
    cb = right.shape[-1]
    bins = parts // 2
    chunks = 16
    return pl.pallas_call(
        functools.partial(cross_kernel, scale, chunks),
        out_shape=jax.ShapeDtypeStruct((bins, 2, rb, cb), jnp.bfloat16),
        in_specs=[pl.BlockSpec(memory_space=pl.ANY), pl.BlockSpec(memory_space=pl.ANY)],
        out_specs=pl.BlockSpec(memory_space=pl.ANY),
        scratch_shapes=[
            pltpu.VMEM((windows, parts, rb), left.dtype),
            pltpu.VMEM((windows, parts, cb), right.dtype),
            pltpu.VMEM((parts, windows, rb), left.dtype),
            pltpu.VMEM((parts, windows, cb), right.dtype),
            pltpu.VMEM((bins, 2, rb, cb), jnp.bfloat16),
            pltpu.SemaphoreType.DMA((2, chunks)),
            pltpu.SemaphoreType.DMA((bins,)),
        ],
        cost_estimate=pl.CostEstimate(
            flops=8 * bins * rb * cb * windows,
            bytes_accessed=2 * (left.size + right.size + bins * 2 * rb * cb),
            transcendentals=0,
        ),
    )(left, right)


def solution(mesh):
    placed = (P(("row", "col"), None), P(), P(), P(("row", "col")))
    return jax.shard_map(
        on_device,
        mesh=mesh,
        in_specs=placed,
        out_specs=P(None, None, "row", "col"),
        check_vma=False,
    )
```

```python
import functools
import math

import jax
import jax.numpy as jnp
from jax import lax
from jax.sharding import PartitionSpec as P
from jax.experimental import pallas as pl
from jax.experimental.pallas import tpu as pltpu

F = 16
WL = 1280
TAPS = 101


floor_level = 0.5


def analysis_kernel(fir_taps, bins, offset, length, slack):
    span = WL + TAPS - 1
    sample_times = jnp.arange(WL, dtype=jnp.int32)
    phase_index = bins[:, None] * sample_times[None, :] % WL
    angles = 2.0 * math.pi / WL * phase_index.astype(jnp.float32)
    centre = (jnp.arange(WL, dtype=jnp.float32) + 0.5) / WL
    window_taper = (0.5 - 0.5 * jnp.cos(2.0 * math.pi * centre)) / math.sqrt(WL)
    pattern = jnp.stack([jnp.cos(angles) * window_taper, -jnp.sin(angles) * window_taper]).reshape(
        2 * F, WL
    )
    lanes = 128
    assert slack + TAPS - 1 <= lanes
    blocks = pl_cdiv(length, lanes)
    width = 2 * lanes
    padded = jnp.pad(pattern, ((0, 0), (lanes, (blocks + 1) * lanes - WL - lanes)))
    windows = jnp.concatenate(
        [
            padded[:, : blocks * lanes].reshape(2 * F, blocks, lanes),
            padded[:, lanes : (blocks + 1) * lanes].reshape(2 * F, blocks, lanes),
        ],
        axis=2,
    )
    vector = lax.dynamic_update_slice(
        jnp.zeros((width + 1,), jnp.float32), fir_taps, (lanes - (TAPS - 1) - offset,)
    )
    band = jnp.tile(vector, lanes)[: lanes * width].reshape(lanes, width)
    kernel = jnp.einsum(
        "bqs,rs->bqr",
        windows,
        band,
        precision=lax.Precision.HIGHEST,
        preferred_element_type=jnp.float32,
    ).reshape(2 * F, blocks * lanes)[:, :length]
    return kernel.astype(jnp.bfloat16)


def pl_cdiv(a, b):
    return (a + b - 1) // b


def whiten(spectra):
    shaped = spectra.reshape(spectra.shape[0], 2, F, spectra.shape[-1])
    magnitude = jnp.sqrt(shaped[:, 0] * shaped[:, 0] + shaped[:, 1] * shaped[:, 1])
    inverse = 1.0 / jnp.maximum(magnitude, floor_level)
    return (shaped * inverse[:, None]).astype(jnp.bfloat16)


MESH = pl.DeviceIdType.MESH


def exchange_kernel(nr, nc, w_ref, rbuf, cbuf, r1, c1, r2, c2, sent, loc):
    r = lax.axis_index("row")
    c = lax.axis_index("col")
    rb = rbuf.shape[-1]
    cb = cbuf.shape[-1]
    nx = nr // 2
    nz = nc // 4
    x, y_lo = r // 2, r % 2
    y_hi, z, core = c // (2 * nz), (c // 2) % nz, c % 2
    sends = []

    def send(src, dst, recv_sem, device):
        cp = pltpu.make_async_remote_copy(
            src_ref=src, dst_ref=dst, send_sem=sent.at[len(sends)], recv_sem=recv_sem,
            device_id=device, device_id_type=MESH,
        )
        cp.start()
        sends.append(cp)

    def arrived(buf, sem, slot):
        if buf is cbuf:
            pltpu.make_async_copy(buf.at[:, slot], buf.at[:, slot], sem.at[slot]).wait()
        else:
            pltpu.make_async_copy(buf.at[slot], buf.at[slot], sem.at[slot]).wait()

    own_r = pltpu.make_async_copy(w_ref.at[:, pl.ds(r * rb, rb)], rbuf.at[c, r], loc.at[0])
    own_r.start()
    own_c = pltpu.make_async_copy(w_ref.at[:, pl.ds(c * cb, cb)], cbuf.at[c, r], loc.at[1])
    own_c.start()
    for d in range(1, nr):
        t = lax.rem(r + d, nr)
        send(w_ref.at[:, pl.ds(t * rb, rb)], rbuf.at[c, r], r1.at[r], (t, c))
    for d in range(1, nc):
        t = lax.rem(c + d, nc)
        send(w_ref.at[:, pl.ds(t * cb, cb)], cbuf.at[c, r], c1.at[c], (r, t))

    step = 1 - 2 * core

    def col_slot(hi, dz):
        return (hi * nz + lax.rem(z + dz + nz, nz)) * 2 + core

    def row_slot(lo, dx):
        return lax.rem(x + dx + nx, nx) * 2 + lo

    sibling_c = c + 1 - 2 * core

    def to_cols(slot, targets):
        for t in targets:
            send(rbuf.at[slot], rbuf.at[slot], r2.at[slot], (r, t))

    def to_rows(slot, targets):
        for t in targets:
            send(cbuf.at[:, slot], cbuf.at[:, slot], c2.at[slot], (t, c))

    partner_c = col_slot(1 - y_hi, 0)
    ring_c = [col_slot(y_hi, 1), col_slot(y_hi, -1)]
    own_r.wait()
    for d in range(1, nr):
        arrived(rbuf.at[c], r1, lax.rem(r + nr - d, nr))
    to_cols(c, [partner_c, sibling_c] + ring_c)

    partner_r = row_slot(1 - y_lo, 0)
    ring_r = [row_slot(y_lo, 1), row_slot(y_lo, -1)]
    own_c.wait()
    for d in range(1, nc):
        src = lax.rem(c + nc - d, nc)
        pltpu.make_async_copy(cbuf.at[src, r], cbuf.at[src, r], c1.at[src]).wait()
    to_rows(r, [partner_r] + ring_r)

    arrived(rbuf, r2, partner_c)
    to_cols(partner_c, ring_c + [sibling_c])
    arrived(cbuf, c2, partner_r)
    to_rows(partner_r, ring_r)

    for hi in (y_hi, 1 - y_hi):
        slot = col_slot(hi, -step)
        arrived(rbuf, r2, slot)
        to_cols(slot, [col_slot(y_hi, step), sibling_c])
    for lo in (y_lo, 1 - y_lo):
        slot = row_slot(lo, -step)
        arrived(cbuf, c2, slot)
        to_rows(slot, [row_slot(y_lo, step)])
    for dz in (1, 2):
        for hi in (y_hi, 1 - y_hi):
            slot = col_slot(hi, step * dz)
            arrived(rbuf, r2, slot)
            to_cols(slot, [sibling_c])

    for hi in range(2):
        for zz in range(nz):
            arrived(rbuf, r2, (hi * nz + zz) * 2 + 1 - core)
    for dx in (1, 2):
        for lo in (y_lo, 1 - y_lo):
            arrived(cbuf, c2, row_slot(lo, step * dx))
    for cp in sends:
        cp.wait_send()


def exchange(w, nr, nc):
    rows, channels = w.shape
    rb = channels // nr
    cb = channels // nc
    dma = pltpu.SemaphoreType.DMA
    return pl.pallas_call(
        functools.partial(exchange_kernel, nr, nc),
        out_shape=(
            jax.ShapeDtypeStruct((nc, nr, rows, rb), w.dtype),
            jax.ShapeDtypeStruct((nc, nr, rows, cb), w.dtype),
        ),
        in_specs=[pl.BlockSpec(memory_space=pl.ANY)],
        out_specs=(pl.BlockSpec(memory_space=pl.ANY), pl.BlockSpec(memory_space=pl.ANY)),
        scratch_shapes=[
            dma((nr,)), dma((nc,)), dma((nc,)), dma((nr,)), dma((2 * (nr + nc),)), dma((2,)),
        ],
        compiler_params=pltpu.CompilerParams(has_side_effects=True),
    )(w)


def on_device(record, fir_taps, bins, offsets):
    local_count = offsets.shape[0]
    assert local_count == 1
    slack = record.shape[0] - (WL + TAPS - 1)
    placed = analysis_kernel(fir_taps, bins, offsets[0], record.shape[0], slack)
    spectra = jnp.dot(placed, record, preferred_element_type=jnp.float32)[None]
    whitened = whiten(spectra)
    channels = whitened.shape[-1]
    row_count = lax.axis_size("row")
    col_count = lax.axis_size("col")
    total_windows = local_count * row_count * col_count
    row_block, col_block = exchange(
        whitened.reshape(2 * F, channels), row_count, col_count
    )
    windows = row_count * col_count * local_count
    rb = channels // row_count
    cb = channels // col_count
    left = row_block.reshape(windows, 2 * F, rb)
    right = col_block.reshape(windows, 2 * F, cb)
    return cross(left, right, 1.0 / total_windows)


def cross_kernel(scale, chunks, l_hbm, r_hbm, out_hbm, l_in, r_in, lt, rt, out_v, sems, out_sems):
    cb = r_hbm.shape[-1]
    size = l_hbm.shape[0] // chunks
    copies = []
    for i in range(chunks):
        part = pl.ds(i * size, size)
        for j, (src, dst) in enumerate(((l_hbm, l_in), (r_hbm, r_in))):
            cp = pltpu.make_async_copy(src.at[part], dst.at[part], sems.at[j, i])
            cp.start()
            copies.append(cp)
    for i in range(chunks):
        part = pl.ds(i * size, size)
        copies[2 * i].wait()
        lt[:, part, :] = pltpu.einshape("nkc->knc", l_in[part])
        copies[2 * i + 1].wait()
        rt[:, part, :] = pltpu.einshape("nkc->knc", r_in[part]) * jnp.asarray(scale, rt.dtype)

    half = lt.shape[0] // 2
    outs = []
    for b in range(half):
        l0, l1 = lt[b], lt[b + half]
        r0, r1 = rt[b], rt[b + half]
        lhs = jnp.concatenate([l0, l1], axis=0)
        rhs = jnp.concatenate(
            [jnp.concatenate([r0, r1], axis=1), jnp.concatenate([r1, -r0], axis=1)], axis=0
        )
        both = lax.dot_general(
            lhs, rhs, (((0,), (0,)), ((), ())), preferred_element_type=jnp.float32
        )
        out_v[b, 0] = both[:, :cb].astype(out_v.dtype)
        out_v[b, 1] = both[:, cb:].astype(out_v.dtype)
        cp = pltpu.make_async_copy(out_v.at[b], out_hbm.at[b], out_sems.at[b])
        cp.start()
        outs.append(cp)
    for cp in outs:
        cp.wait()


def cross(left, right, scale):
    windows, parts, rb = left.shape
    cb = right.shape[-1]
    bins = parts // 2
    chunks = 16
    return pl.pallas_call(
        functools.partial(cross_kernel, scale, chunks),
        out_shape=jax.ShapeDtypeStruct((bins, 2, rb, cb), jnp.bfloat16),
        in_specs=[pl.BlockSpec(memory_space=pl.ANY), pl.BlockSpec(memory_space=pl.ANY)],
        out_specs=pl.BlockSpec(memory_space=pl.ANY),
        scratch_shapes=[
            pltpu.VMEM((windows, parts, rb), left.dtype),
            pltpu.VMEM((windows, parts, cb), right.dtype),
            pltpu.VMEM((parts, windows, rb), left.dtype),
            pltpu.VMEM((parts, windows, cb), right.dtype),
            pltpu.VMEM((bins, 2, rb, cb), jnp.bfloat16),
            pltpu.SemaphoreType.DMA((2, chunks)),
            pltpu.SemaphoreType.DMA((bins,)),
        ],
        cost_estimate=pl.CostEstimate(
            flops=8 * bins * rb * cb * windows,
            bytes_accessed=2 * (left.size + right.size + bins * 2 * rb * cb),
            transcendentals=0,
        ),
    )(left, right)


def solution(mesh):
    placed = (P(("row", "col"), None), P(), P(), P(("row", "col")))
    return jax.shard_map(
        on_device,
        mesh=mesh,
        in_specs=placed,
        out_specs=P(None, None, "row", "col"),
        check_vma=False,
    )
```

```python
import functools
import math

import jax
import jax.numpy as jnp
from jax import lax
from jax.sharding import PartitionSpec as P
from jax.experimental import pallas as pl
from jax.experimental.pallas import tpu as pltpu

F = 16
WL = 1280
TAPS = 101


floor_level = 0.5


def analysis_kernel(fir_taps, bins, offset, length, slack):
    span = WL + TAPS - 1
    sample_times = jnp.arange(WL, dtype=jnp.int32)
    phase_index = bins[:, None] * sample_times[None, :] % WL
    angles = 2.0 * math.pi / WL * phase_index.astype(jnp.float32)
    centre = (jnp.arange(WL, dtype=jnp.float32) + 0.5) / WL
    window_taper = (0.5 - 0.5 * jnp.cos(2.0 * math.pi * centre)) / math.sqrt(WL)
    pattern = jnp.stack([jnp.cos(angles) * window_taper, -jnp.sin(angles) * window_taper]).reshape(
        2 * F, WL
    )
    lanes = 128
    assert slack + TAPS - 1 <= lanes
    blocks = pl_cdiv(length, lanes)
    width = 2 * lanes
    padded = jnp.pad(pattern, ((0, 0), (lanes, (blocks + 1) * lanes - WL - lanes)))
    windows = jnp.concatenate(
        [
            padded[:, : blocks * lanes].reshape(2 * F, blocks, lanes),
            padded[:, lanes : (blocks + 1) * lanes].reshape(2 * F, blocks, lanes),
        ],
        axis=2,
    )
    vector = lax.dynamic_update_slice(
        jnp.zeros((width + 1,), jnp.float32), fir_taps, (lanes - (TAPS - 1) - offset,)
    )
    band = jnp.tile(vector, lanes)[: lanes * width].reshape(lanes, width)
    kernel = jnp.einsum(
        "bqs,rs->bqr",
        windows,
        band,
        precision=lax.Precision.HIGHEST,
        preferred_element_type=jnp.float32,
    ).reshape(2 * F, blocks * lanes)[:, :length]
    return kernel.astype(jnp.bfloat16)


def pl_cdiv(a, b):
    return (a + b - 1) // b


def whiten(spectra):
    shaped = spectra.reshape(spectra.shape[0], 2, F, spectra.shape[-1])
    squared = shaped[:, 0] * shaped[:, 0] + shaped[:, 1] * shaped[:, 1]
    inverse = jnp.minimum(lax.rsqrt(squared), 1.0 / floor_level)
    return (shaped * inverse[:, None]).astype(jnp.bfloat16)


MESH = pl.DeviceIdType.MESH


def exchange_kernel(nr, nc, w_ref, rbuf, cbuf, r1, c1, r2, c2, sent, loc):
    r = lax.axis_index("row")
    c = lax.axis_index("col")
    rb = rbuf.shape[-1]
    cb = cbuf.shape[-1]
    nx = nr // 2
    nz = nc // 4
    x, y_lo = r // 2, r % 2
    y_hi, z, core = c // (2 * nz), (c // 2) % nz, c % 2
    sends = []

    def send(src, dst, recv_sem, device):
        cp = pltpu.make_async_remote_copy(
            src_ref=src, dst_ref=dst, send_sem=sent.at[len(sends)], recv_sem=recv_sem,
            device_id=device, device_id_type=MESH,
        )
        cp.start()
        sends.append(cp)

    def arrived(buf, sem, slot):
        if buf is cbuf:
            pltpu.make_async_copy(buf.at[:, slot], buf.at[:, slot], sem.at[slot]).wait()
        else:
            pltpu.make_async_copy(buf.at[slot], buf.at[slot], sem.at[slot]).wait()

    own_r = pltpu.make_async_copy(w_ref.at[:, pl.ds(r * rb, rb)], rbuf.at[c, r], loc.at[0])
    own_r.start()
    own_c = pltpu.make_async_copy(w_ref.at[:, pl.ds(c * cb, cb)], cbuf.at[c, r], loc.at[1])
    own_c.start()
    for d in range(1, nr):
        t = lax.rem(r + d, nr)
        send(w_ref.at[:, pl.ds(t * rb, rb)], rbuf.at[c, r], r1.at[r], (t, c))
    for d in range(1, nc):
        t = lax.rem(c + d, nc)
        send(w_ref.at[:, pl.ds(t * cb, cb)], cbuf.at[c, r], c1.at[c], (r, t))

    step = 1 - 2 * core

    def col_slot(hi, dz):
        return (hi * nz + lax.rem(z + dz + nz, nz)) * 2 + core

    def row_slot(lo, dx):
        return lax.rem(x + dx + nx, nx) * 2 + lo

    sibling_c = c + 1 - 2 * core

    def to_cols(slot, targets):
        for t in targets:
            send(rbuf.at[slot], rbuf.at[slot], r2.at[slot], (r, t))

    def to_rows(slot, targets):
        for t in targets:
            send(cbuf.at[:, slot], cbuf.at[:, slot], c2.at[slot], (t, c))

    partner_c = col_slot(1 - y_hi, 0)
    ring_c = [col_slot(y_hi, 1), col_slot(y_hi, -1)]
    own_r.wait()
    for d in range(1, nr):
        arrived(rbuf.at[c], r1, lax.rem(r + nr - d, nr))
    to_cols(c, [partner_c, sibling_c] + ring_c)

    partner_r = row_slot(1 - y_lo, 0)
    ring_r = [row_slot(y_lo, 1), row_slot(y_lo, -1)]
    own_c.wait()
    for d in range(1, nc):
        src = lax.rem(c + nc - d, nc)
        pltpu.make_async_copy(cbuf.at[src, r], cbuf.at[src, r], c1.at[src]).wait()
    to_rows(r, [partner_r] + ring_r)

    arrived(rbuf, r2, partner_c)
    to_cols(partner_c, ring_c + [sibling_c])
    arrived(cbuf, c2, partner_r)
    to_rows(partner_r, ring_r)

    for hi in (y_hi, 1 - y_hi):
        slot = col_slot(hi, -step)
        arrived(rbuf, r2, slot)
        to_cols(slot, [col_slot(y_hi, step), sibling_c])
    for lo in (y_lo, 1 - y_lo):
        slot = row_slot(lo, -step)
        arrived(cbuf, c2, slot)
        to_rows(slot, [row_slot(y_lo, step)])
    for dz in (1, 2):
        for hi in (y_hi, 1 - y_hi):
            slot = col_slot(hi, step * dz)
            arrived(rbuf, r2, slot)
            to_cols(slot, [sibling_c])

    for hi in range(2):
        for zz in range(nz):
            arrived(rbuf, r2, (hi * nz + zz) * 2 + 1 - core)
    for dx in (1, 2):
        for lo in (y_lo, 1 - y_lo):
            arrived(cbuf, c2, row_slot(lo, step * dx))
    for cp in sends:
        cp.wait_send()


def exchange(w, nr, nc):
    rows, channels = w.shape
    rb = channels // nr
    cb = channels // nc
    dma = pltpu.SemaphoreType.DMA
    return pl.pallas_call(
        functools.partial(exchange_kernel, nr, nc),
        out_shape=(
            jax.ShapeDtypeStruct((nc, nr, rows, rb), w.dtype),
            jax.ShapeDtypeStruct((nc, nr, rows, cb), w.dtype),
        ),
        in_specs=[pl.BlockSpec(memory_space=pl.ANY)],
        out_specs=(pl.BlockSpec(memory_space=pl.ANY), pl.BlockSpec(memory_space=pl.ANY)),
        scratch_shapes=[
            dma((nr,)), dma((nc,)), dma((nc,)), dma((nr,)), dma((2 * (nr + nc),)), dma((2,)),
        ],
        compiler_params=pltpu.CompilerParams(has_side_effects=True),
    )(w)


def on_device(record, fir_taps, bins, offsets):
    local_count = offsets.shape[0]
    assert local_count == 1
    slack = record.shape[0] - (WL + TAPS - 1)
    placed = analysis_kernel(fir_taps, bins, offsets[0], record.shape[0], slack)
    spectra = jnp.dot(placed, record, preferred_element_type=jnp.float32)[None]
    whitened = whiten(spectra)
    channels = whitened.shape[-1]
    row_count = lax.axis_size("row")
    col_count = lax.axis_size("col")
    total_windows = local_count * row_count * col_count
    row_block, col_block = exchange(
        whitened.reshape(2 * F, channels), row_count, col_count
    )
    windows = row_count * col_count * local_count
    rb = channels // row_count
    cb = channels // col_count
    left = row_block.reshape(windows, 2 * F, rb)
    right = col_block.reshape(windows, 2 * F, cb)
    return cross(left, right, 1.0 / total_windows)


def cross_kernel(scale, chunks, l_hbm, r_hbm, out_hbm, l_in, r_in, lt, rt, out_v, sems, out_sems):
    cb = r_hbm.shape[-1]
    size = l_hbm.shape[0] // chunks
    copies = []
    for i in range(chunks):
        part = pl.ds(i * size, size)
        for j, (src, dst) in enumerate(((l_hbm, l_in), (r_hbm, r_in))):
            cp = pltpu.make_async_copy(src.at[part], dst.at[part], sems.at[j, i])
            cp.start()
            copies.append(cp)
    for i in range(chunks):
        part = pl.ds(i * size, size)
        copies[2 * i].wait()
        lt[:, part, :] = pltpu.einshape("nkc->knc", l_in[part])
        copies[2 * i + 1].wait()
        rt[:, part, :] = pltpu.einshape("nkc->knc", r_in[part]) * jnp.asarray(scale, rt.dtype)

    half = lt.shape[0] // 2
    outs = []
    for b in range(half):
        l0, l1 = lt[b], lt[b + half]
        r0, r1 = rt[b], rt[b + half]
        lhs = jnp.concatenate([l0, l1], axis=0)
        rhs = jnp.concatenate(
            [jnp.concatenate([r0, r1], axis=1), jnp.concatenate([r1, -r0], axis=1)], axis=0
        )
        both = lax.dot_general(
            lhs, rhs, (((0,), (0,)), ((), ())), preferred_element_type=jnp.float32
        )
        out_v[b, 0] = both[:, :cb].astype(out_v.dtype)
        out_v[b, 1] = both[:, cb:].astype(out_v.dtype)
        cp = pltpu.make_async_copy(out_v.at[b], out_hbm.at[b], out_sems.at[b])
        cp.start()
        outs.append(cp)
    for cp in outs:
        cp.wait()


def cross(left, right, scale):
    windows, parts, rb = left.shape
    cb = right.shape[-1]
    bins = parts // 2
    chunks = 16
    return pl.pallas_call(
        functools.partial(cross_kernel, scale, chunks),
        out_shape=jax.ShapeDtypeStruct((bins, 2, rb, cb), jnp.bfloat16),
        in_specs=[pl.BlockSpec(memory_space=pl.ANY), pl.BlockSpec(memory_space=pl.ANY)],
        out_specs=pl.BlockSpec(memory_space=pl.ANY),
        scratch_shapes=[
            pltpu.VMEM((windows, parts, rb), left.dtype),
            pltpu.VMEM((windows, parts, cb), right.dtype),
            pltpu.VMEM((parts, windows, rb), left.dtype),
            pltpu.VMEM((parts, windows, cb), right.dtype),
            pltpu.VMEM((bins, 2, rb, cb), jnp.bfloat16),
            pltpu.SemaphoreType.DMA((2, chunks)),
            pltpu.SemaphoreType.DMA((bins,)),
        ],
        cost_estimate=pl.CostEstimate(
            flops=8 * bins * rb * cb * windows,
            bytes_accessed=2 * (left.size + right.size + bins * 2 * rb * cb),
            transcendentals=0,
        ),
    )(left, right)


def solution(mesh):
    placed = (P(("row", "col"), None), P(), P(), P(("row", "col")))
    return jax.shard_map(
        on_device,
        mesh=mesh,
        in_specs=placed,
        out_specs=P(None, None, "row", "col"),
        check_vma=False,
    )
```

```python
import functools
import math

import jax
import jax.numpy as jnp
from jax import lax
from jax.sharding import PartitionSpec as P
from jax.experimental import pallas as pl
from jax.experimental.pallas import tpu as pltpu

F = 16
WL = 1280
TAPS = 101


floor_level = 0.5


def analysis_kernel(fir_taps, bins, offset, length, slack):
    span = WL + TAPS - 1
    sample_times = jnp.arange(WL, dtype=jnp.int32)
    phase_index = bins[:, None] * sample_times[None, :] % WL
    angles = 2.0 * math.pi / WL * phase_index.astype(jnp.float32)
    centre = (jnp.arange(WL, dtype=jnp.float32) + 0.5) / WL
    window_taper = (0.5 - 0.5 * jnp.cos(2.0 * math.pi * centre)) / math.sqrt(WL)
    pattern = jnp.stack([jnp.cos(angles) * window_taper, -jnp.sin(angles) * window_taper]).reshape(
        2 * F, WL
    )
    lanes = 128
    assert slack + TAPS - 1 <= lanes
    blocks = pl_cdiv(length, lanes)
    width = 2 * lanes
    padded = jnp.pad(pattern, ((0, 0), (lanes, (blocks + 1) * lanes - WL - lanes)))
    windows = jnp.concatenate(
        [
            padded[:, : blocks * lanes].reshape(2 * F, blocks, lanes),
            padded[:, lanes : (blocks + 1) * lanes].reshape(2 * F, blocks, lanes),
        ],
        axis=2,
    )
    vector = lax.dynamic_update_slice(
        jnp.zeros((width + 1,), jnp.float32), fir_taps, (lanes - (TAPS - 1) - offset,)
    )
    band = jnp.tile(vector, lanes)[: lanes * width].reshape(lanes, width)
    kernel = jnp.einsum(
        "bqs,rs->bqr",
        windows,
        band,
        precision=lax.Precision.HIGHEST,
        preferred_element_type=jnp.float32,
    ).reshape(2 * F, blocks * lanes)[:, :length]
    return kernel.astype(jnp.bfloat16)


def pl_cdiv(a, b):
    return (a + b - 1) // b


def whiten(spectra):
    shaped = spectra.reshape(spectra.shape[0], 2, F, spectra.shape[-1])
    magnitude = jnp.sqrt(shaped[:, 0] * shaped[:, 0] + shaped[:, 1] * shaped[:, 1])
    inverse = 1.0 / jnp.maximum(magnitude, floor_level)
    return (shaped * inverse[:, None]).astype(jnp.bfloat16)


MESH = pl.DeviceIdType.MESH


def exchange_kernel(nr, nc, w_ref, rbuf, cbuf, r1, c1, r2, c2, sent, loc):
    r = lax.axis_index("row")
    c = lax.axis_index("col")
    rb = rbuf.shape[-1]
    cb = cbuf.shape[-1]
    nx = nr // 2
    nz = nc // 4
    x, y_lo = r // 2, r % 2
    y_hi, z, core = c // (2 * nz), (c // 2) % nz, c % 2
    sends = []

    def send(src, dst, recv_sem, device):
        cp = pltpu.make_async_remote_copy(
            src_ref=src, dst_ref=dst, send_sem=sent.at[len(sends)], recv_sem=recv_sem,
            device_id=device, device_id_type=MESH,
        )
        cp.start()
        sends.append(cp)

    def arrived(buf, sem, slot):
        if buf is cbuf:
            pltpu.make_async_copy(buf.at[:, slot], buf.at[:, slot], sem.at[slot]).wait()
        else:
            pltpu.make_async_copy(buf.at[slot], buf.at[slot], sem.at[slot]).wait()

    own_r = pltpu.make_async_copy(w_ref.at[:, pl.ds(r * rb, rb)], rbuf.at[c, r], loc.at[0])
    own_r.start()
    own_c = pltpu.make_async_copy(w_ref.at[:, pl.ds(c * cb, cb)], cbuf.at[c, r], loc.at[1])
    own_c.start()
    for d in range(1, nr):
        t = lax.rem(r + d, nr)
        send(w_ref.at[:, pl.ds(t * rb, rb)], rbuf.at[c, r], r1.at[r], (t, c))
    for d in range(1, nc):
        t = lax.rem(c + d, nc)
        send(w_ref.at[:, pl.ds(t * cb, cb)], cbuf.at[c, r], c1.at[c], (r, t))

    step = 1 - 2 * core

    def col_slot(hi, dz):
        return (hi * nz + lax.rem(z + dz + nz, nz)) * 2 + core

    def row_slot(lo, dx):
        return lax.rem(x + dx + nx, nx) * 2 + lo

    sibling_c = c + 1 - 2 * core

    def to_cols(slot, targets):
        for t in targets:
            send(rbuf.at[slot], rbuf.at[slot], r2.at[slot], (r, t))

    def to_rows(slot, targets):
        for t in targets:
            send(cbuf.at[:, slot], cbuf.at[:, slot], c2.at[slot], (t, c))

    partner_c = col_slot(1 - y_hi, 0)
    ring_c = [col_slot(y_hi, 1), col_slot(y_hi, -1)]
    own_r.wait()
    for d in range(1, nr):
        arrived(rbuf.at[c], r1, lax.rem(r + nr - d, nr))
    to_cols(c, [partner_c, sibling_c] + ring_c)

    partner_r = row_slot(1 - y_lo, 0)
    ring_r = [row_slot(y_lo, 1), row_slot(y_lo, -1)]
    own_c.wait()
    for d in range(1, nc):
        src = lax.rem(c + nc - d, nc)
        pltpu.make_async_copy(cbuf.at[src, r], cbuf.at[src, r], c1.at[src]).wait()
    to_rows(r, [partner_r] + ring_r)

    arrived(rbuf, r2, partner_c)
    to_cols(partner_c, ring_c + [sibling_c])
    arrived(cbuf, c2, partner_r)
    to_rows(partner_r, ring_r)

    for hi in (y_hi, 1 - y_hi):
        slot = col_slot(hi, -step)
        arrived(rbuf, r2, slot)
        to_cols(slot, [col_slot(y_hi, step), sibling_c])
    for lo in (y_lo, 1 - y_lo):
        slot = row_slot(lo, -step)
        arrived(cbuf, c2, slot)
        to_rows(slot, [row_slot(y_lo, step)])
    for dz in (1, 2):
        for hi in (y_hi, 1 - y_hi):
            slot = col_slot(hi, step * dz)
            arrived(rbuf, r2, slot)
            to_cols(slot, [sibling_c])

    for hi in range(2):
        for zz in range(nz):
            arrived(rbuf, r2, (hi * nz + zz) * 2 + 1 - core)
    for dx in (1, 2):
        for lo in (y_lo, 1 - y_lo):
            arrived(cbuf, c2, row_slot(lo, step * dx))
    for cp in sends:
        cp.wait_send()


def exchange(w, nr, nc):
    rows, channels = w.shape
    rb = channels // nr
    cb = channels // nc
    dma = pltpu.SemaphoreType.DMA
    return pl.pallas_call(
        functools.partial(exchange_kernel, nr, nc),
        out_shape=(
            jax.ShapeDtypeStruct((nc, nr, rows, rb), w.dtype),
            jax.ShapeDtypeStruct((nc, nr, rows, cb), w.dtype),
        ),
        in_specs=[pl.BlockSpec(memory_space=pl.ANY)],
        out_specs=(pl.BlockSpec(memory_space=pl.ANY), pl.BlockSpec(memory_space=pl.ANY)),
        scratch_shapes=[
            dma((nr,)), dma((nc,)), dma((nc,)), dma((nr,)), dma((2 * (nr + nc),)), dma((2,)),
        ],
        compiler_params=pltpu.CompilerParams(has_side_effects=True),
    )(w)


def on_device(record, fir_taps, bins, offsets):
    local_count = offsets.shape[0]
    assert local_count == 1
    slack = record.shape[0] - (WL + TAPS - 1)
    placed = analysis_kernel(fir_taps, bins, offsets[0], record.shape[0], slack)
    spectra = jnp.dot(placed, record, preferred_element_type=jnp.float32)[None]
    whitened = whiten(spectra)
    channels = whitened.shape[-1]
    row_count = lax.axis_size("row")
    col_count = lax.axis_size("col")
    total_windows = local_count * row_count * col_count
    row_block, col_block = exchange(
        whitened.reshape(2 * F, channels), row_count, col_count
    )
    windows = row_count * col_count * local_count
    rb = channels // row_count
    cb = channels // col_count
    left = row_block.reshape(windows, 2 * F, rb)
    right = col_block.reshape(windows, 2 * F, cb)
    return cross(left, right, 1.0 / total_windows)


def cross_kernel(scale, chunks, l_hbm, r_hbm, out_hbm, l_in, r_in, lt, rt, out_v, sems, out_sems):
    cb = r_hbm.shape[-1]
    size = l_hbm.shape[0] // chunks
    copies = []
    for i in range(chunks):
        part = pl.ds(i * size, size)
        for j, (src, dst) in enumerate(((l_hbm, l_in), (r_hbm, r_in))):
            cp = pltpu.make_async_copy(src.at[part], dst.at[part], sems.at[j, i])
            cp.start()
            copies.append(cp)
    for i in range(chunks):
        part = pl.ds(i * size, size)
        copies[2 * i].wait()
        lt[:, part, :] = pltpu.einshape("nkc->knc", l_in[part])
        copies[2 * i + 1].wait()
        rt[:, part, :] = pltpu.einshape("nkc->knc", r_in[part]) * jnp.asarray(scale, rt.dtype)

    half = lt.shape[0] // 2
    outs = []
    for b in range(half):
        l0, l1 = lt[b], lt[b + half]
        r0, r1 = rt[b], rt[b + half]
        lhs = jnp.concatenate([l0, l1], axis=0)
        rhs = jnp.concatenate(
            [jnp.concatenate([r0, r1], axis=1), jnp.concatenate([r1, -r0], axis=1)], axis=0
        )
        both = lax.dot_general(
            lhs, rhs, (((0,), (0,)), ((), ())), preferred_element_type=jnp.float32
        )
        out_v[b, 0] = both[:, :cb].astype(out_v.dtype)
        out_v[b, 1] = both[:, cb:].astype(out_v.dtype)
        cp = pltpu.make_async_copy(out_v.at[b], out_hbm.at[b], out_sems.at[b])
        cp.start()
        outs.append(cp)
    for cp in outs:
        cp.wait()


def cross(left, right, scale):
    windows, parts, rb = left.shape
    cb = right.shape[-1]
    bins = parts // 2
    chunks = 8
    return pl.pallas_call(
        functools.partial(cross_kernel, scale, chunks),
        out_shape=jax.ShapeDtypeStruct((bins, 2, rb, cb), jnp.bfloat16),
        in_specs=[pl.BlockSpec(memory_space=pl.ANY), pl.BlockSpec(memory_space=pl.ANY)],
        out_specs=pl.BlockSpec(memory_space=pl.ANY),
        scratch_shapes=[
            pltpu.VMEM((windows, parts, rb), left.dtype),
            pltpu.VMEM((windows, parts, cb), right.dtype),
            pltpu.VMEM((parts, windows, rb), left.dtype),
            pltpu.VMEM((parts, windows, cb), right.dtype),
            pltpu.VMEM((bins, 2, rb, cb), jnp.bfloat16),
            pltpu.SemaphoreType.DMA((2, chunks)),
            pltpu.SemaphoreType.DMA((bins,)),
        ],
        cost_estimate=pl.CostEstimate(
            flops=8 * bins * rb * cb * windows,
            bytes_accessed=2 * (left.size + right.size + bins * 2 * rb * cb),
            transcendentals=0,
        ),
    )(left, right)


def solution(mesh):
    placed = (P(("row", "col"), None), P(), P(), P(("row", "col")))
    return jax.shard_map(
        on_device,
        mesh=mesh,
        in_specs=placed,
        out_specs=P(None, None, "row", "col"),
        check_vma=False,
    )
```
